32 devices in a mesh: ctx: 16 (over z, y, x), tp: 2 (over core).
Axes of the slice: x: 2, y: 2, z: 4, core: 2. Of those that a mesh axis runs over, the one named last changes fastest.
Arguments:
- tokens: bfloat16 [4, 2048, 1280], P(None, 'ctx'), may hold values from -6 to 6
- cotangent: bfloat16 [4, 2048, 1280], P(None, 'ctx'), may hold values from -6 to 6
- doc_lengths: int32 [4, 8], replicated, may hold values from 1 to 1536, 2048 in all within a row
- w_query: bfloat16 [1280, 1280], P('ctx', 'tp'), may hold values from -0.15625 to 0.15625
- w_key: bfloat16 [1280, 1280], P('ctx', 'tp'), may hold values from -0.15625 to 0.15625
- w_value: bfloat16 [1280, 1280], P('ctx', 'tp'), may hold values from -0.15625 to 0.15625
- w_out: bfloat16 [1280, 1280], P('tp', 'ctx'), may hold values from -0.625 to 0.625
- w_up: bfloat16 [1280, 1280], P('ctx', 'tp'), may hold values from -0.15625 to 0.15625
- w_down: bfloat16 [1280, 1280], P('tp', 'ctx'), may hold values from -0.25 to 0.25
- gain_attn: bfloat16 [1280], P('ctx'), may hold values from 0.099609375 to 1.8984375
- gain_mlp: bfloat16 [1280], P('ctx'), may hold values from 0.099609375 to 1.8984375
- query_scale: float32 [80], replicated, may hold values from 0.06 to 0.3
Outputs:
- layer_out: bfloat16 [4, 2048, 1280], P(None, 'ctx')
- grad_tokens: float32 [4, 2048, 1280], P(None, 'ctx')
- grad_query: float32 [1280, 1280], P('ctx', 'tp')
- grad_key: float32 [1280, 1280], P('ctx', 'tp')
- grad_value: float32 [1280, 1280], P('ctx', 'tp')
- grad_out: float32 [1280, 1280], P('tp', 'ctx')
- grad_up: float32 [1280, 1280], P('ctx', 'tp')
- grad_down: float32 [1280, 1280], P('tp', 'ctx')
- grad_gain_attn: float32 [1280], P('ctx')
- grad_gain_mlp: float32 [1280], P('ctx')
- grad_scale: float32 [80], replicated
The draws below stay inside these ranges and needn't reach their ends.
Inputs may be any that keep to these rules, and one draw needn't show every extreme that they name: `doc_lengths`: each row holds the lengths of the 8 documents of one stream in order; they sum to 2048, and the longest is exactly 1536.
All inputs are finite; a program needn't handle non-finite values.
Results may differ from the reference program's by a relative error of at most 0.024.
Values may be sent and summed in bfloat16 or wider, within the bound.
No kernel may reach another device: no remote copies, remote signals or barrier semaphores. Data moves between devices by JAX's collectives and lax.ppermute only.
A program may use at most 192 MiB of HBM per device.

```python
import math
import jax
import jax.numpy as jnp
import numpy as np
from jax import lax

D = 1280
HEAD_DIM = 80
FF = 1280
MB = 4
NDOC = 8
HD = 1280
STREAM = 2048
DOC_MAX = 1536
N_TP = 2


def steps_of(own_key, shape, split, least, largest):
    level = 1.0
    for position, parts in split:
        steps = jax.random.uniform(jax.random.fold_in(jax.random.fold_in(own_key, 6), position), (parts,), jnp.float32, least / len(split), largest / len(split))
        level = level * jnp.repeat(jnp.exp(steps), shape[position] // parts).reshape((-1,) + (1,) * (len(shape) - 1 - position))
    return level


def profile(number_of, total, bound, lean):
    portions = [(1 << 20) // math.isqrt(rank ** lean) + 1 for rank in range(2, number_of + 1)]
    spare, holding = total - bound - (number_of - 1), [1] * (number_of - 1)
    while spare > 0:
        movable = [i for i in range(number_of - 1) if holding[i] < bound]
        pool, budget = sum([portions[i] for i in movable]), spare
        for i in movable:
            more = min(bound - holding[i], max(1, budget * portions[i] // pool), spare)
            holding[i] = holding[i] + more
            spare = spare - more
    return np.array([bound] + holding)


def ragged(own_key, amount, total, bound, lean):
    if amount == 2:
        one = jax.random.randint(own_key, (), max(1, total - bound), min(bound, total - 1) + 1)
        return jnp.stack([one, total - one])
    sizes = jnp.asarray(profile(amount, total, bound, lean), jnp.int32)
    couples = (amount - 1) // 2
    giver, receiver = sizes[1:1 + 2 * couples:2], sizes[2:2 + 2 * couples:2]
    margin = jnp.minimum(giver - 1, bound - receiver)
    shifted = jax.random.randint(jax.random.fold_in(own_key, 1), (couples,), 0, 1 << 20) % (margin + 1)
    sizes = sizes.at[1:1 + 2 * couples:2].set(giver - shifted).at[2:2 + 2 * couples:2].set(receiver + shifted)
    return sizes[jax.random.permutation(jax.random.fold_in(own_key, 2), amount)]


def bell_draw(own_key, shape, deviation, bound, cuts=(), kind=jnp.bfloat16):
    array = jax.random.normal(own_key, shape, jnp.float32) * deviation
    if len(cuts) > 0:
        array = steps_of(own_key, shape, cuts, -0.22, 0.18) * array
    return jnp.clip(array, min=-bound, max=bound).astype(kind)


def setup_inputs(seed: int = 0) -> dict:
    splits = jax.random.split(jax.random.key(seed), 13)
    return {
        "tokens": bell_draw(splits[0], (MB, STREAM, D), 1.0, 6.0, ((1, 16),)),
        "cotangent": bell_draw(splits[1], (MB, STREAM, D), 1.0, 6.0, ((1, 16),)),
        "doc_lengths": jax.vmap(lambda own: ragged(own, NDOC, STREAM, DOC_MAX, 2))(jax.random.split(splits[2], MB)).reshape((MB, NDOC)).astype(jnp.int32),
        "w_query": bell_draw(splits[3], (D, HD), D ** -0.5, 0.15625, ((0, 16), (1, 2))),
        "w_key": bell_draw(splits[4], (D, HD), D ** -0.5, 0.15625, ((0, 16), (1, 2))),
        "w_value": bell_draw(splits[5], (D, HD), D ** -0.5, 0.15625, ((0, 16), (1, 2))),
        "w_out": bell_draw(splits[6], (HD, D), (HD // 16) ** -0.5, 0.625, ((0, 2), (1, 16))),
        "w_up": bell_draw(splits[7], (D, FF), D ** -0.5, 0.15625, ((0, 16), (1, 2))),
        "w_down": bell_draw(splits[8], (FF, D), (FF // 2) ** -0.5, 0.25, ((0, 2), (1, 16))),
        "gain_attn": jnp.clip(1.0 + 0.18 * jax.random.normal(splits[9], (D,), jnp.float32), 0.099609375, 1.8984375).astype(jnp.bfloat16),
        "gain_mlp": jnp.clip(1.0 + 0.18 * jax.random.normal(splits[10], (D,), jnp.float32), 0.099609375, 1.8984375).astype(jnp.bfloat16),
        "query_scale": jnp.clip(jnp.exp(jax.random.uniform(splits[11], (HEAD_DIM,), jnp.float32, math.log(0.06), math.log(0.3))), 0.06, 0.3),
    }


@jax.custom_vjp
def low(v):
    return lax.optimization_barrier(v.astype(jnp.bfloat16)).astype(jnp.float32)

@jax.custom_vjp
def low_back(v):
    return v

def low_keep(v):
    return (low(v), None)

def low_pass(kept, grad):
    return (grad,)

def back_keep(v):
    return (v, None)

def back_low(kept, grad):
    return (low(grad),)
low.defvjp(low_keep, low_pass)
low_back.defvjp(back_keep, back_low)
EPSILON = 1e-06
MASKED = -1e+30
EXACT = lax.Precision.HIGHEST

def inverse_rms(values):
    return lax.rsqrt(lax.optimization_barrier(jnp.mean(values * values, axis=-1, keepdims=True)) + EPSILON)

def segment_ids(lengths, length):
    starts = jnp.cumsum(lengths) - lengths
    positions = jnp.arange(length, dtype=jnp.int32)
    return lax.optimization_barrier(jnp.sum((starts[None, :] <= positions[:, None]).astype(jnp.int32), axis=1)).astype(jnp.int32)

def attention(queries, keys, values, segments):
    length, head_count, head_size = queries.shape
    block_rows = min(512, length)
    block_count = length // block_rows
    positions = jnp.arange(length, dtype=jnp.int32)

    def attend_block(packed):
        query_block, seg_block, pos_block = packed
        scores = low_back(jnp.einsum('qhd,khd->hqk', query_block, keys, precision=EXACT))
        allowed = (positions[None, :] <= pos_block[:, None]) & (segments[None, :] == seg_block[:, None])
        scores = jnp.where(allowed[None], scores, MASKED)
        row_top = lax.optimization_barrier(jnp.max(scores, axis=-1, keepdims=True))
        log_total = row_top + jnp.log(lax.optimization_barrier(jnp.sum(jnp.exp(scores - row_top), axis=-1, keepdims=True)))
        probs = jnp.where(allowed[None], jnp.exp(scores - log_total), 0.0)
        return jnp.einsum('hqk,khd->qhd', low(probs), values, precision=EXACT)
    result = lax.map(jax.checkpoint(attend_block), (queries.reshape(block_count, block_rows, head_count, head_size), segments.reshape(block_count, block_rows), positions.reshape(block_count, block_rows)))
    return result.reshape(length, head_count, head_size)

def layer_forward(stream_in, segments, w_query, w_key, w_value, w_out, w_up, w_down, gain_attn, gain_mlp, query_scale):
    length = stream_in.shape[0]
    head_size = query_scale.shape[0]
    head_count = w_query.shape[1] // head_size
    normed_one = low(stream_in * inverse_rms(stream_in) * gain_attn)
    query_raw = low_back(jnp.dot(normed_one, w_query, precision=EXACT))
    queries = low(query_raw.reshape(length, head_count, head_size) * query_scale)
    keys = low(low_back(jnp.dot(normed_one, w_key, precision=EXACT))).reshape(length, head_count, head_size)
    values = low(low_back(jnp.dot(normed_one, w_value, precision=EXACT))).reshape(length, head_count, head_size)
    attended = attention(queries, keys, values, segments)
    attended = low(low_back(attended)).reshape(length, head_count * head_size)
    group = head_count * head_size // N_TP
    partials = jnp.einsum('sgc,gcd->sgd', attended.reshape(length, N_TP, group), w_out.reshape(N_TP, group, w_out.shape[1]), precision=EXACT)
    attn_out = low_back(lax.optimization_barrier(jnp.sum(low(partials), axis=1)))
    hidden = stream_in + attn_out
    normed_two = low(hidden * inverse_rms(hidden) * gain_mlp)
    up_raw = low_back(jnp.dot(normed_two, w_up, precision=EXACT))
    activated = low(jax.nn.silu(up_raw))
    unit_group = w_up.shape[1] // N_TP
    mlp_parts = jnp.einsum('sgc,gcd->sgd', activated.reshape(length, N_TP, unit_group), w_down.reshape(N_TP, unit_group, w_down.shape[1]), precision=EXACT)
    return hidden + lax.optimization_barrier(jnp.sum(low(mlp_parts), axis=1))

def reference(tokens, cotangent, doc_lengths, w_query, w_key, w_value, w_out, w_up, w_down, gain_attn, gain_mlp, query_scale):
    weights = tuple((weight.astype(jnp.float32) for weight in (w_query, w_key, w_value, w_out, w_up, w_down, gain_attn, gain_mlp, query_scale)))
    sums = tuple((jnp.zeros(weight.shape, jnp.float32) for weight in weights))
    outputs = []
    input_grads = []
    for micro_step in range(tokens.shape[0]):
        segments = segment_ids(doc_lengths[micro_step], tokens.shape[1])

        def forward(stream_in, *params):
            return layer_forward(stream_in, segments, *params)
        result, pull = jax.vjp(forward, tokens[micro_step].astype(jnp.float32), *weights)
        grads = pull(cotangent[micro_step].astype(jnp.float32))
        outputs.append(result.astype(jnp.bfloat16))
        input_grads.append(grads[0])
        sums = tuple((total + extra for total, extra in zip(sums, grads[1:])))
    return (jnp.stack(outputs), jnp.stack(input_grads), sums[0], sums[1], sums[2], sums[3], sums[4], sums[5], sums[6], sums[7], sums[8])
```

```python
import functools

import jax
import jax.numpy as jnp
from jax import lax
from jax.experimental import pallas as pl
from jax.experimental.pallas import tpu as pltpu
from jax.sharding import PartitionSpec as P

EPSILON = 1e-06
MASKED = -1e30
LANES = 128
BF = jnp.bfloat16
F32 = jnp.float32
VMEM_LIMIT = 56 * 1024 * 1024


def vmem():
    return pl.BlockSpec(memory_space=pltpu.VMEM)


def smem():
    return pl.BlockSpec(memory_space=pltpu.SMEM)


def call(kernel, out_shape, in_kinds, scratch=(), flops=0, moved=0):
    return pl.pallas_call(
        kernel,
        out_shape=out_shape,
        in_specs=[smem() if kind == "s" else vmem() for kind in in_kinds],
        out_specs=jax.tree.map(lambda _: vmem(), out_shape),
        scratch_shapes=list(scratch),
        compiler_params=pltpu.CompilerParams(vmem_limit_bytes=VMEM_LIMIT),
        cost_estimate=pl.CostEstimate(
            flops=int(flops), transcendentals=0, bytes_accessed=int(moved)
        ),
    )


def struct(shape, dtype):
    return jax.ShapeDtypeStruct(tuple(shape), dtype)


def nn(a, b):
    return jnp.dot(a, b, preferred_element_type=F32)


def nt(a, b):
    return lax.dot_general(a, b, (((1,), (1,)), ((), ())), preferred_element_type=F32)


def tn(a, b):
    return lax.dot_general(a, b, (((0,), (0,)), ((), ())), preferred_element_type=F32)


def assemble_kernel(ids, own, other, out):
    groups, half, _ = own.shape
    z, c = ids[0], ids[2]
    for kz in range(groups):
        g = z ^ kz
        out[g, pl.ds(pl.multiple_of(c * half, half), half), :] = own[kz].astype(out.dtype)
        out[g, pl.ds(pl.multiple_of((1 - c) * half, half), half), :] = other[kz].astype(out.dtype)


def assemble(ids, own, other, dtype):
    groups, half, width = own.shape
    return call(
        assemble_kernel, struct((groups, 2 * half, width), dtype), "svv", moved=3 * own.size * 4
    )(ids, own, other)


def project_kernel(members, head_pairs, ids, *refs):
    pieces = refs[: 2 * members]
    w, gain, scale, proj, normed = refs[2 * members :]
    groups, half, width = pieces[0].shape
    z, j, c = ids[0], ids[1], ids[2]
    for kc in range(2):
        for kj in range(members):
            x = pieces[kc * members + kj][...].reshape(groups * half, width).astype(F32)
            r = lax.rsqrt(jnp.mean(x * x, axis=-1, keepdims=True) + EPSILON)
            xn = (x * r * gain[...]).astype(BF)
            y = nn(xn, w[...])
            y = (y * scale[...]).astype(BF)
            for kz in range(groups):
                base = (z ^ kz) * (members * 2) + (j ^ kj) * 2 + (c ^ kc)
                rows = pl.ds(pl.multiple_of(base * half, half), half)
                normed[rows, :] = xn[kz * half : (kz + 1) * half]
                proj[rows, :] = y[kz * half : (kz + 1) * half]


def attend_kernel(heads, size, members, block, ids, first, proj, doc, sent, kept, vt):
    stream = proj.shape[0]
    j = ids[1]
    for h in range(heads):
        cols = slice((2 * heads + h) * LANES, (2 * heads + h + 1) * LANES)
        vt[h] = proj[:, cols].T

    def one_query_block(qb, _):
        rows = pl.ds(pl.multiple_of(qb * block, block), block)
        doc_row = doc[:, rows]
        qpos = qb * block + lax.broadcasted_iota(jnp.int32, (1, block), 1)
        queries = [proj[rows, h * LANES : (h + 1) * LANES] for h in range(heads)]

        def one_key_block(kb, carry):
            keys = pl.ds(pl.multiple_of(kb * block, block), block)
            kpos = kb * block + lax.broadcasted_iota(jnp.int32, (block, block), 0)
            allowed = (kpos <= qpos) & (kpos >= doc_row)
            new = []
            for h in range(heads):
                top, total, acc = carry[h]
                k = proj[keys, (heads + h) * LANES : (heads + h + 1) * LANES]
                s = jnp.where(allowed, nt(k, queries[h]), MASKED)
                top2 = jnp.maximum(top, jnp.max(s, axis=0, keepdims=True))
                p = jnp.exp(s - top2)
                alpha = jnp.exp(top - top2)
                total = total * alpha + jnp.sum(p, axis=0, keepdims=True)
                acc = acc * alpha + nn(vt[h, :, keys], p.astype(BF))
                new.append((top2, total, acc))
            return tuple(new)

        zero = (
            jnp.full((1, block), MASKED, F32),
            jnp.zeros((1, block), F32),
            jnp.zeros((LANES, block), F32),
        )
        done = lax.fori_loop(first[qb], qb + 1, one_key_block, (zero,) * heads)
        for h in range(heads):
            top, total, acc = done[h]
            o = acc / total
            kept[h, :LANES, rows] = o
            kept[h, LANES : LANES + 8, rows] = jnp.broadcast_to(top + jnp.log(total), (8, block))
            low = o[:size].astype(BF)
            for part in range(block // LANES):
                pb = qb * (block // LANES) + part
                group, member = pb // members, pb % members
                lanes = pl.ds(pl.multiple_of(group * LANES, LANES), LANES)
                sent[member ^ j, h * size : (h + 1) * size, lanes] = low[
                    :, part * LANES : (part + 1) * LANES
                ]
        return 0

    lax.fori_loop(0, stream // block, one_query_block, 0)


def attend_back_kernel(heads, size, members, block, ids, last, proj, doc, kept, scale, *refs):
    pieces = refs[:members]
    grads, scale_sum, dot_, do_, kt, dqt, delta = refs[members:]
    stream = proj.shape[0]
    groups = pieces[0].shape[1] // LANES
    j = ids[1]
    for h in range(heads):
        kt[h] = proj[:, (heads + h) * LANES : (heads + h + 1) * LANES].T
        dot_[h, size:, :] = jnp.zeros((LANES - size, stream), BF)
        for kj in range(members):
            for g in range(groups):
                at = pl.ds(pl.multiple_of((g * members + (j ^ kj)) * LANES, LANES), LANES)
                dot_[h, :size, at] = pieces[kj][h * size : (h + 1) * size, g * LANES : (g + 1) * LANES]
        do_[h] = dot_[h].T
        delta[h] = jnp.broadcast_to(
            jnp.sum(dot_[h].astype(F32) * kept[h, :LANES, :], axis=0, keepdims=True), (8, stream)
        )
        dqt[h] = jnp.zeros((LANES, stream), F32)

    def one_key_block(kb, _):
        keys = pl.ds(pl.multiple_of(kb * block, block), block)
        kpos = kb * block + lax.broadcasted_iota(jnp.int32, (block, block), 0)
        ks = [proj[keys, (heads + h) * LANES : (heads + h + 1) * LANES] for h in range(heads)]
        vs = [proj[keys, (2 * heads + h) * LANES : (2 * heads + h + 1) * LANES] for h in range(heads)]

        def one_query_block(qb, carry):
            rows = pl.ds(pl.multiple_of(qb * block, block), block)
            qpos = qb * block + lax.broadcasted_iota(jnp.int32, (1, block), 1)
            allowed = (kpos <= qpos) & (kpos >= doc[:, rows])
            new = []
            for h in range(heads):
                dk, dv = carry[h]
                q = proj[rows, h * LANES : (h + 1) * LANES]
                s = nt(ks[h], q)
                p = jnp.where(allowed, jnp.exp(s - kept[h, LANES : LANES + 1, rows]), 0.0)
                dp = nn(vs[h], dot_[h, :, rows])
                ds = (p * (dp - delta[h, 0:1, rows])).astype(BF)
                dv = dv + nn(p.astype(BF), do_[h, rows, :])
                dk = dk + nn(ds, q)
                dqt[h, :, rows] += nn(kt[h, :, keys], ds)
                new.append((dk, dv))
            return tuple(new)

        zero = jnp.zeros((block, LANES), F32)
        done = lax.fori_loop(kb, last[kb], one_query_block, ((zero, zero),) * heads)
        for h in range(heads):
            grads[keys, (heads + h) * LANES : (heads + h + 1) * LANES] = done[h][0].astype(BF)
            grads[keys, (2 * heads + h) * LANES : (2 * heads + h + 1) * LANES] = done[h][1].astype(BF)
        return 0

    lax.fori_loop(0, stream // block, one_key_block, 0)
    total = jnp.zeros((1, LANES), F32)
    for h in range(heads):
        dq = dqt[h].T
        q = proj[:, h * LANES : (h + 1) * LANES].astype(F32)
        total = total + jnp.sum(dq * q, axis=0, keepdims=True)
        grads[:, h * LANES : (h + 1) * LANES] = (dq * scale[...]).astype(BF)
    scale_sum[...] = total / scale[...]


def inverse_rms(values):
    return lax.rsqrt(jnp.mean(values * values, axis=-1, keepdims=True) + EPSILON)


def stream_per_group(
    tokens,
    cotangent,
    doc_lengths,
    w_query,
    w_key,
    w_value,
    w_out,
    w_up,
    w_down,
    gain_attn,
    gain_mlp,
    query_scale,
):
    groups, tok_rows, width = tokens.shape
    count = lax.axis_size("ctx")
    members = count // groups
    size = query_scale.shape[0]
    local = w_query.shape[1]
    heads = local // size // members
    half = tok_rows // 2
    stream = tok_rows * count
    mine = heads * size
    block = 256
    me = lax.axis_index("ctx")
    z, j, c = me // members, me % members, lax.axis_index("tp")
    ids = jnp.stack([z, j, c]).astype(jnp.int32)

    def across(a, mask):
        return lax.ppermute(a, "ctx", [(i, i ^ mask) for i in range(count)])

    def swap(a):
        return lax.ppermute(a, "tp", [(0, 1), (1, 0)])

    def by_group(a):
        parts = []
        for kz in range(groups):
            part = lax.dynamic_index_in_dim(a, z ^ kz, 0, keepdims=False)
            parts.append(across(part, kz * members) if kz else part)
        return parts

    def natural(a, number, own):
        return jnp.stack(
            [lax.dynamic_index_in_dim(a, own ^ k, 0, keepdims=False) for k in range(number)]
        )

    lengths = lax.dynamic_index_in_dim(doc_lengths, z, 0, keepdims=False)
    ends = jnp.cumsum(lengths)
    starts = ends - lengths
    positions = jnp.arange(stream, dtype=jnp.int32)
    before = starts[:, None] <= positions[None, :]
    doc = jnp.max(jnp.where(before, starts[:, None], 0), axis=0, keepdims=True)
    doc_end = jnp.max(jnp.where(before, ends[:, None], 0), axis=0)
    first = doc[0, ::block] // block
    last = (doc_end[block - 1 :: block] + block - 1) // block

    def half_rows(a):
        return lax.dynamic_slice_in_dim(a, c * half, half, axis=1)

    own_piece = jnp.stack(by_group(half_rows(tokens)))
    pieces = [own_piece] + [across(own_piece, kj) for kj in range(1, members)]
    pieces = pieces + [swap(piece) for piece in pieces]

    packed = jnp.stack(
        [
            jnp.concatenate(
                [w[:, k * mine : (k + 1) * mine] for w in (w_query, w_key, w_value)]
                + [gain_attn[:, None], gain_mlp[:, None]]
                + [jnp.zeros((w_query.shape[0], 30), BF)],
                axis=1,
            )
            for k in range(members)
        ]
    )
    cols = [lax.dynamic_index_in_dim(packed, j ^ kj, 0, keepdims=False) for kj in range(members)]
    cols = jnp.stack([cols[0]] + [across(cols[kj], kj) for kj in range(1, members)])
    cols = natural(cols, members, j)
    cols = jnp.stack([cols] + [across(cols, kz * members) for kz in range(1, groups)])
    cols = natural(cols, groups, z).reshape(width, -1)
    gain_one = cols[:, 3 * mine].astype(F32)[None, :]
    gain_two = cols[:, 3 * mine + 1].astype(F32)[None, :]
    w_qkv = jnp.pad(
        cols[:, : 3 * mine].reshape(width, 3 * heads, size), ((0, 0), (0, 0), (0, LANES - size))
    ).reshape(width, 3 * heads * LANES)
    scale_row = jnp.pad(query_scale, (0, LANES - size), constant_values=1.0)[None, :]
    scale_all = jnp.concatenate(
        [scale_row] * heads + [jnp.ones((1, 2 * heads * LANES), F32)], axis=1
    )

    shards = jnp.concatenate([w_up, w_out.T, w_down.T], axis=1)
    whole = lax.all_gather(shards, "ctx", axis=0, tiled=True)
    up_full = whole[:, :local]
    out_t = whole[:, local : 2 * local]
    down_t = whole[:, 2 * local :]

    g_own = jnp.stack(by_group(half_rows(cotangent)))
    g_low = assemble(ids, g_own, swap(g_own), BF).reshape(groups * tok_rows, width)
    x_low = assemble(ids, pieces[0], pieces[members], BF).reshape(groups * tok_rows, width)

    proj, normed = call(
        functools.partial(project_kernel, members, heads),
        (struct((stream, 3 * heads * LANES), BF), struct((stream, width), BF)),
        "s" + "v" * (2 * members + 3),
        flops=2 * stream * width * 3 * heads * LANES,
        moved=stream * width * 4,
    )(ids, *pieces, w_qkv, gain_one, scale_all)

    sent, kept = call(
        functools.partial(attend_kernel, heads, size, members, block),
        (
            struct((members, mine, groups * tok_rows), BF),
            struct((heads, LANES + 8, stream), F32),
        ),
        "ssvv",
        scratch=[pltpu.VMEM((heads, LANES, stream), BF)],
        flops=2 * stream * stream * LANES * heads,
        moved=stream * LANES * heads * 10,
    )(ids, first, proj, doc)

    arrived = jnp.stack([sent[0]] + [across(sent[kj], kj) for kj in range(1, members)])
    ob_t = natural(arrived, members, j).reshape(local, groups * tok_rows)

    attn = lax.dot_general(ob_t, out_t, (((0,), (1,)), ((), ())), preferred_element_type=F32)
    attn = attn.astype(BF)
    x = x_low.astype(F32)
    hidden = x + (attn.astype(F32) + swap(attn).astype(F32))
    scale_two = inverse_rms(hidden)
    normed_two = (hidden * scale_two * gain_two).astype(BF)
    up_raw = nn(normed_two, up_full)
    sigma = jax.nn.sigmoid(up_raw)
    activated = (up_raw * sigma).astype(BF)
    mlp = nt(activated, down_t).astype(BF)
    layer = (hidden + (mlp.astype(F32) + swap(mlp).astype(F32))).astype(BF)
    grad_act = nn(g_low, down_t)
    grad_up_raw = (grad_act * sigma * (1.0 + up_raw * (1.0 - sigma))).astype(BF)
    part_two = nt(grad_up_raw, up_full).astype(BF)
    grad_two = part_two.astype(F32) + swap(part_two).astype(F32)
    gain_two_part = jnp.sum(grad_two * hidden * scale_two, axis=0)
    weighted = grad_two * gain_two
    grad_hidden = (
        g_low.astype(F32)
        + scale_two * weighted
        - hidden * scale_two**3 * jnp.mean(weighted * hidden, axis=-1, keepdims=True)
    )
    hidden_low = grad_hidden.astype(BF)
    do_t = lax.dot_general(out_t, hidden_low, (((0,), (1,)), ((), ())), preferred_element_type=F32)
    do_t = do_t.astype(BF).reshape(members, mine, groups * tok_rows)
    do_pieces = []
    for kj in range(members):
        piece = lax.dynamic_index_in_dim(do_t, j ^ kj, 0, keepdims=False)
        do_pieces.append(across(piece, kj) if kj else piece)

    grad_weights = jnp.concatenate(
        [
            tn(normed_two, grad_up_raw).astype(BF),
            lax.dot_general(hidden_low, ob_t, (((0,), (1,)), ((), ())), preferred_element_type=F32).astype(BF),
            tn(g_low, activated).astype(BF),
        ],
        axis=1,
    )
    grad_shards = lax.psum_scatter(grad_weights, "ctx", scatter_dimension=0, tiled=True)

    grads, scale_part = call(
        functools.partial(attend_back_kernel, heads, size, members, block),
        (struct((stream, 3 * heads * LANES), BF), struct((1, LANES), F32)),
        "ssvvvv" + "v" * members,
        scratch=[
            pltpu.VMEM((heads, LANES, stream), BF),
            pltpu.VMEM((heads, stream, LANES), BF),
            pltpu.VMEM((heads, LANES, stream), BF),
            pltpu.VMEM((heads, LANES, stream), F32),
            pltpu.VMEM((heads, 8, stream), F32),
        ],
        flops=5 * stream * stream * LANES * heads,
        moved=stream * LANES * heads * 20,
    )(ids, last, proj, doc, kept, scale_row, *do_pieces)

    part_one = nt(grads, w_qkv).astype(BF).reshape(groups, members, 2, half, width)
    kept_half = lax.dynamic_index_in_dim(part_one, c, 2, keepdims=False)
    other_half = lax.dynamic_index_in_dim(part_one, 1 - c, 2, keepdims=False)
    both = (kept_half.astype(F32) + swap(other_half).astype(F32)).astype(BF)
    grad_one = None
    for kj in range(members):
        piece = lax.dynamic_index_in_dim(both, j ^ kj, 1, keepdims=False)
        piece = (across(piece, kj) if kj else piece).astype(F32)
        grad_one = piece if grad_one is None else grad_one + piece
    x_half = half_rows(x.reshape(groups, tok_rows, width))
    dh_half = half_rows(grad_hidden.reshape(groups, tok_rows, width))
    scale_one = inverse_rms(x_half)
    gain_one_part = jnp.sum(grad_one * x_half * scale_one, axis=(0, 1))
    weighted_one = grad_one * gain_one
    grad_x = (
        dh_half
        + scale_one * weighted_one
        - x_half * scale_one**3 * jnp.mean(weighted_one * x_half, axis=-1, keepdims=True)
    ).astype(BF)
    gx_own = jnp.stack(by_group(grad_x))
    grad_tokens = assemble(ids, gx_own, swap(gx_own), F32)
    out_own = jnp.stack(by_group(half_rows(layer.reshape(groups, tok_rows, width))))
    layer_out = assemble(ids, out_own, swap(out_own), BF)

    grad_qkv = tn(normed, grads).reshape(width, 3 * heads, LANES)[:, :, :size]
    grad_qkv = grad_qkv.reshape(groups, width // groups, 3 * mine).astype(BF)
    total = None
    for part in by_group(grad_qkv):
        total = part.astype(F32) if total is None else total + part.astype(F32)
    total = total.astype(BF).reshape(members, width // count, 3 * mine)
    rows = []
    for kj in range(members):
        piece = lax.dynamic_index_in_dim(total, j ^ kj, 0, keepdims=False)
        rows.append(across(piece, kj) if kj else piece)
    rows = natural(jnp.stack(rows), members, j).astype(F32)
    grad_q, grad_k, grad_v = (
        jnp.moveaxis(rows[:, :, k * mine : (k + 1) * mine], 0, 1).reshape(width // count, local)
        for k in range(3)
    )

    small = jnp.concatenate(
        [gain_one_part, jnp.where(c == 0, gain_two_part, 0.0), scale_part[0]], axis=0
    )
    small = lax.psum(small, ("ctx", "tp"))
    shard = width // count
    grad_gain_one = lax.dynamic_slice_in_dim(small, me * shard, shard)
    grad_gain_two = lax.dynamic_slice_in_dim(small, width + me * shard, shard)
    grad_shards = grad_shards.astype(F32)
    return (
        layer_out,
        grad_tokens,
        grad_q,
        grad_k,
        grad_v,
        grad_shards[:, local : 2 * local].T,
        grad_shards[:, :local],
        grad_shards[:, 2 * local :].T,
        grad_gain_one,
        grad_gain_two,
        small[2 * width : 2 * width + size],
    )


def fits(shapes, mesh):
    groups, stream, width = shapes[0].shape
    count, cores = mesh.shape["ctx"], mesh.shape["tp"]
    size = shapes[11].shape[0]
    if cores != 2 or count % groups:
        return False
    members = count // groups
    local_heads = shapes[3].shape[1] // cores // size
    return (
        groups & (groups - 1) == 0
        and members & (members - 1) == 0
        and local_heads % members == 0
        and stream // count == LANES
        and stream % 256 == 0
        and members % 2 == 0
        and size % 16 == 0
        and size <= LANES
        and width % (LANES * 2) == 0
    )


def segment_of(starts, positions):
    return jnp.sum((starts[None, :] <= positions[:, None]).astype(jnp.int32), axis=1)


def contract_rows(left, right):
    return lax.dot_general(
        left, right, (((0,), (0,)), ((), ())), preferred_element_type=jnp.float32
    )


def contract_cols(left, right):
    return lax.dot_general(
        left, right, (((1,), (1,)), ((), ())), preferred_element_type=jnp.float32
    )


def per_device(
    tokens,
    cotangent,
    doc_lengths,
    w_query,
    w_key,
    w_value,
    w_out,
    w_up,
    w_down,
    gain_attn,
    gain_mlp,
    query_scale,
):
    micro_count, tok_rows, model_width = tokens.shape
    head_size = query_scale.shape[0]
    local_cols = w_query.shape[1]
    head_count = local_cols // head_size
    stream = tok_rows * lax.axis_size("ctx")
    key_block = min(512, stream)
    block_count = stream // key_block
    positions = lax.axis_index("ctx") * tok_rows + jnp.arange(tok_rows, dtype=jnp.int32)
    local_sums = None
    scale_sum = jnp.zeros((head_size,), jnp.float32)
    outputs = []
    input_grads = []
    for micro_step in range(micro_count):
        gathered = (
            lax.all_gather(w_query, "ctx", axis=0, tiled=True),
            lax.all_gather(w_key, "ctx", axis=0, tiled=True),
            lax.all_gather(w_value, "ctx", axis=0, tiled=True),
            lax.all_gather(w_up, "ctx", axis=0, tiled=True),
            lax.all_gather(gain_attn, "ctx", axis=0, tiled=True),
            lax.all_gather(gain_mlp, "ctx", axis=0, tiled=True),
            lax.all_gather(w_out, "ctx", axis=1, tiled=True),
            lax.all_gather(w_down, "ctx", axis=1, tiled=True),
        )
        w_qkv = jnp.concatenate([gathered[0], gathered[1], gathered[2]], axis=1)
        up_full = gathered[3]
        gain_one = gathered[4].astype(jnp.float32)
        gain_two = gathered[5].astype(jnp.float32)
        out_full = gathered[6]
        down_full = gathered[7]
        lengths = doc_lengths[micro_step]
        starts = jnp.cumsum(lengths) - lengths
        query_seg = segment_of(starts, positions)
        stream_in = tokens[micro_step].astype(jnp.float32)
        scale_one = inverse_rms(stream_in)
        normed_one = (stream_in * scale_one * gain_one).astype(jnp.bfloat16)
        projected = jnp.dot(normed_one, w_qkv, preferred_element_type=jnp.float32)
        query_raw = projected[:, :local_cols].reshape(tok_rows, head_count, head_size)
        query_heads = (query_raw * query_scale).astype(jnp.bfloat16)
        key_local = projected[:, local_cols : 2 * local_cols].astype(jnp.bfloat16)
        value_local = projected[:, 2 * local_cols :].astype(jnp.bfloat16)
        row_top = jnp.full((head_count, tok_rows), MASKED, jnp.float32)
        key_piece = lax.all_gather(key_local, "ctx", axis=0, tiled=True)
        value_piece = lax.all_gather(value_local, "ctx", axis=0, tiled=True)
        length = key_piece.shape[0]
        key_pos = jnp.arange(length, dtype=jnp.int32)
        allowed = (key_pos[None, :] <= positions[:, None]) & (
            segment_of(starts, key_pos)[None, :] == query_seg[:, None]
        )
        scores = jnp.einsum(
            "qhd,khd->hqk",
            query_heads,
            key_piece.reshape(length, head_count, head_size),
            preferred_element_type=jnp.float32,
        )
        scores = jnp.where(allowed[None], scores, MASKED)
        new_top = jnp.maximum(row_top, jnp.max(scores, axis=-1))
        probs = jnp.where(allowed[None], jnp.exp(scores - new_top[:, :, None]), 0.0)
        row_sum = jnp.sum(probs, axis=-1)
        update = jnp.einsum(
            "hqk,khd->qhd",
            probs.astype(jnp.bfloat16),
            value_piece.reshape(length, head_count, head_size),
            preferred_element_type=jnp.float32,
        )
        weighted = update
        row_top, row_sum, weighted = (new_top, row_sum, weighted)
        attn_heads = weighted / jnp.transpose(row_sum)[:, :, None]
        log_total = row_top + jnp.log(row_sum)
        attn_low = attn_heads.reshape(tok_rows, local_cols).astype(jnp.bfloat16)
        attn_out = lax.psum(
            jnp.dot(attn_low, out_full, preferred_element_type=jnp.float32).astype(jnp.bfloat16),
            "tp",
        ).astype(jnp.float32)
        hidden = stream_in + attn_out
        scale_two = inverse_rms(hidden)
        normed_two = (hidden * scale_two * gain_two).astype(jnp.bfloat16)
        up_raw = jnp.dot(normed_two, up_full, preferred_element_type=jnp.float32)
        activated = jax.nn.silu(up_raw).astype(jnp.bfloat16)
        mlp_out = lax.psum(
            jnp.dot(activated, down_full, preferred_element_type=jnp.float32).astype(jnp.bfloat16),
            "tp",
        ).astype(jnp.float32)
        outputs.append((hidden + mlp_out).astype(jnp.bfloat16))
        grad_out = cotangent[micro_step]
        grad_down = contract_rows(activated, grad_out)
        grad_act = contract_cols(grad_out, down_full)
        sigma = jax.nn.sigmoid(up_raw)
        grad_up_raw = (grad_act * sigma * (1.0 + up_raw * (1.0 - sigma))).astype(jnp.bfloat16)
        grad_up = contract_rows(normed_two, grad_up_raw)
        grad_normed_two = lax.psum(
            contract_cols(grad_up_raw, up_full).astype(jnp.bfloat16), "tp"
        ).astype(jnp.float32)
        grad_gain_two = jnp.sum(grad_normed_two * hidden * scale_two, axis=0)
        weighted_two = grad_normed_two * gain_two
        grad_hidden = (
            grad_out.astype(jnp.float32)
            + scale_two * weighted_two
            - hidden * scale_two**3 * jnp.mean(weighted_two * hidden, axis=-1, keepdims=True)
        )
        hidden_low = grad_hidden.astype(jnp.bfloat16)
        grad_out_proj = contract_rows(attn_low, hidden_low)
        grad_attn = (
            contract_cols(hidden_low, out_full)
            .astype(jnp.bfloat16)
            .reshape(tok_rows, head_count, head_size)
        )
        delta = jnp.einsum("qhd,qhd->hq", grad_attn.astype(jnp.float32), attn_heads)
        key_all, value_all = (
            lax.all_gather(key_local, "ctx", axis=0, tiled=True),
            lax.all_gather(value_local, "ctx", axis=0, tiled=True),
        )

        def block_terms(key_piece, value_piece, offset):
            key_heads = key_piece.reshape(key_block, head_count, head_size)
            value_heads = value_piece.reshape(key_block, head_count, head_size)
            key_pos = offset + jnp.arange(key_block, dtype=jnp.int32)
            allowed = (key_pos[None, :] <= positions[:, None]) & (
                segment_of(starts, key_pos)[None, :] == query_seg[:, None]
            )
            scores = jnp.einsum(
                "qhd,khd->hqk", query_heads, key_heads, preferred_element_type=jnp.float32
            )
            probs = jnp.where(allowed[None], jnp.exp(scores - log_total[:, :, None]), 0.0)
            grad_probs = jnp.einsum(
                "qhd,khd->hqk", grad_attn, value_heads, preferred_element_type=jnp.float32
            )
            grad_scores = (probs * (grad_probs - delta[:, :, None])).astype(jnp.bfloat16)
            return (key_heads, probs, grad_scores)

        key_blocks = (
            key_all.reshape(block_count, key_block, local_cols),
            value_all.reshape(block_count, key_block, local_cols),
            jnp.arange(block_count, dtype=jnp.int32) * key_block,
        )
        zero_query = jnp.zeros((tok_rows, head_count, head_size), jnp.float32)

        def grad_block(grad_query, packed):
            key_heads, probs, grad_scores = block_terms(packed[0], packed[1], packed[2])
            grad_value = jnp.einsum(
                "hqk,qhd->khd",
                probs.astype(jnp.bfloat16),
                grad_attn,
                preferred_element_type=jnp.float32,
            )
            grad_query = grad_query + jnp.einsum(
                "hqk,khd->qhd", grad_scores, key_heads, preferred_element_type=jnp.float32
            )
            grad_key = jnp.einsum(
                "hqk,qhd->khd", grad_scores, query_heads, preferred_element_type=jnp.float32
            )
            return (
                grad_query,
                (
                    grad_key.reshape(key_block, local_cols),
                    grad_value.reshape(key_block, local_cols),
                ),
            )

        grad_query, (key_terms, value_terms) = lax.scan(grad_block, zero_query, key_blocks)
        key_grad, value_grad = (
            lax.psum_scatter(
                key_terms.reshape(stream, local_cols).astype(jnp.bfloat16),
                "ctx",
                scatter_dimension=0,
                tiled=True,
            ).astype(jnp.float32),
            lax.psum_scatter(
                value_terms.reshape(stream, local_cols).astype(jnp.bfloat16),
                "ctx",
                scatter_dimension=0,
                tiled=True,
            ).astype(jnp.float32),
        )
        grad_query_raw = (
            (grad_query * query_scale).astype(jnp.bfloat16).reshape(tok_rows, local_cols)
        )
        scale_part = jnp.sum(grad_query * query_raw, axis=(0, 1))
        grad_cols = jnp.concatenate(
            [grad_query_raw, key_grad.astype(jnp.bfloat16), value_grad.astype(jnp.bfloat16)], axis=1
        )
        grad_qkv = contract_rows(normed_one, grad_cols)
        grad_normed_one, scale_total = (
            lax.psum(contract_cols(grad_cols, w_qkv).astype(jnp.bfloat16), "tp").astype(
                jnp.float32
            ),
            lax.psum(scale_part.astype(jnp.bfloat16), "tp").astype(jnp.float32),
        )
        scale_sum = scale_sum + scale_total
        grad_gain_one = jnp.sum(grad_normed_one * stream_in * scale_one, axis=0)
        weighted_one = grad_normed_one * gain_one
        input_grads.append(
            grad_hidden
            + scale_one * weighted_one
            - stream_in * scale_one**3 * jnp.mean(weighted_one * stream_in, axis=-1, keepdims=True)
        )
        grads = (
            grad_qkv[:, :local_cols],
            grad_qkv[:, local_cols : 2 * local_cols],
            grad_qkv[:, 2 * local_cols :],
            grad_up,
            grad_gain_one,
            grad_gain_two,
            grad_out_proj,
            grad_down,
        )
        shares = (
            lax.psum_scatter(
                grads[0].astype(jnp.bfloat16), "ctx", scatter_dimension=0, tiled=True
            ).astype(jnp.float32),
            lax.psum_scatter(
                grads[1].astype(jnp.bfloat16), "ctx", scatter_dimension=0, tiled=True
            ).astype(jnp.float32),
            lax.psum_scatter(
                grads[2].astype(jnp.bfloat16), "ctx", scatter_dimension=0, tiled=True
            ).astype(jnp.float32),
            lax.psum_scatter(
                grads[3].astype(jnp.bfloat16), "ctx", scatter_dimension=0, tiled=True
            ).astype(jnp.float32),
            lax.psum_scatter(
                grads[4].astype(jnp.bfloat16), "ctx", scatter_dimension=0, tiled=True
            ).astype(jnp.float32),
            lax.psum_scatter(
                grads[5].astype(jnp.bfloat16), "ctx", scatter_dimension=0, tiled=True
            ).astype(jnp.float32),
            lax.psum_scatter(
                grads[6].astype(jnp.bfloat16), "ctx", scatter_dimension=1, tiled=True
            ).astype(jnp.float32),
            lax.psum_scatter(
                grads[7].astype(jnp.bfloat16), "ctx", scatter_dimension=1, tiled=True
            ).astype(jnp.float32),
        )
        local_sums = (
            shares
            if local_sums is None
            else tuple((total + extra for total, extra in zip(local_sums, shares)))
        )
    scale_grad = lax.psum(scale_sum, "ctx")
    return (
        jnp.stack(outputs),
        jnp.stack(input_grads),
        local_sums[0],
        local_sums[1],
        local_sums[2],
        local_sums[6],
        local_sums[3],
        local_sums[7],
        local_sums[4],
        local_sums[5],
        scale_grad,
    )


def solution(mesh):
    in_specs = (
        P(None, "ctx", None),
        P(None, "ctx", None),
        P(),
        P("ctx", "tp"),
        P("ctx", "tp"),
        P("ctx", "tp"),
        P("tp", "ctx"),
        P("ctx", "tp"),
        P("tp", "ctx"),
        P("ctx"),
        P("ctx"),
        P(),
    )
    out_specs = (
        P(None, "ctx", None),
        P(None, "ctx", None),
        P("ctx", "tp"),
        P("ctx", "tp"),
        P("ctx", "tp"),
        P("tp", "ctx"),
        P("ctx", "tp"),
        P("tp", "ctx"),
        P("ctx"),
        P("ctx"),
        P(),
    )

    def run(*arrays):
        body = stream_per_group if fits(arrays, mesh) else per_device
        return jax.shard_map(
            body, mesh=mesh, in_specs=in_specs, out_specs=out_specs, check_vma=False
        )(*arrays)

    return run
```

```python
import functools
import math

import jax
import jax.numpy as jnp
from jax import lax
from jax.experimental import pallas as pl
from jax.experimental.pallas import tpu as pltpu
from jax.sharding import PartitionSpec as P

EPSILON = 1e-06
MASKED = -1e30
LANES = 128
WIDE = 512
BF = jnp.bfloat16
F32 = jnp.float32
SPARE_VMEM = 12 * 1024 * 1024


def call(kernel, out_shape, kinds, scratch=(), flops=0, moved=0, aliases=None):
    vmem = pl.BlockSpec(memory_space=pltpu.VMEM)
    smem = pl.BlockSpec(memory_space=pltpu.SMEM)
    hbm = pl.BlockSpec(memory_space=pl.ANY)
    room = sum(
        math.prod(ref.shape) * jnp.dtype(ref.dtype).itemsize
        for ref in scratch
        if ref.memory_space == pltpu.VMEM
    )
    return pl.pallas_call(
        kernel,
        out_shape=out_shape,
        in_specs=[{"s": smem, "v": vmem, "h": hbm}[kind] for kind in kinds],
        out_specs=jax.tree.map(lambda _: vmem, out_shape),
        scratch_shapes=list(scratch),
        input_output_aliases=aliases or {},
        compiler_params=pltpu.CompilerParams(vmem_limit_bytes=room + SPARE_VMEM),
        cost_estimate=pl.CostEstimate(
            flops=int(flops), transcendentals=0, bytes_accessed=int(moved)
        ),
    )


def struct(shape, dtype):
    return jax.ShapeDtypeStruct(tuple(shape), dtype)


def nn(a, b):
    return jnp.dot(a, b, preferred_element_type=F32)


def nt(a, b):
    return lax.dot_general(a, b, (((1,), (1,)), ((), ())), preferred_element_type=F32)


def tn(a, b):
    return lax.dot_general(a, b, (((0,), (0,)), ((), ())), preferred_element_type=F32)


def at(start, size, step=None):
    return pl.ds(pl.multiple_of(start, step or size), size)


def inverse_rms(values):
    return lax.rsqrt(jnp.mean(values * values, axis=-1, keepdims=True) + EPSILON)


def split_kernel(ids, whole, *out):
    z, c = ids[0], ids[2]
    half = out[0].shape[0]
    for kz in range(len(out)):
        out[kz][...] = whole[z ^ kz, at(c * half, half), :]


def split(ids, whole):
    groups, rows, width = whole.shape
    return call(
        split_kernel,
        (struct((rows // 2, width), whole.dtype),) * groups,
        "sv",
        moved=whole.size * 4,
    )(ids, whole)


def assemble_kernel(ids, own, other, out):
    groups, half, _ = own.shape
    c = ids[2]
    for kz in range(groups):
        out[ids[0] ^ kz, at(c * half, half), :] = own[kz].astype(out.dtype)
        out[ids[0] ^ kz, at((1 - c) * half, half), :] = other[kz].astype(out.dtype)


def assemble(ids, own, other, dtype):
    groups, half, width = own.shape
    return call(
        assemble_kernel, struct((groups, 2 * half, width), dtype), "svv", moved=own.size * 12
    )(ids, own, other)


def place_kernel(groups, ids, *refs):
    own, other, out = refs[:groups], refs[groups : 2 * groups], refs[2 * groups]
    half = own[0].shape[0]
    z, c = ids[0], ids[2]
    for kz in range(groups):
        out[z ^ kz, at(c * half, half), :] = own[kz][...].astype(out.dtype)
        out[z ^ kz, at((1 - c) * half, half), :] = other[kz][...].astype(out.dtype)


def pack_kernel(mine, ids, query, key, value, gains, *refs):
    out, tmp = refs[:-1], refs[-1]
    rows = query.shape[0]
    rest = jnp.concatenate([gains[...], jnp.zeros((rows, WIDE - 3 * mine - 2), BF)], axis=1)
    for k in range(len(out)):
        cols = slice(k * mine, (k + 1) * mine)
        tmp[k] = jnp.concatenate([query[:, cols], key[:, cols], value[:, cols], rest], axis=1)
    for kj in range(len(out)):
        out[kj][...] = tmp[ids[1] ^ kj]


def stack_kernel(up, out_t, down_t, out):
    cols = up.shape[1]
    for g in range(out.shape[0]):
        for n, part in enumerate((up, out_t, down_t)):
            out[g, :, n * cols : (n + 1) * cols] = part[...]


def spread_kernel(heads, size, ids, pieces, w, w_t, gains, rows_ref):
    groups, members, rows, _ = pieces.shape
    for kz in range(groups):
        for kj in range(members):
            where = at((kz * members + (ids[1] ^ kj)) * rows, rows, 16)
            rows_ref[where, :] = pieces[kz, kj]
    block = rows_ref[...]
    zeros = jnp.zeros((block.shape[0], LANES - size), BF)
    for h in range(3 * heads):
        w[:, h * LANES : (h + 1) * LANES] = jnp.concatenate(
            [block[:, h * size : (h + 1) * size], zeros], axis=1
        )
    w_t[...] = w[...].T
    first = 3 * heads * size - (WIDE - LANES)
    gains[...] = block[:, WIDE - LANES :].astype(F32).T[first : first + 8, :]


def order_kernel(ids, *refs):
    pieces, out = refs[:-3], refs[-3:]
    groups, rows, _ = pieces[0].shape
    members, cols = len(pieces), out[0].shape[1]
    for kj in range(members):
        for kz in range(groups):
            where = at((kz * members + (ids[1] ^ kj)) * rows, rows, 16)
            for n in range(3):
                out[n][where, :] = pieces[kj][kz, :, n * cols : (n + 1) * cols]


def project_kernel(members, ids, *refs):
    pieces = refs[: 2 * members]
    w, gains, scale, proj, normed = refs[2 * members :]
    groups, half, width = pieces[0].shape
    z, j, c = ids[0], ids[1], ids[2]
    for kj in range(members):
        for kc in range(2):
            x = pieces[kc * members + kj][...].reshape(groups * half, width).astype(F32)
            xn = (x * inverse_rms(x) * gains[0:1, :]).astype(BF)
            y = (nn(xn, w[...]) * scale[...]).astype(BF)
            for kz in range(groups):
                base = (z ^ kz) * (members * 2) + (j ^ kj) * 2 + (c ^ kc)
                normed[at(base * half, half), :] = xn[kz * half : (kz + 1) * half]
                proj[at(base * half, half), :] = y[kz * half : (kz + 1) * half]


def doc_bounds(lengths, z, place):
    start, begin, end = jnp.int32(0), jnp.int32(0), jnp.int32(0)
    for d in range(lengths.shape[1]):
        stop = start + lengths[z, d]
        inside = start <= place
        begin = jnp.where(inside, start, begin)
        end = jnp.where(inside, stop, end)
        start = stop
    return begin, end


def doc_starts(lengths, z, stream):
    place = lax.broadcasted_iota(jnp.int32, (8, stream), 1)
    start, row = jnp.int32(0), jnp.zeros((8, stream), jnp.int32)
    for d in range(lengths.shape[1]):
        row = jnp.where(place >= start, start, row)
        start = start + lengths[z, d]
    return row


def attend_kernel(heads, size, members, bq, bk, ids, lengths, proj, *refs):
    outs, (kept, sent, vt, doc) = refs[:members], refs[members:]
    stream = proj.shape[0]
    z, j = ids[0], ids[1]
    doc[...] = doc_starts(lengths, z, stream)
    for h in range(heads):
        vt[h] = proj[:, (2 * heads + h) * LANES : (2 * heads + h + 1) * LANES].T

    def one_query_block(qb, _):
        rows = at(qb * bq, bq)
        qpos = qb * bq + lax.broadcasted_iota(jnp.int32, (1, bq), 1)
        queries = [proj[rows, h * LANES : (h + 1) * LANES] for h in range(heads)]

        def one_key_block(masked, kb, carry):
            keys = at(kb * bk, bk)
            if masked:
                kpos = kb * bk + lax.broadcasted_iota(jnp.int32, (bk, bq), 0)
                allowed = (kpos <= qpos) & (kpos >= doc[0:1, rows])
            new = []
            for h in range(heads):
                top, total, acc = carry[h]
                k = proj[keys, (heads + h) * LANES : (heads + h + 1) * LANES]
                s = nt(k, queries[h])
                if masked:
                    s = jnp.where(allowed, s, MASKED)
                top2 = jnp.maximum(top, jnp.max(s, axis=0, keepdims=True))
                p = jnp.exp(s - top2)
                alpha = jnp.exp(top - top2)
                total = total * alpha + jnp.sum(p, axis=0, keepdims=True)
                acc = acc * alpha + nn(vt[h, :, keys], p.astype(BF))
                new.append((top2, total, acc))
            return tuple(new)

        zero = (
            jnp.full((1, bq), MASKED, F32),
            jnp.zeros((1, bq), F32),
            jnp.zeros((LANES, bq), F32),
        )
        begin, _ = doc_bounds(lengths, z, qb * bq)
        late, _ = doc_bounds(lengths, z, qb * bq + bq - 1)
        first, whole, diagonal = begin // bk, (late + bk - 1) // bk, qb * bq // bk
        whole = jnp.minimum(whole, diagonal)
        masked = functools.partial(one_key_block, True)
        carry = lax.fori_loop(first, whole, masked, (zero,) * heads)
        carry = lax.fori_loop(whole, diagonal, functools.partial(one_key_block, False), carry)
        carry = lax.fori_loop(diagonal, (qb * bq + bq + bk - 1) // bk, masked, carry)
        for h in range(heads):
            top, total, acc = carry[h]
            o = acc / total
            kept[h, :LANES, rows] = o
            kept[h, LANES:, rows] = jnp.broadcast_to(top + jnp.log(total), (8, bq))
            low = o[:size].astype(BF)
            for part in range(bq // LANES):
                block = qb * (bq // LANES) + part
                lanes = at(block // members * LANES, LANES)
                sent[(block % members) ^ j, h * size : (h + 1) * size, lanes] = low[
                    :, part * LANES : (part + 1) * LANES
                ]
        return 0

    lax.fori_loop(0, stream // bq, one_query_block, 0)
    for kj in range(members):
        outs[kj][...] = sent[kj]


def attend_back_kernel(heads, size, members, bq, bk, ids, lengths, proj, kept, scale, *refs):
    pieces = refs[:members]
    grads, scale_sum, dot_, do_, kt, dqt, delta, doc = refs[members:]
    stream = proj.shape[0]
    groups = pieces[0].shape[1] // LANES
    z, j = ids[0], ids[1]
    doc[...] = doc_starts(lengths, z, stream)
    for h in range(heads):
        kt[h] = proj[:, (heads + h) * LANES : (heads + h + 1) * LANES].T
        dot_[h, size:, :] = jnp.zeros((LANES - size, stream), BF)
        for kj in range(members):
            for g in range(groups):
                lanes = at((g * members + (j ^ kj)) * LANES, LANES)
                dot_[h, :size, lanes] = pieces[kj][
                    h * size : (h + 1) * size, g * LANES : (g + 1) * LANES
                ]
        do_[h] = dot_[h].T
        delta[h] = jnp.broadcast_to(
            jnp.sum(dot_[h].astype(F32) * kept[h, :LANES, :], axis=0, keepdims=True), (8, stream)
        )
        dqt[h] = jnp.zeros((LANES, stream), F32)

    def one_key_block(kb, _):
        keys = at(kb * bk, bk)
        kpos = kb * bk + lax.broadcasted_iota(jnp.int32, (bk, bq), 0)
        ks = [proj[keys, (heads + h) * LANES : (heads + h + 1) * LANES] for h in range(heads)]
        vs = [
            proj[keys, (2 * heads + h) * LANES : (2 * heads + h + 1) * LANES] for h in range(heads)
        ]

        def one_query_block(masked, qb, carry):
            rows = at(qb * bq, bq)
            if masked:
                qpos = qb * bq + lax.broadcasted_iota(jnp.int32, (1, bq), 1)
                allowed = (kpos <= qpos) & (kpos >= doc[0:1, rows])
            new = []
            for h in range(heads):
                dk, dv = carry[h]
                q = proj[rows, h * LANES : (h + 1) * LANES]
                p = jnp.exp(nt(ks[h], q) - kept[h, LANES : LANES + 1, rows])
                if masked:
                    p = jnp.where(allowed, p, 0.0)
                dp = nn(vs[h], dot_[h, :, rows])
                ds = (p * (dp - delta[h, 0:1, rows])).astype(BF)
                dv = dv + nn(p.astype(BF), do_[h, rows, :])
                dk = dk + nn(ds, q)
                dqt[h, :, rows] += nn(kt[h, :, keys], ds)
                new.append((dk, dv))
            return tuple(new)

        _, early = doc_bounds(lengths, z, kb * bk)
        _, final = doc_bounds(lengths, z, kb * bk + bk - 1)
        first = kb * bk // bq
        open_ = (kb * bk + bk + bq - 1) // bq
        last = (final + bq - 1) // bq
        open_ = jnp.minimum(open_, last)
        shut = jnp.maximum(jnp.minimum(early // bq, last), open_)
        zero = jnp.zeros((bk, LANES), F32)
        masked = functools.partial(one_query_block, True)
        carry = lax.fori_loop(first, open_, masked, ((zero, zero),) * heads)
        carry = lax.fori_loop(open_, shut, functools.partial(one_query_block, False), carry)
        carry = lax.fori_loop(shut, last, masked, carry)
        for h in range(heads):
            for n in range(2):
                cols = ((n + 1) * heads + h) * LANES
                grads[keys, cols : cols + LANES] = carry[h][n].astype(BF)
        return 0

    lax.fori_loop(0, stream // bk, one_key_block, 0)
    total = jnp.zeros((1, LANES), F32)
    for h in range(heads):
        dq = dqt[h].T
        q = proj[:, h * LANES : (h + 1) * LANES].astype(F32)
        total = total + jnp.sum(dq * q, axis=0, keepdims=True)
        grads[:, h * LANES : (h + 1) * LANES] = (dq * scale[...]).astype(BF)
    scale_sum[...] = jnp.broadcast_to(total / scale[...], (LANES, LANES)).T


def out_kernel(ids, *refs):
    pieces, (w, ob_t, part) = refs[:-3], refs[-3:]
    mine = pieces[0].shape[0]
    for kj in range(len(pieces)):
        ob_t[at((ids[1] ^ kj) * mine, mine, 16), :] = pieces[kj][...]
    part[...] = nt(ob_t[...].T, w[...]).astype(BF)


def mlp_kernel(groups, ids, *refs):
    x_own, x_other = refs[0], refs[1]
    g_own, g_other, attn, attn_other, up, down, gains = refs[2:9]
    hidden, normed, act, grad_up, cot, part, back = refs[9:]
    half = x_own.shape[1]
    z, c = ids[0], ids[2]
    for kz in range(groups):
        for kc in range(2):
            rows = at((z ^ kz) * (2 * half) + (c ^ kc) * half, half)
            hidden[rows, :] = (x_other if kc else x_own)[kz].astype(F32) + (
                attn[rows, :].astype(F32) + attn_other[rows, :].astype(F32)
            )
            cot[rows, :] = (g_other if kc else g_own)[kz]
    step = hidden.shape[0] // 2
    for r in range(2):
        rows = slice(r * step, (r + 1) * step)
        h = hidden[rows, :]
        xn = (h * inverse_rms(h) * gains[1:2, :]).astype(BF)
        u = nn(xn, up[...])
        sigma = jax.nn.sigmoid(u)
        a = (u * sigma).astype(BF)
        da = nn(cot[rows, :], down[...])
        du = (da * sigma * (1.0 + u * (1.0 - sigma))).astype(BF)
        part[rows, :] = nt(a, down[...]).astype(BF)
        back[rows, :] = nt(du, up[...]).astype(BF)
        normed[rows, :] = xn
        act[rows, :] = a
        grad_up[rows, :] = du


def hidden_kernel(groups, members, ids, *refs):
    hidden, cot, part, part_other, back, back_other, w, gains = refs[:8]
    low, dh_half = refs[8:10]
    pieces, out = refs[10 : 10 + members], refs[10 + members : 10 + members + groups]
    dh, lay, do_t = refs[10 + members + groups :]
    rows_all = hidden.shape[0]
    half = rows_all // groups // 2
    mine = pieces[0].shape[0]
    z, j, c = ids[0], ids[1], ids[2]
    step = rows_all // 2
    for r in range(2):
        rows = slice(r * step, (r + 1) * step)
        h = hidden[rows, :]
        scale = inverse_rms(h)
        grad = back[rows, :].astype(F32) + back_other[rows, :].astype(F32)
        weighted = grad * gains[1:2, :]
        d = (
            cot[rows, :].astype(F32)
            + scale * weighted
            - h * scale**3 * jnp.mean(weighted * h, axis=-1, keepdims=True)
        )
        dh[rows, :] = d
        low[rows, :] = d.astype(BF)
        lay[rows, :] = (
            h + (part[rows, :].astype(F32) + part_other[rows, :].astype(F32))
        ).astype(BF)
    do_t[...] = nn(low[...], w[...]).T.astype(BF)
    for kj in range(members):
        pieces[kj][...] = do_t[at((j ^ kj) * mine, mine, 16), :]
    for g in range(groups):
        out[g][...] = lay[at((z ^ g) * 2 * half + c * half, half), :]
        dh_half[g] = dh[at(g * 2 * half + c * half, half), :]


def by_member(ids, full, out, first=0):
    groups, rows, _ = out[0].shape
    for kj in range(len(out)):
        for g in range(groups):
            where = at((g * len(out) + (ids[1] ^ kj)) * rows, rows, 16)
            out[kj][g, :, first : first + full.shape[1]] = full[where, :]


def feed_weights_kernel(ids, normed, grad_up, cot, act, *refs):
    out, full = refs[:-1], refs[-1]
    full[...] = tn(normed[...], grad_up[...]).astype(BF)
    by_member(ids, full, out)
    full[...] = tn(cot[...], act[...]).astype(BF)
    by_member(ids, full, out, full.shape[1])


def out_weights_kernel(ids, low, ob_t, *refs):
    out, full = refs[:-1], refs[-1]
    full[...] = tn(low[...], ob_t[...].T).astype(BF)
    by_member(ids, full, out)


def sum_members_kernel(*refs):
    total = refs[0][...].astype(F32)
    for part in refs[1:-1]:
        total = total + part[...].astype(F32)
    refs[-1][...] = total.astype(BF)


def feed_rows_kernel(parts, up, grad_up, grad_down, gain):
    cols = up.shape[1]
    total = parts[0].astype(F32)
    for g in range(1, parts.shape[0]):
        total = total + parts[g].astype(F32)
    grad_up[...] = total[:, :cols]
    grad_down[...] = total[:, cols:].T
    term = jnp.sum(total[:, :cols] * up[...].astype(F32), axis=1, keepdims=True)
    gain[...] = jnp.broadcast_to(term, gain.shape)


def out_rows_kernel(parts, out):
    total = parts[0].astype(F32)
    for g in range(1, parts.shape[0]):
        total = total + parts[g].astype(F32)
    out[...] = total.T


def input_rows(ids, grads, rows_ref, kj, which, members, half):
    for g in range(rows_ref.shape[0] // half):
        base = (g * members + (ids[1] ^ kj)) * 2 + (ids[2] ^ which)
        rows_ref[g * half : (g + 1) * half, :] = grads[at(base * half, half), :]
    return rows_ref[...]


def input_there_kernel(ids, grads, w, out, rows_ref):
    members, groups, half, width = out.shape
    for kj in range(members):
        y = nn(input_rows(ids, grads, rows_ref, kj, 1, members, half), w[...])
        out[kj] = y.reshape(groups, half, width).astype(BF)


def input_here_kernel(ids, grads, w, other, *refs):
    out, rows_ref = refs[:-1], refs[-1]
    members, (groups, half, width) = len(out), out[0].shape
    for kj in reversed(range(members)):
        y = nn(input_rows(ids, grads, rows_ref, kj, 0, members, half), w[...])
        y = y + other[kj].reshape(groups * half, width).astype(F32)
        out[kj][...] = y.reshape(groups, half, width).astype(BF)


def qkv_weights_kernel(heads, size, count, normed, grads, scale_sum, out, full):
    full[...] = tn(normed[...], grads[...])
    rows = out.shape[0] // count
    pad = WIDE - 3 * heads * size
    s = scale_sum[:size, :pad]
    high = s.astype(BF)
    rest = (s - high.astype(F32)).astype(BF)
    lane = lax.broadcasted_iota(jnp.int32, (size, pad), 1)
    tail = jnp.where(lane == 0, high, jnp.where(lane == 1, rest, jnp.zeros_like(rest)))
    tail = [tail, jnp.zeros((rows - size, pad), BF)] if rows > size else [tail]
    tail = jnp.concatenate(tail, axis=0)
    for n in range(count):
        block = full[n * rows : (n + 1) * rows, :].astype(BF)
        out[n * rows : (n + 1) * rows, :] = jnp.concatenate(
            [block[:, h * LANES : h * LANES + size] for h in range(3 * heads)] + [tail], axis=1
        )


def qkv_sum_kernel(ids, parts, *refs):
    out, tmp = refs[:-1], refs[-1]
    total = parts[0].astype(F32)
    for g in range(1, parts.shape[0]):
        total = total + parts[g].astype(F32)
    tmp[...] = total
    rows = out[0].shape[0]
    for kj in range(len(out)):
        out[kj][...] = tmp[at((ids[1] ^ kj) * rows, rows, 16), :].astype(BF)


def qkv_rows_kernel(mine, ids, *refs):
    members = len(refs) - 8
    pieces, (query, key, value, dq, dk, dv, small, tmp) = refs[:members], refs[members:]
    for kj in range(members):
        tmp[ids[1] ^ kj] = pieces[kj][...].astype(F32)
    gain = None
    for n, (w, dw) in enumerate(((query, dq), (key, dk), (value, dv))):
        dw[...] = jnp.concatenate(
            [tmp[k][:, n * mine : (n + 1) * mine] for k in range(members)], axis=1
        )
        term = jnp.sum(dw[...] * w[...].astype(F32), axis=1, keepdims=True)
        gain = term if gain is None else gain + term
    scale = tmp[0][:, 3 * mine : 3 * mine + 2]
    for k in range(1, members):
        scale = scale + tmp[k][:, 3 * mine : 3 * mine + 2]
    scale = jnp.sum(scale, axis=1, keepdims=True)
    lane = lax.broadcasted_iota(jnp.int32, small.shape, 1)
    small[...] = jnp.where(lane == 0, gain, jnp.where(lane == 1, scale, 0.0))


def tokens_kernel(groups, ids, *refs):
    x, dh, gains = refs[:3]
    parts, out = refs[3:-groups], refs[-groups:]
    z = ids[0]
    for kz in range(groups):
        grad = parts[0][z ^ kz].astype(F32)
        for part in parts[1:]:
            grad = grad + part[z ^ kz].astype(F32)
        xx = x[kz].astype(F32)
        scale = inverse_rms(xx)
        weighted = grad * gains[0:1, :]
        out[kz][...] = (
            dh[z ^ kz]
            + scale * weighted
            - xx * scale**3 * jnp.mean(weighted * xx, axis=-1, keepdims=True)
        ).astype(BF)


def stream_per_group(
    tokens,
    cotangent,
    doc_lengths,
    w_query,
    w_key,
    w_value,
    w_out,
    w_up,
    w_down,
    gain_attn,
    gain_mlp,
    query_scale,
):
    groups, tok_rows, width = tokens.shape
    count = lax.axis_size("ctx")
    members = count // groups
    size = query_scale.shape[0]
    local = w_query.shape[1]
    shard = width // count
    heads = local // size // members
    half = tok_rows // 2
    stream = tok_rows * count
    mine = heads * size
    rows = groups * tok_rows
    padded = 3 * heads * LANES
    me = lax.axis_index("ctx")
    ids = jnp.stack([me // members, me % members, lax.axis_index("tp")]).astype(jnp.int32)

    planes = [[g * members + k for k in range(members)] for g in range(groups)]
    lines = [[g * members + k for g in range(groups)] for k in range(members)]

    def across(a, mask):
        return lax.ppermute(a, "ctx", [(i, i ^ mask) for i in range(count)])

    def shift(a, by):
        pairs = [(i, i + by * members) for i in range(count)]
        return lax.ppermute(a, "ctx", [(i, k) for i, k in pairs if 0 <= k < count])

    def swap(a):
        return lax.ppermute(a, "tp", [(0, 1), (1, 0)])

    def to_groups(parts):
        return [parts[0]] + [across(parts[k], k * members) for k in range(1, groups)]

    def to_members(parts):
        return [parts[0]] + [across(parts[k], k) for k in range(1, members)]

    def exchange(a, teams):
        return lax.all_to_all(a, "ctx", 0, 0, axis_index_groups=teams, tiled=True)

    def tie(*values):
        return lax.optimization_barrier(values)

    def quarter(own, beside, above):
        cut = groups // 2
        return jnp.concatenate([across(above[:cut], 1), across(beside[cut:], 2)])

    packed = call(
        functools.partial(pack_kernel, mine),
        (struct((shard, WIDE), BF),) * members,
        "svvvv",
        scratch=[pltpu.VMEM((members, shard, WIDE), BF)],
        moved=shard * WIDE * members * 4,
    )(ids, w_query, w_key, w_value, jnp.stack([gain_attn, gain_mlp], axis=1))
    own = jnp.stack(to_groups(split(ids, tokens)))

    shards = call(
        stack_kernel,
        struct((groups, shard, 3 * local), BF),
        "vvv",
        moved=groups * shard * local * 8,
    )(w_up, w_out.T, w_down.T)
    own, packed, shards = tie(own, packed, shards)
    shards = exchange(shards, lines)
    cols = jnp.stack(to_members(packed))
    pieces, cols, shards = tie(to_members([own] * members), cols, shards)
    cols = jnp.concatenate([cols] * groups)

    cols = exchange(cols, lines).reshape(groups, members, shard, WIDE)
    others = [swap(piece) for piece in pieces]
    if members == 4:
        beside, above = across(shards, 1), across(shards, 2)
        cols, others, beside, above = tie(cols, others, beside, above)
        shards = [shards, beside, above, quarter(shards, beside, above)]
    else:
        cols, others, shards = tie(cols, others, to_members([shards] * members))
    pieces = pieces + others
    g_parts, cols = tie(split(ids, cotangent), cols)
    g_own = to_groups(g_parts)
    w_qkv, w_qkv_t, gains = call(
        functools.partial(spread_kernel, heads, size),
        (struct((width, padded), BF), struct((padded, width), BF), struct((8, width), F32)),
        "sv",
        scratch=[pltpu.VMEM((width, WIDE), BF)],
        moved=width * padded * 6,
    )(ids, cols)
    scale_row = jnp.pad(query_scale, (0, LANES - size), constant_values=1.0)[None, :]
    scale_all = jnp.concatenate(
        [scale_row] * heads + [jnp.ones((1, 2 * heads * LANES), F32)], axis=1
    )

    proj, normed = call(
        functools.partial(project_kernel, members),
        (struct((stream, padded), BF), struct((stream, width), BF)),
        "s" + "v" * (2 * members + 3),
        flops=2 * stream * width * padded,
        moved=stream * width * 4,
    )(ids, *pieces, w_qkv, gains, scale_all)

    bq, bk = 512, 512
    *sent, kept = call(
        functools.partial(attend_kernel, heads, size, members, bq, bk),
        (struct((mine, rows), BF),) * members + (struct((heads, LANES + 8, stream), F32),),
        "ssv",
        scratch=[
            pltpu.VMEM((members, mine, rows), BF),
            pltpu.VMEM((heads, LANES, stream), BF),
            pltpu.VMEM((8, stream), jnp.int32),
        ],
        flops=2 * stream * stream * LANES * heads,
        moved=stream * LANES * heads * 10,
    )(ids, doc_lengths, proj)
    sent, shards, g_own = tie(sent, shards, g_own)
    arrived = to_members(sent)
    g_own = jnp.stack(g_own)
    g_other = swap(g_own)
    up_full, out_t, down_t = call(
        order_kernel,
        (struct((width, local), BF),) * 3,
        "s" + "v" * members,
        moved=width * local * 12,
    )(ids, *shards)

    ob_t, attn = call(
        out_kernel,
        (struct((local, rows), BF), struct((rows, width), BF)),
        "s" + "v" * (members + 1),
        flops=2 * rows * local * width,
        moved=local * width * 4,
    )(ids, *arrived, out_t)
    hidden, normed_two, activated, grad_up_raw, cot, part, back = call(
        functools.partial(mlp_kernel, groups),
        (
            struct((rows, width), F32),
            struct((rows, width), BF),
            struct((rows, local), BF),
            struct((rows, local), BF),
            struct((rows, width), BF),
            struct((rows, width), BF),
            struct((rows, width), BF),
        ),
        "s" + "v" * 9,
        flops=8 * rows * local * width,
        moved=local * width * 12,
    )(ids, pieces[0], pieces[members], g_own, g_other, attn, swap(attn), up_full, down_t, gains)
    back_other, part_other = swap(back), swap(part)
    feed_grads = call(
        feed_weights_kernel,
        (struct((groups, shard, 2 * local), BF),) * members,
        "svvvv",
        scratch=[pltpu.VMEM((width, local), BF)],
        flops=4 * rows * local * width,
        moved=local * width * 8,
    )(ids, normed_two, grad_up_raw, cot, activated)
    back_other, part_other, feed_grads = tie(back_other, part_other, feed_grads)
    hidden_low, dh_half, *results = call(
        functools.partial(hidden_kernel, groups, members),
        (struct((rows, width), BF), struct((groups, half, width), F32))
        + (struct((mine, rows), BF),) * members
        + (struct((half, width), BF),) * groups,
        "s" + "v" * 8,
        scratch=[
            pltpu.VMEM((rows, width), F32),
            pltpu.VMEM((rows, width), BF),
            pltpu.VMEM((local, rows), BF),
        ],
        flops=2 * rows * local * width,
        moved=local * width * 12,
    )(ids, hidden, cot, part, part_other, back, back_other, out_t, gains)
    do_pieces, out_parts = to_members(results[:members]), results[members:]
    out_grads = call(
        out_weights_kernel,
        (struct((groups, shard, local), BF),) * members,
        "svv",
        scratch=[pltpu.VMEM((width, local), BF)],
        flops=2 * rows * local * width,
        moved=local * width * 4,
    )(ids, hidden_low, ob_t)
    do_pieces, out_grads, out_parts, feed_grads = tie(do_pieces, out_grads, out_parts, feed_grads)

    feed_grads = to_members(feed_grads)
    out_own = to_groups(out_parts)

    def sum_members(parts):
        return call(
            sum_members_kernel,
            struct(parts[0].shape, BF),
            "v" * members,
            moved=parts[0].size * 12,
        )(*parts)

    grads, scale_sum = call(
        functools.partial(attend_back_kernel, heads, size, members, bq, bk),
        (struct((stream, padded), BF), struct((LANES, LANES), F32)),
        "ssvvv" + "v" * members,
        scratch=[
            pltpu.VMEM((heads, LANES, stream), BF),
            pltpu.VMEM((heads, stream, LANES), BF),
            pltpu.VMEM((heads, LANES, stream), BF),
            pltpu.VMEM((heads, LANES, stream), F32),
            pltpu.VMEM((heads, 8, stream), F32),
            pltpu.VMEM((8, stream), jnp.int32),
        ],
        flops=5 * stream * stream * LANES * heads,
        moved=stream * LANES * heads * 20,
    )(ids, doc_lengths, proj, kept, scale_row, *do_pieces)
    grads, feed_grads, out_own[1], out_own[2] = tie(grads, feed_grads, out_own[1], out_own[2])
    feed_grads = exchange(sum_members(feed_grads), lines)
    out_grads, grads = tie(out_grads, grads)
    out_grads = to_members(out_grads)

    rows_scratch = [pltpu.VMEM((groups * half, padded), BF)]
    there = call(
        input_there_kernel,
        struct((members, groups, half, width), BF),
        "svv",
        scratch=rows_scratch,
        flops=stream * width * padded,
        moved=stream * width * 2,
    )(ids, grads, w_qkv_t)
    there = swap(there)
    qkv_parts = call(
        functools.partial(qkv_weights_kernel, heads, size, count),
        struct((width, WIDE), BF),
        "vvv",
        scratch=[pltpu.VMEM((width, padded), F32)],
        flops=2 * stream * width * padded,
        moved=stream * width * 4,
    )(normed, grads, scale_sum)
    there, qkv_parts, out_grads, out_own, feed_grads = tie(
        there, qkv_parts, out_grads, out_own, feed_grads
    )
    here = call(
        input_here_kernel,
        (struct((groups, half, width), BF),) * members,
        "svvv",
        scratch=rows_scratch,
        flops=stream * width * padded,
        moved=stream * width * 2,
    )(ids, grads, w_qkv_t, there)
    here, qkv_parts = tie(here, qkv_parts)
    sums = to_members(here)
    qkv_parts = exchange(qkv_parts, lines).reshape(groups, width // groups, WIDE)
    out_grads = sum_members(out_grads)
    grad_up, grad_down, gain_two = call(
        feed_rows_kernel,
        (struct((shard, local), F32), struct((local, shard), F32), struct((shard, LANES), F32)),
        "vv",
        moved=shard * local * 24,
    )(feed_grads, w_up)
    out_own = jnp.stack(out_own)
    layer_out = assemble(ids, out_own, swap(out_own), BF)
    sums, qkv_parts, out_grads, layer_out, gain_two = tie(
        sums, qkv_parts, out_grads, layer_out, gain_two
    )
    grad_x = call(
        functools.partial(tokens_kernel, groups),
        (struct((half, width), BF),) * groups,
        "svvv" + "v" * len(sums),
        moved=groups * half * width * 12,
    )(ids, pieces[0], dh_half, gains, *sums)
    grad_x, qkv_parts, out_grads = tie(grad_x, qkv_parts, out_grads)
    gx_own = to_groups(grad_x)
    qkv_parts = call(
        qkv_sum_kernel,
        (struct((shard, WIDE), BF),) * members,
        "sv",
        scratch=[pltpu.VMEM((width // groups, WIDE), F32)],
        moved=width * WIDE * 4,
    )(ids, qkv_parts)
    gx_own[1], qkv_parts, out_grads = tie(gx_own[1], qkv_parts, out_grads)
    qkv_parts = to_members(qkv_parts)
    out_grads = exchange(out_grads, lines)
    gx_own, qkv_parts = tie(gx_own, qkv_parts)
    gx_other = [swap(piece) for piece in gx_own]
    grad_out = call(
        out_rows_kernel, struct((local, shard), F32), "v", moved=shard * local * 12
    )(out_grads)
    grad_q, grad_k, grad_v, small = call(
        functools.partial(qkv_rows_kernel, mine),
        (struct((shard, local), F32),) * 3 + (struct((shard, LANES), F32),),
        "s" + "v" * (members + 3),
        scratch=[pltpu.VMEM((members, shard, WIDE), F32)],
        moved=shard * local * 24,
    )(ids, *qkv_parts, w_query, w_key, w_value)
    lane = lax.broadcasted_iota(jnp.int32, small.shape, 1)
    small = jnp.where(lane == 2, gain_two, small)
    small = small + swap(small)
    gx_other, small = tie(gx_other, small)
    grad_tokens = call(
        functools.partial(place_kernel, groups),
        struct((groups, tok_rows, width), F32),
        "s" + "v" * (2 * groups),
        moved=rows * width * 8,
    )(ids, *gx_own, *gx_other)
    return (
        layer_out,
        grad_tokens,
        grad_q,
        grad_k,
        grad_v,
        grad_out,
        grad_up,
        grad_down,
        small[:, 0] / gain_attn.astype(F32),
        small[:, 2] / gain_mlp.astype(F32),
        small[:size, 1],
    )


def fits(shapes, mesh):
    groups, stream, width = shapes[0].shape
    count, cores = mesh.shape["ctx"], mesh.shape["tp"]
    size = shapes[11].shape[0]
    if cores != 2 or count % groups:
        return False
    members = count // groups
    local_heads = shapes[3].shape[1] // cores // size
    return (
        groups & (groups - 1) == 0
        and members & (members - 1) == 0
        and members % 2 == 0
        and local_heads % members == 0
        and stream // count == LANES
        and stream % 512 == 0
        and size % 16 == 0
        and size <= LANES
        and size <= width // count
        and width // count % 16 == 0
        and 3 * local_heads // members * size + 2 <= WIDE
        and 3 * local_heads // members * size >= WIDE - LANES
        and width % (LANES * 2) == 0
    )


def segment_of(starts, positions):
    return jnp.sum((starts[None, :] <= positions[:, None]).astype(jnp.int32), axis=1)


def contract_rows(left, right):
    return lax.dot_general(
        left, right, (((0,), (0,)), ((), ())), preferred_element_type=jnp.float32
    )


def contract_cols(left, right):
    return lax.dot_general(
        left, right, (((1,), (1,)), ((), ())), preferred_element_type=jnp.float32
    )


def per_device(
    tokens,
    cotangent,
    doc_lengths,
    w_query,
    w_key,
    w_value,
    w_out,
    w_up,
    w_down,
    gain_attn,
    gain_mlp,
    query_scale,
):
    micro_count, tok_rows, model_width = tokens.shape
    head_size = query_scale.shape[0]
    local_cols = w_query.shape[1]
    head_count = local_cols // head_size
    stream = tok_rows * lax.axis_size("ctx")
    key_block = min(512, stream)
    block_count = stream // key_block
    positions = lax.axis_index("ctx") * tok_rows + jnp.arange(tok_rows, dtype=jnp.int32)
    local_sums = None
    scale_sum = jnp.zeros((head_size,), jnp.float32)
    outputs = []
    input_grads = []
    for micro_step in range(micro_count):
        gathered = (
            lax.all_gather(w_query, "ctx", axis=0, tiled=True),
            lax.all_gather(w_key, "ctx", axis=0, tiled=True),
            lax.all_gather(w_value, "ctx", axis=0, tiled=True),
            lax.all_gather(w_up, "ctx", axis=0, tiled=True),
            lax.all_gather(gain_attn, "ctx", axis=0, tiled=True),
            lax.all_gather(gain_mlp, "ctx", axis=0, tiled=True),
            lax.all_gather(w_out, "ctx", axis=1, tiled=True),
            lax.all_gather(w_down, "ctx", axis=1, tiled=True),
        )
        w_qkv = jnp.concatenate([gathered[0], gathered[1], gathered[2]], axis=1)
        up_full = gathered[3]
        gain_one = gathered[4].astype(jnp.float32)
        gain_two = gathered[5].astype(jnp.float32)
        out_full = gathered[6]
        down_full = gathered[7]
        lengths = doc_lengths[micro_step]
        starts = jnp.cumsum(lengths) - lengths
        query_seg = segment_of(starts, positions)
        stream_in = tokens[micro_step].astype(jnp.float32)
        scale_one = inverse_rms(stream_in)
        normed_one = (stream_in * scale_one * gain_one).astype(jnp.bfloat16)
        projected = jnp.dot(normed_one, w_qkv, preferred_element_type=jnp.float32)
        query_raw = projected[:, :local_cols].reshape(tok_rows, head_count, head_size)
        query_heads = (query_raw * query_scale).astype(jnp.bfloat16)
        key_local = projected[:, local_cols : 2 * local_cols].astype(jnp.bfloat16)
        value_local = projected[:, 2 * local_cols :].astype(jnp.bfloat16)
        row_top = jnp.full((head_count, tok_rows), MASKED, jnp.float32)
        key_piece = lax.all_gather(key_local, "ctx", axis=0, tiled=True)
        value_piece = lax.all_gather(value_local, "ctx", axis=0, tiled=True)
        length = key_piece.shape[0]
        key_pos = jnp.arange(length, dtype=jnp.int32)
        allowed = (key_pos[None, :] <= positions[:, None]) & (
            segment_of(starts, key_pos)[None, :] == query_seg[:, None]
        )
        scores = jnp.einsum(
            "qhd,khd->hqk",
            query_heads,
            key_piece.reshape(length, head_count, head_size),
            preferred_element_type=jnp.float32,
        )
        scores = jnp.where(allowed[None], scores, MASKED)
        new_top = jnp.maximum(row_top, jnp.max(scores, axis=-1))
        probs = jnp.where(allowed[None], jnp.exp(scores - new_top[:, :, None]), 0.0)
        row_sum = jnp.sum(probs, axis=-1)
        update = jnp.einsum(
            "hqk,khd->qhd",
            probs.astype(jnp.bfloat16),
            value_piece.reshape(length, head_count, head_size),
            preferred_element_type=jnp.float32,
        )
        weighted = update
        row_top, row_sum, weighted = (new_top, row_sum, weighted)
        attn_heads = weighted / jnp.transpose(row_sum)[:, :, None]
        log_total = row_top + jnp.log(row_sum)
        attn_low = attn_heads.reshape(tok_rows, local_cols).astype(jnp.bfloat16)
        attn_out = lax.psum(
            jnp.dot(attn_low, out_full, preferred_element_type=jnp.float32).astype(jnp.bfloat16),
            "tp",
        ).astype(jnp.float32)
        hidden = stream_in + attn_out
        scale_two = inverse_rms(hidden)
        normed_two = (hidden * scale_two * gain_two).astype(jnp.bfloat16)
        up_raw = jnp.dot(normed_two, up_full, preferred_element_type=jnp.float32)
        activated = jax.nn.silu(up_raw).astype(jnp.bfloat16)
        mlp_out = lax.psum(
            jnp.dot(activated, down_full, preferred_element_type=jnp.float32).astype(jnp.bfloat16),
            "tp",
        ).astype(jnp.float32)
        outputs.append((hidden + mlp_out).astype(jnp.bfloat16))
        grad_out = cotangent[micro_step]
        grad_down = contract_rows(activated, grad_out)
        grad_act = contract_cols(grad_out, down_full)
        sigma = jax.nn.sigmoid(up_raw)
        grad_up_raw = (grad_act * sigma * (1.0 + up_raw * (1.0 - sigma))).astype(jnp.bfloat16)
        grad_up = contract_rows(normed_two, grad_up_raw)
        grad_normed_two = lax.psum(
            contract_cols(grad_up_raw, up_full).astype(jnp.bfloat16), "tp"
        ).astype(jnp.float32)
        grad_gain_two = jnp.sum(grad_normed_two * hidden * scale_two, axis=0)
        weighted_two = grad_normed_two * gain_two
        grad_hidden = (
            grad_out.astype(jnp.float32)
            + scale_two * weighted_two
            - hidden * scale_two**3 * jnp.mean(weighted_two * hidden, axis=-1, keepdims=True)
        )
        hidden_low = grad_hidden.astype(jnp.bfloat16)
        grad_out_proj = contract_rows(attn_low, hidden_low)
        grad_attn = (
            contract_cols(hidden_low, out_full)
            .astype(jnp.bfloat16)
            .reshape(tok_rows, head_count, head_size)
        )
        delta = jnp.einsum("qhd,qhd->hq", grad_attn.astype(jnp.float32), attn_heads)
        key_all, value_all = (
            lax.all_gather(key_local, "ctx", axis=0, tiled=True),
            lax.all_gather(value_local, "ctx", axis=0, tiled=True),
        )

        def block_terms(key_piece, value_piece, offset):
            key_heads = key_piece.reshape(key_block, head_count, head_size)
            value_heads = value_piece.reshape(key_block, head_count, head_size)
            key_pos = offset + jnp.arange(key_block, dtype=jnp.int32)
            allowed = (key_pos[None, :] <= positions[:, None]) & (
                segment_of(starts, key_pos)[None, :] == query_seg[:, None]
            )
            scores = jnp.einsum(
                "qhd,khd->hqk", query_heads, key_heads, preferred_element_type=jnp.float32
            )
            probs = jnp.where(allowed[None], jnp.exp(scores - log_total[:, :, None]), 0.0)
            grad_probs = jnp.einsum(
                "qhd,khd->hqk", grad_attn, value_heads, preferred_element_type=jnp.float32
            )
            grad_scores = (probs * (grad_probs - delta[:, :, None])).astype(jnp.bfloat16)
            return (key_heads, probs, grad_scores)

        key_blocks = (
            key_all.reshape(block_count, key_block, local_cols),
            value_all.reshape(block_count, key_block, local_cols),
            jnp.arange(block_count, dtype=jnp.int32) * key_block,
        )
        zero_query = jnp.zeros((tok_rows, head_count, head_size), jnp.float32)

        def grad_block(grad_query, packed):
            key_heads, probs, grad_scores = block_terms(packed[0], packed[1], packed[2])
            grad_value = jnp.einsum(
                "hqk,qhd->khd",
                probs.astype(jnp.bfloat16),
                grad_attn,
                preferred_element_type=jnp.float32,
            )
            grad_query = grad_query + jnp.einsum(
                "hqk,khd->qhd", grad_scores, key_heads, preferred_element_type=jnp.float32
            )
            grad_key = jnp.einsum(
                "hqk,qhd->khd", grad_scores, query_heads, preferred_element_type=jnp.float32
            )
            return (
                grad_query,
                (
                    grad_key.reshape(key_block, local_cols),
                    grad_value.reshape(key_block, local_cols),
                ),
            )

        grad_query, (key_terms, value_terms) = lax.scan(grad_block, zero_query, key_blocks)
        key_grad, value_grad = (
            lax.psum_scatter(
                key_terms.reshape(stream, local_cols).astype(jnp.bfloat16),
                "ctx",
                scatter_dimension=0,
                tiled=True,
            ).astype(jnp.float32),
            lax.psum_scatter(
                value_terms.reshape(stream, local_cols).astype(jnp.bfloat16),
                "ctx",
                scatter_dimension=0,
                tiled=True,
            ).astype(jnp.float32),
        )
        grad_query_raw = (
            (grad_query * query_scale).astype(jnp.bfloat16).reshape(tok_rows, local_cols)
        )
        scale_part = jnp.sum(grad_query * query_raw, axis=(0, 1))
        grad_cols = jnp.concatenate(
            [grad_query_raw, key_grad.astype(jnp.bfloat16), value_grad.astype(jnp.bfloat16)], axis=1
        )
        grad_qkv = contract_rows(normed_one, grad_cols)
        grad_normed_one, scale_total = (
            lax.psum(contract_cols(grad_cols, w_qkv).astype(jnp.bfloat16), "tp").astype(
                jnp.float32
            ),
            lax.psum(scale_part.astype(jnp.bfloat16), "tp").astype(jnp.float32),
        )
        scale_sum = scale_sum + scale_total
        grad_gain_one = jnp.sum(grad_normed_one * stream_in * scale_one, axis=0)
        weighted_one = grad_normed_one * gain_one
        input_grads.append(
            grad_hidden
            + scale_one * weighted_one
            - stream_in * scale_one**3 * jnp.mean(weighted_one * stream_in, axis=-1, keepdims=True)
        )
        grads = (
            grad_qkv[:, :local_cols],
            grad_qkv[:, local_cols : 2 * local_cols],
            grad_qkv[:, 2 * local_cols :],
            grad_up,
            grad_gain_one,
            grad_gain_two,
            grad_out_proj,
            grad_down,
        )
        shares = (
            lax.psum_scatter(
                grads[0].astype(jnp.bfloat16), "ctx", scatter_dimension=0, tiled=True
            ).astype(jnp.float32),
            lax.psum_scatter(
                grads[1].astype(jnp.bfloat16), "ctx", scatter_dimension=0, tiled=True
            ).astype(jnp.float32),
            lax.psum_scatter(
                grads[2].astype(jnp.bfloat16), "ctx", scatter_dimension=0, tiled=True
            ).astype(jnp.float32),
            lax.psum_scatter(
                grads[3].astype(jnp.bfloat16), "ctx", scatter_dimension=0, tiled=True
            ).astype(jnp.float32),
            lax.psum_scatter(
                grads[4].astype(jnp.bfloat16), "ctx", scatter_dimension=0, tiled=True
            ).astype(jnp.float32),
            lax.psum_scatter(
                grads[5].astype(jnp.bfloat16), "ctx", scatter_dimension=0, tiled=True
            ).astype(jnp.float32),
            lax.psum_scatter(
                grads[6].astype(jnp.bfloat16), "ctx", scatter_dimension=1, tiled=True
            ).astype(jnp.float32),
            lax.psum_scatter(
                grads[7].astype(jnp.bfloat16), "ctx", scatter_dimension=1, tiled=True
            ).astype(jnp.float32),
        )
        local_sums = (
            shares
            if local_sums is None
            else tuple((total + extra for total, extra in zip(local_sums, shares)))
        )
    scale_grad = lax.psum(scale_sum, "ctx")
    return (
        jnp.stack(outputs),
        jnp.stack(input_grads),
        local_sums[0],
        local_sums[1],
        local_sums[2],
        local_sums[6],
        local_sums[3],
        local_sums[7],
        local_sums[4],
        local_sums[5],
        scale_grad,
    )


def solution(mesh):
    in_specs = (
        P(None, "ctx", None),
        P(None, "ctx", None),
        P(),
        P("ctx", "tp"),
        P("ctx", "tp"),
        P("ctx", "tp"),
        P("tp", "ctx"),
        P("ctx", "tp"),
        P("tp", "ctx"),
        P("ctx"),
        P("ctx"),
        P(),
    )
    out_specs = (
        P(None, "ctx", None),
        P(None, "ctx", None),
        P("ctx", "tp"),
        P("ctx", "tp"),
        P("ctx", "tp"),
        P("tp", "ctx"),
        P("ctx", "tp"),
        P("tp", "ctx"),
        P("ctx"),
        P("ctx"),
        P(),
    )

    def run(*arrays):
        body = stream_per_group if fits(arrays, mesh) else per_device
        return jax.shard_map(
            body, mesh=mesh, in_specs=in_specs, out_specs=out_specs, check_vma=False
        )(*arrays)

    return run
```

```python
import functools
import math

import jax
import jax.numpy as jnp
from jax import lax
from jax.experimental import pallas as pl
from jax.experimental.pallas import tpu as pltpu
from jax.sharding import PartitionSpec as P

EPSILON = 1e-06
MASKED = -1e30
LANES = 128
WIDE = 512
BF = jnp.bfloat16
F32 = jnp.float32
SPARE_VMEM = 12 * 1024 * 1024


def call(kernel, out_shape, kinds, scratch=(), flops=0, moved=0, aliases=None):
    vmem = pl.BlockSpec(memory_space=pltpu.VMEM)
    smem = pl.BlockSpec(memory_space=pltpu.SMEM)
    hbm = pl.BlockSpec(memory_space=pl.ANY)
    room = sum(
        math.prod(ref.shape) * jnp.dtype(ref.dtype).itemsize
        for ref in scratch
        if ref.memory_space == pltpu.VMEM
    )
    return pl.pallas_call(
        kernel,
        out_shape=out_shape,
        in_specs=[{"s": smem, "v": vmem, "h": hbm}[kind] for kind in kinds],
        out_specs=jax.tree.map(lambda _: vmem, out_shape),
        scratch_shapes=list(scratch),
        input_output_aliases=aliases or {},
        compiler_params=pltpu.CompilerParams(vmem_limit_bytes=room + SPARE_VMEM),
        cost_estimate=pl.CostEstimate(
            flops=int(flops), transcendentals=0, bytes_accessed=int(moved)
        ),
    )


def struct(shape, dtype):
    return jax.ShapeDtypeStruct(tuple(shape), dtype)


def nn(a, b):
    return jnp.dot(a, b, preferred_element_type=F32)


def nt(a, b):
    return lax.dot_general(a, b, (((1,), (1,)), ((), ())), preferred_element_type=F32)


def tn(a, b):
    return lax.dot_general(a, b, (((0,), (0,)), ((), ())), preferred_element_type=F32)


def at(start, size, step=None):
    return pl.ds(pl.multiple_of(start, step or size), size)


def inverse_rms(values):
    return lax.rsqrt(jnp.mean(values * values, axis=-1, keepdims=True) + EPSILON)


def split_kernel(ids, whole, *out):
    z, c = ids[0], ids[2]
    half = out[0].shape[0]
    for kz in range(len(out)):
        out[kz][...] = whole[z ^ kz, at(c * half, half), :]


def split(ids, whole):
    groups, rows, width = whole.shape
    return call(
        split_kernel,
        (struct((rows // 2, width), whole.dtype),) * groups,
        "sv",
        moved=whole.size * 4,
    )(ids, whole)


def assemble_kernel(ids, own, other, out):
    groups, half, _ = own.shape
    c = ids[2]
    for kz in range(groups):
        out[ids[0] ^ kz, at(c * half, half), :] = own[kz].astype(out.dtype)
        out[ids[0] ^ kz, at((1 - c) * half, half), :] = other[kz].astype(out.dtype)


def assemble(ids, own, other, dtype):
    groups, half, width = own.shape
    return call(
        assemble_kernel, struct((groups, 2 * half, width), dtype), "svv", moved=own.size * 12
    )(ids, own, other)


def place_kernel(groups, ids, *refs):
    own, other, out = refs[:groups], refs[groups : 2 * groups], refs[2 * groups]
    half = own[0].shape[0]
    z, c = ids[0], ids[2]
    for kz in range(groups):
        out[z ^ kz, at(c * half, half), :] = own[kz][...].astype(out.dtype)
        out[z ^ kz, at((1 - c) * half, half), :] = other[kz][...].astype(out.dtype)


def pack_kernel(mine, ids, query, key, value, gains, *refs):
    out, tmp = refs[:-1], refs[-1]
    rows = query.shape[0]
    rest = jnp.concatenate([gains[...], jnp.zeros((rows, WIDE - 3 * mine - 2), BF)], axis=1)
    for k in range(len(out)):
        cols = slice(k * mine, (k + 1) * mine)
        tmp[k] = jnp.concatenate([query[:, cols], key[:, cols], value[:, cols], rest], axis=1)
    for kj in range(len(out)):
        out[kj][...] = tmp[ids[1] ^ kj]


def stack_kernel(up, out_t, down_t, out):
    cols = up.shape[1]
    for g in range(out.shape[0]):
        for n, part in enumerate((up, out_t, down_t)):
            out[g, :, n * cols : (n + 1) * cols] = part[...]


def spread_kernel(heads, size, ids, pieces, w, w_t, gains, rows_ref):
    groups, members, rows, _ = pieces.shape
    for kz in range(groups):
        for kj in range(members):
            where = at((kz * members + (ids[1] ^ kj)) * rows, rows, 16)
            rows_ref[where, :] = pieces[kz, kj]
    block = rows_ref[...]
    zeros = jnp.zeros((block.shape[0], LANES - size), BF)
    for h in range(3 * heads):
        w[:, h * LANES : (h + 1) * LANES] = jnp.concatenate(
            [block[:, h * size : (h + 1) * size], zeros], axis=1
        )
    w_t[...] = w[...].T
    first = 3 * heads * size - (WIDE - LANES)
    gains[...] = block[:, WIDE - LANES :].astype(F32).T[first : first + 8, :]


def order_kernel(ids, *refs):
    pieces, out = refs[:-3], refs[-3:]
    groups, rows, _ = pieces[0].shape
    members, cols = len(pieces), out[0].shape[1]
    for kj in range(members):
        for kz in range(groups):
            where = at((kz * members + (ids[1] ^ kj)) * rows, rows, 16)
            for n in range(3):
                out[n][where, :] = pieces[kj][kz, :, n * cols : (n + 1) * cols]


def project_kernel(members, step, ids, *refs):
    pieces = refs[: 2 * members]
    w, gain, scale, proj, normed = refs[2 * members :]
    groups, half, _ = pieces[0].shape
    z, j, c = ids[0], ids[1], ids[2]
    for kj in range(members):
        for kc in range(2):
            for kz in range(groups):
                base = (z ^ kz) * (members * 2) + (j ^ kj) * 2 + (c ^ kc)
                normed[at(base * half, half), :] = pieces[kc * members + kj][kz]

    def block(n, _):
        rows = at(n * step, step)
        x = normed[rows, :].astype(F32)
        xn = (x * inverse_rms(x) * gain[0:1, :]).astype(BF)
        normed[rows, :] = xn
        proj[rows, :] = (nn(xn, w[...]) * scale[...]).astype(BF)
        return 0

    lax.fori_loop(0, normed.shape[0] // step, block, 0)


def doc_bounds(lengths, z, place):
    start, begin, end = jnp.int32(0), jnp.int32(0), jnp.int32(0)
    for d in range(lengths.shape[1]):
        stop = start + lengths[z, d]
        inside = start <= place
        begin = jnp.where(inside, start, begin)
        end = jnp.where(inside, stop, end)
        start = stop
    return begin, end


def doc_starts(lengths, z, stream):
    place = lax.broadcasted_iota(jnp.int32, (8, stream), 1)
    start, row = jnp.int32(0), jnp.zeros((8, stream), jnp.int32)
    for d in range(lengths.shape[1]):
        row = jnp.where(place >= start, start, row)
        start = start + lengths[z, d]
    return row


def attend_kernel(heads, size, members, bq, bk, ids, lengths, proj, *refs):
    outs, (kept, sent, vt, doc) = refs[:members], refs[members:]
    stream = proj.shape[0]
    z, j = ids[0], ids[1]
    doc[...] = doc_starts(lengths, z, stream)
    for h in range(heads):
        vt[h] = proj[:, (2 * heads + h) * LANES : (2 * heads + h + 1) * LANES].T

    def one_query_block(qb, _):
        rows = at(qb * bq, bq)
        qpos = qb * bq + lax.broadcasted_iota(jnp.int32, (1, bq), 1)
        queries = [proj[rows, h * LANES : (h + 1) * LANES] for h in range(heads)]

        def one_key_block(kb, carry):
            keys = at(kb * bk, bk)
            kpos = kb * bk + lax.broadcasted_iota(jnp.int32, (bk, bq), 0)
            allowed = (kpos <= qpos) & (kpos >= doc[0:1, rows])
            new = []
            for h in range(heads):
                top, total, acc = carry[h]
                k = proj[keys, (heads + h) * LANES : (heads + h + 1) * LANES]
                s = jnp.where(allowed, nt(k, queries[h]), MASKED)
                top2 = jnp.maximum(top, jnp.max(s, axis=0, keepdims=True))
                p = jnp.exp(s - top2)
                alpha = jnp.exp(top - top2)
                total = total * alpha + jnp.sum(p, axis=0, keepdims=True)
                acc = acc * alpha + nn(vt[h, :, keys], p.astype(BF))
                new.append((top2, total, acc))
            return tuple(new)

        zero = (
            jnp.full((1, bq), MASKED, F32),
            jnp.zeros((1, bq), F32),
            jnp.zeros((LANES, bq), F32),
        )
        begin, _ = doc_bounds(lengths, z, qb * bq)
        end = (qb * bq + bq + bk - 1) // bk
        carry = lax.fori_loop(begin // bk, end, one_key_block, (zero,) * heads)
        for h in range(heads):
            top, total, acc = carry[h]
            o = acc / total
            kept[h, :LANES, rows] = o
            kept[h, LANES:, rows] = jnp.broadcast_to(top + jnp.log(total), (8, bq))
            low = o[:size].astype(BF)
            for part in range(bq // LANES):
                block = qb * (bq // LANES) + part
                lanes = at(block // members * LANES, LANES)
                sent[(block % members) ^ j, h * size : (h + 1) * size, lanes] = low[
                    :, part * LANES : (part + 1) * LANES
                ]
        return 0

    lax.fori_loop(0, stream // bq, one_query_block, 0)
    for kj in range(members):
        outs[kj][...] = sent[kj]


def store_weights(heads, size, count, scale_sum, full, out):
    rows = out.shape[0] // count
    pad = WIDE - 3 * heads * size
    s = scale_sum[:size, :pad]
    high = s.astype(BF)
    rest = (s - high.astype(F32)).astype(BF)
    lane = lax.broadcasted_iota(jnp.int32, (size, pad), 1)
    tail = jnp.where(lane == 0, high, jnp.where(lane == 1, rest, jnp.zeros_like(rest)))
    tail = [tail, jnp.zeros((rows - size, pad), BF)] if rows > size else [tail]
    tail = jnp.concatenate(tail, axis=0)
    for n in range(count):
        block = full[n * rows : (n + 1) * rows, :].astype(BF)
        out[n * rows : (n + 1) * rows, :] = jnp.concatenate(
            [block[:, h * LANES : h * LANES + size] for h in range(3 * heads)] + [tail], axis=1
        )


def attend_back_kernel(heads, size, members, bq, bk, ids, lengths, proj, kept, scale, w, normed, *refs):
    pieces = refs[:members]
    grads, there, weights, dot_, do_, kt, dqt, delta, doc, rows_ref, full = refs[members:]
    stream = proj.shape[0]
    groups = pieces[0].shape[1] // LANES
    z, j = ids[0], ids[1]
    doc[...] = doc_starts(lengths, z, stream)
    for h in range(heads):
        kt[h] = proj[:, (heads + h) * LANES : (heads + h + 1) * LANES].T
        dot_[h, size:, :] = jnp.zeros((LANES - size, stream), BF)
        for kj in range(members):
            for g in range(groups):
                lanes = at((g * members + (j ^ kj)) * LANES, LANES)
                dot_[h, :size, lanes] = pieces[kj][
                    h * size : (h + 1) * size, g * LANES : (g + 1) * LANES
                ]
        do_[h] = dot_[h].T
        delta[h] = jnp.broadcast_to(
            jnp.sum(dot_[h].astype(F32) * kept[h, :LANES, :], axis=0, keepdims=True), (8, stream)
        )
        dqt[h] = jnp.zeros((LANES, stream), F32)

    def one_key_block(kb, _):
        keys = at(kb * bk, bk)
        kpos = kb * bk + lax.broadcasted_iota(jnp.int32, (bk, bq), 0)
        ks = [proj[keys, (heads + h) * LANES : (heads + h + 1) * LANES] for h in range(heads)]
        vs = [
            proj[keys, (2 * heads + h) * LANES : (2 * heads + h + 1) * LANES] for h in range(heads)
        ]

        def one_query_block(qb, carry):
            rows = at(qb * bq, bq)
            qpos = qb * bq + lax.broadcasted_iota(jnp.int32, (1, bq), 1)
            allowed = (kpos <= qpos) & (kpos >= doc[0:1, rows])
            new = []
            for h in range(heads):
                dk, dv = carry[h]
                q = proj[rows, h * LANES : (h + 1) * LANES]
                p = jnp.exp(nt(ks[h], q) - kept[h, LANES : LANES + 1, rows])
                p = jnp.where(allowed, p, 0.0)
                dp = nn(vs[h], dot_[h, :, rows])
                ds = (p * (dp - delta[h, 0:1, rows])).astype(BF)
                dv = dv + nn(p.astype(BF), do_[h, rows, :])
                dk = dk + nn(ds, q)
                dqt[h, :, rows] += nn(kt[h, :, keys], ds)
                new.append((dk, dv))
            return tuple(new)

        _, final = doc_bounds(lengths, z, kb * bk + bk - 1)
        zero = jnp.zeros((bk, LANES), F32)
        carry = lax.fori_loop(
            kb * bk // bq, (final + bq - 1) // bq, one_query_block, ((zero, zero),) * heads
        )
        for h in range(heads):
            for n in range(2):
                cols = ((n + 1) * heads + h) * LANES
                grads[keys, cols : cols + LANES] = carry[h][n].astype(BF)
        return 0

    lax.fori_loop(0, stream // bk, one_key_block, 0)
    total = jnp.zeros((1, LANES), F32)
    for h in range(heads):
        dq = dqt[h].T
        q = proj[:, h * LANES : (h + 1) * LANES].astype(F32)
        total = total + jnp.sum(dq * q, axis=0, keepdims=True)
        grads[:, h * LANES : (h + 1) * LANES] = (dq * scale[...]).astype(BF)
    _, _, half, width = there.shape

    def one_member(kj, _):
        y = nn(input_rows(ids, grads, rows_ref, kj, 1, members, half), w[...])
        there[kj] = y.reshape(groups, half, width).astype(BF)
        return 0

    lax.fori_loop(0, members, one_member, 0)
    total = jnp.broadcast_to(total / scale[...], (LANES, LANES)).T
    full[...] = tn(normed[...], grads[...])
    store_weights(heads, size, groups * members, total, full, weights)


def out_kernel(ids, *refs):
    pieces, (w, ob_t, part) = refs[:-3], refs[-3:]
    mine = pieces[0].shape[0]
    for kj in range(len(pieces)):
        ob_t[at((ids[1] ^ kj) * mine, mine, 16), :] = pieces[kj][...]
    part[...] = nt(ob_t[...].T, w[...]).astype(BF)


def mlp_kernel(groups, ids, *refs):
    x_own, x_other = refs[0], refs[1]
    g_own, g_other, attn, attn_other, up, down, gains = refs[2:9]
    hidden, normed, act, grad_up, cot, part, back = refs[9:]
    half = x_own.shape[1]
    z, c = ids[0], ids[2]
    for kz in range(groups):
        for kc in range(2):
            rows = at((z ^ kz) * (2 * half) + (c ^ kc) * half, half)
            hidden[rows, :] = (x_other if kc else x_own)[kz].astype(F32) + (
                attn[rows, :].astype(F32) + attn_other[rows, :].astype(F32)
            )
            cot[rows, :] = (g_other if kc else g_own)[kz]
    step = hidden.shape[0] // 2

    def block(n, _):
        rows = at(n * step, step)
        h = hidden[rows, :]
        xn = (h * inverse_rms(h) * gains[1:2, :]).astype(BF)
        u = nn(xn, up[...])
        sigma = jax.nn.sigmoid(u)
        a = (u * sigma).astype(BF)
        da = nn(cot[rows, :], down[...])
        du = (da * sigma * (1.0 + u * (1.0 - sigma))).astype(BF)
        part[rows, :] = nt(a, down[...]).astype(BF)
        back[rows, :] = nt(du, up[...]).astype(BF)
        normed[rows, :] = xn
        act[rows, :] = a
        grad_up[rows, :] = du
        return 0

    lax.fori_loop(0, 2, block, 0)


def hidden_kernel(groups, members, ids, *refs):
    hidden, cot, part, part_other, back, back_other, w, gains = refs[:8]
    low, dh_half = refs[8:10]
    pieces, out = refs[10 : 10 + members], refs[10 + members : 10 + members + groups]
    dh, lay, do_t = refs[10 + members + groups :]
    rows_all = hidden.shape[0]
    half = rows_all // groups // 2
    mine = pieces[0].shape[0]
    z, j, c = ids[0], ids[1], ids[2]
    step = rows_all // groups

    def block(n, _):
        rows = at(n * step, step)
        h = hidden[rows, :]
        scale = inverse_rms(h)
        grad = back[rows, :].astype(F32) + back_other[rows, :].astype(F32)
        weighted = grad * gains[1:2, :]
        d = (
            cot[rows, :].astype(F32)
            + scale * weighted
            - h * scale**3 * jnp.mean(weighted * h, axis=-1, keepdims=True)
        )
        dh[rows, :] = d
        low[rows, :] = d.astype(BF)
        lay[rows, :] = (
            h + (part[rows, :].astype(F32) + part_other[rows, :].astype(F32))
        ).astype(BF)
        return 0

    lax.fori_loop(0, groups, block, 0)
    do_t[...] = nn(low[...], w[...]).T.astype(BF)
    for kj in range(members):
        pieces[kj][...] = do_t[at((j ^ kj) * mine, mine, 16), :]
    for g in range(groups):
        out[g][...] = lay[at((z ^ g) * 2 * half + c * half, half), :]
        dh_half[g] = dh[at(g * 2 * half + c * half, half), :]


def by_member(ids, full, out, first=0):
    groups, rows, _ = out[0].shape
    for kj in range(len(out)):
        for g in range(groups):
            where = at((g * len(out) + (ids[1] ^ kj)) * rows, rows, 16)
            out[kj][g, :, first : first + full.shape[1]] = full[where, :]


def feed_weights_kernel(ids, normed, grad_up, cot, act, *refs):
    out, full = refs[:-1], refs[-1]
    full[...] = tn(normed[...], grad_up[...]).astype(BF)
    by_member(ids, full, out)
    full[...] = tn(cot[...], act[...]).astype(BF)
    by_member(ids, full, out, full.shape[1])


def out_weights_kernel(ids, low, ob_t, *refs):
    out, full = refs[:-1], refs[-1]
    full[...] = tn(low[...], ob_t[...].T).astype(BF)
    by_member(ids, full, out)


def sum_members_kernel(*refs):
    total = refs[0][...].astype(F32)
    for part in refs[1:-1]:
        total = total + part[...].astype(F32)
    refs[-1][...] = total.astype(BF)


def sum_split_kernel(members, ids, *refs):
    parts, out, tmp = refs[:members], refs[members:-1], refs[-1]
    total = parts[0][...].astype(F32)
    for part in parts[1:]:
        total = total + part[...].astype(F32)
    tmp[...] = total.astype(BF)
    for kz in range(len(out)):
        out[kz][...] = tmp[ids[0] ^ kz]


def rows_kernel(groups, parts, up, *refs):
    outs, (grad_up, grad_down, grad_out, gain) = refs[:groups], refs[groups:]
    cols = up.shape[1]
    total = parts[0].astype(F32)
    for g in range(1, parts.shape[0]):
        total = total + parts[g].astype(F32)
    grad_up[...] = total[:, :cols]
    grad_down[...] = total[:, cols:].T
    term = jnp.sum(total[:, :cols] * up[...].astype(F32), axis=1, keepdims=True)
    gain[...] = jnp.broadcast_to(term, gain.shape)
    total = outs[0][...].astype(F32)
    for part in outs[1:]:
        total = total + part[...].astype(F32)
    grad_out[...] = total.T


def input_rows(ids, grads, rows_ref, kj, which, members, half):
    for g in range(rows_ref.shape[0] // half):
        base = (g * members + (ids[1] ^ kj)) * 2 + (ids[2] ^ which)
        rows_ref[g * half : (g + 1) * half, :] = grads[at(base * half, half), :]
    return rows_ref[...]


def input_here_kernel(ids, grads, w, other, *refs):
    out, rows_ref = refs[:-1], refs[-1]
    members, (groups, half, width) = len(out), out[0].shape
    for kj in reversed(range(members)):
        y = nn(input_rows(ids, grads, rows_ref, kj, 0, members, half), w[...])
        y = y + other[kj].reshape(groups * half, width).astype(F32)
        out[kj][...] = y.reshape(groups, half, width).astype(BF)


def qkv_sum_kernel(ids, parts, *refs):
    out, tmp = refs[:-1], refs[-1]
    total = parts[0].astype(F32)
    for g in range(1, parts.shape[0]):
        total = total + parts[g].astype(F32)
    tmp[...] = total
    rows = out[0].shape[0]
    for kj in range(len(out)):
        out[kj][...] = tmp[at((ids[1] ^ kj) * rows, rows, 16), :].astype(BF)


def qkv_rows_kernel(mine, ids, *refs):
    members = len(refs) - 8
    pieces, (query, key, value, dq, dk, dv, small, tmp) = refs[:members], refs[members:]
    for kj in range(members):
        tmp[ids[1] ^ kj] = pieces[kj][...].astype(F32)
    gain = None
    for n, (w, dw) in enumerate(((query, dq), (key, dk), (value, dv))):
        dw[...] = jnp.concatenate(
            [tmp[k][:, n * mine : (n + 1) * mine] for k in range(members)], axis=1
        )
        term = jnp.sum(dw[...] * w[...].astype(F32), axis=1, keepdims=True)
        gain = term if gain is None else gain + term
    scale = tmp[0][:, 3 * mine : 3 * mine + 2]
    for k in range(1, members):
        scale = scale + tmp[k][:, 3 * mine : 3 * mine + 2]
    scale = jnp.sum(scale, axis=1, keepdims=True)
    lane = lax.broadcasted_iota(jnp.int32, small.shape, 1)
    small[...] = jnp.where(lane == 0, gain, jnp.where(lane == 1, scale, 0.0))


def tokens_kernel(groups, ids, *refs):
    x, dh, gains = refs[:3]
    parts, out = refs[3:-groups], refs[-groups:]
    z = ids[0]
    for kz in range(groups):
        grad = parts[0][z ^ kz].astype(F32)
        for part in parts[1:]:
            grad = grad + part[z ^ kz].astype(F32)
        xx = x[kz].astype(F32)
        scale = inverse_rms(xx)
        weighted = grad * gains[0:1, :]
        out[kz][...] = (
            dh[z ^ kz]
            + scale * weighted
            - xx * scale**3 * jnp.mean(weighted * xx, axis=-1, keepdims=True)
        ).astype(BF)


def stream_per_group(
    tokens,
    cotangent,
    doc_lengths,
    w_query,
    w_key,
    w_value,
    w_out,
    w_up,
    w_down,
    gain_attn,
    gain_mlp,
    query_scale,
):
    groups, tok_rows, width = tokens.shape
    count = lax.axis_size("ctx")
    members = count // groups
    size = query_scale.shape[0]
    local = w_query.shape[1]
    shard = width // count
    heads = local // size // members
    half = tok_rows // 2
    stream = tok_rows * count
    mine = heads * size
    rows = groups * tok_rows
    padded = 3 * heads * LANES
    me = lax.axis_index("ctx")
    ids = jnp.stack([me // members, me % members, lax.axis_index("tp")]).astype(jnp.int32)

    planes = [[g * members + k for k in range(members)] for g in range(groups)]
    lines = [[g * members + k for g in range(groups)] for k in range(members)]

    def across(a, mask):
        return lax.ppermute(a, "ctx", [(i, i ^ mask) for i in range(count)])

    def shift(a, by):
        pairs = [(i, i + by * members) for i in range(count)]
        return lax.ppermute(a, "ctx", [(i, k) for i, k in pairs if 0 <= k < count])

    def swap(a):
        return lax.ppermute(a, "tp", [(0, 1), (1, 0)])

    def to_groups(parts):
        return [parts[0]] + [across(parts[k], k * members) for k in range(1, groups)]

    def to_members(parts):
        return [parts[0]] + [across(parts[k], k) for k in range(1, members)]

    def exchange(a, teams):
        return lax.all_to_all(a, "ctx", 0, 0, axis_index_groups=teams, tiled=True)

    def tie(*values):
        return lax.optimization_barrier(values)

    def quarter(own, beside, above):
        cut = groups // 2
        return jnp.concatenate([across(above[:cut], 1), across(beside[cut:], 2)])

    packed = call(
        functools.partial(pack_kernel, mine),
        (struct((shard, WIDE), BF),) * members,
        "svvvv",
        scratch=[pltpu.VMEM((members, shard, WIDE), BF)],
        moved=shard * WIDE * members * 4,
    )(ids, w_query, w_key, w_value, jnp.stack([gain_attn, gain_mlp], axis=1))
    own = jnp.stack(to_groups(split(ids, tokens)))

    shards = call(
        stack_kernel,
        struct((groups, shard, 3 * local), BF),
        "vvv",
        moved=groups * shard * local * 8,
    )(w_up, w_out.T, w_down.T)
    own, packed, shards = tie(own, packed, shards)
    shards = exchange(shards, lines)
    cols = to_members(packed)
    late, cols = tie(own, cols)
    pieces = to_members([own] * (members - 1) + [late])
    pieces, cols, shards = tie(pieces, jnp.stack(cols), shards)
    cols = jnp.concatenate([cols] * groups)

    cols = exchange(cols, lines).reshape(groups, members, shard, WIDE)
    others = [swap(piece) for piece in pieces]
    if members == 4:
        beside, above = across(shards, 1), across(shards, 2)
        cols, others, beside, above = tie(cols, others, beside, above)
        shards = [shards, beside, above, quarter(shards, beside, above)]
    else:
        cols, others, shards = tie(cols, others, to_members([shards] * members))
    pieces = pieces + others
    g_parts, cols = tie(split(ids, cotangent), cols)
    g_own = to_groups(g_parts)
    w_qkv, w_qkv_t, gains = call(
        functools.partial(spread_kernel, heads, size),
        (struct((width, padded), BF), struct((padded, width), BF), struct((8, width), F32)),
        "sv",
        scratch=[pltpu.VMEM((width, WIDE), BF)],
        moved=width * padded * 6,
    )(ids, cols)
    scale_row = jnp.pad(query_scale, (0, LANES - size), constant_values=1.0)[None, :]
    scale_all = jnp.concatenate(
        [scale_row] * heads + [jnp.ones((1, 2 * heads * LANES), F32)], axis=1
    )

    proj, normed = call(
        functools.partial(project_kernel, members, 512),
        (struct((stream, padded), BF), struct((stream, width), BF)),
        "s" + "v" * (2 * members + 3),
        flops=2 * stream * width * padded,
        moved=stream * width * 4,
    )(ids, *pieces, w_qkv, gains, scale_all)

    bq, bk = 512, 512
    *sent, kept = call(
        functools.partial(attend_kernel, heads, size, members, bq, bk),
        (struct((mine, rows), BF),) * members + (struct((heads, LANES + 8, stream), F32),),
        "ssv",
        scratch=[
            pltpu.VMEM((members, mine, rows), BF),
            pltpu.VMEM((heads, LANES, stream), BF),
            pltpu.VMEM((8, stream), jnp.int32),
        ],
        flops=2 * stream * stream * LANES * heads,
        moved=stream * LANES * heads * 10,
    )(ids, doc_lengths, proj)
    sent, shards, g_own = tie(sent, shards, g_own)
    arrived = to_members(sent)
    g_own = jnp.stack(g_own)
    g_other = swap(g_own)
    up_full, out_t, down_t = call(
        order_kernel,
        (struct((width, local), BF),) * 3,
        "s" + "v" * members,
        moved=width * local * 12,
    )(ids, *shards)

    ob_t, attn = call(
        out_kernel,
        (struct((local, rows), BF), struct((rows, width), BF)),
        "s" + "v" * (members + 1),
        flops=2 * rows * local * width,
        moved=local * width * 4,
    )(ids, *arrived, out_t)
    hidden, normed_two, activated, grad_up_raw, cot, part, back = call(
        functools.partial(mlp_kernel, groups),
        (
            struct((rows, width), F32),
            struct((rows, width), BF),
            struct((rows, local), BF),
            struct((rows, local), BF),
            struct((rows, width), BF),
            struct((rows, width), BF),
            struct((rows, width), BF),
        ),
        "s" + "v" * 9,
        flops=8 * rows * local * width,
        moved=local * width * 12,
    )(ids, pieces[0], pieces[members], g_own, g_other, attn, swap(attn), up_full, down_t, gains)
    back_other, part_other = swap(back), swap(part)
    feed_grads = call(
        feed_weights_kernel,
        (struct((groups, shard, 2 * local), BF),) * members,
        "svvvv",
        scratch=[pltpu.VMEM((width, local), BF)],
        flops=4 * rows * local * width,
        moved=local * width * 8,
    )(ids, normed_two, grad_up_raw, cot, activated)
    back_other, part_other, feed_grads = tie(back_other, part_other, feed_grads)
    hidden_low, dh_half, *results = call(
        functools.partial(hidden_kernel, groups, members),
        (struct((rows, width), BF), struct((groups, half, width), F32))
        + (struct((mine, rows), BF),) * members
        + (struct((half, width), BF),) * groups,
        "s" + "v" * 8,
        scratch=[
            pltpu.VMEM((rows, width), F32),
            pltpu.VMEM((rows, width), BF),
            pltpu.VMEM((local, rows), BF),
        ],
        flops=2 * rows * local * width,
        moved=local * width * 12,
    )(ids, hidden, cot, part, part_other, back, back_other, out_t, gains)
    do_pieces, out_parts = to_members(results[:members]), results[members:]
    out_grads = call(
        out_weights_kernel,
        (struct((groups, shard, local), BF),) * members,
        "svv",
        scratch=[pltpu.VMEM((width, local), BF)],
        flops=2 * rows * local * width,
        moved=local * width * 4,
    )(ids, hidden_low, ob_t)
    do_pieces, out_grads, out_parts, feed_grads = tie(do_pieces, out_grads, out_parts, feed_grads)

    feed_grads = to_members(feed_grads)
    out_own = to_groups(out_parts)

    grads, there, qkv_parts = call(
        functools.partial(attend_back_kernel, heads, size, members, bq, bk),
        (
            struct((stream, padded), BF),
            struct((members, groups, half, width), BF),
            struct((width, WIDE), BF),
        ),
        "ssvvvvv" + "v" * members,
        scratch=[
            pltpu.VMEM((heads, LANES, stream), BF),
            pltpu.VMEM((heads, stream, LANES), BF),
            pltpu.VMEM((heads, LANES, stream), BF),
            pltpu.VMEM((heads, LANES, stream), F32),
            pltpu.VMEM((heads, 8, stream), F32),
            pltpu.VMEM((8, stream), jnp.int32),
            pltpu.VMEM((groups * half, padded), BF),
            pltpu.VMEM((width, padded), F32),
        ],
        flops=5 * stream * stream * LANES * heads,
        moved=stream * LANES * heads * 20,
    )(ids, doc_lengths, proj, kept, scale_row, w_qkv_t, normed, *do_pieces)
    there, grads, qkv_parts, feed_grads, out_own[1], out_own[2], out_grads = tie(
        there, grads, qkv_parts, feed_grads, out_own[1], out_own[2], out_grads
    )

    there = swap(there)
    here = call(
        input_here_kernel,
        (struct((groups, half, width), BF),) * members,
        "svvv",
        scratch=[pltpu.VMEM((groups * half, padded), BF)],
        flops=stream * width * padded,
        moved=stream * width * 2,
    )(ids, grads, w_qkv_t, there)
    here, feed_grads, qkv_parts = tie(here, feed_grads, qkv_parts)
    sums = to_members(here)
    qkv_parts = exchange(qkv_parts, lines).reshape(groups, width // groups, WIDE)
    feed_grads = call(
        sum_members_kernel,
        struct((groups, shard, 2 * local), BF),
        "v" * members,
        moved=groups * shard * local * 24,
    )(*feed_grads)
    sums, feed_grads = tie(sums, feed_grads)
    grad_x = call(
        functools.partial(tokens_kernel, groups),
        (struct((half, width), BF),) * groups,
        "svvv" + "v" * len(sums),
        moved=groups * half * width * 12,
    )(ids, pieces[0], dh_half, gains, *sums)
    grad_x, qkv_parts, out_own = tie(grad_x, qkv_parts, out_own)
    gx_own = to_groups(grad_x)
    out_own = jnp.stack(out_own)
    layer_out = assemble(ids, out_own, swap(out_own), BF)
    qkv_parts = call(
        qkv_sum_kernel,
        (struct((shard, WIDE), BF),) * members,
        "sv",
        scratch=[pltpu.VMEM((width // groups, WIDE), F32)],
        moved=width * WIDE * 4,
    )(ids, qkv_parts)
    gx_own, qkv_parts, layer_out, out_grads, feed_grads = tie(
        gx_own, qkv_parts, layer_out, out_grads, feed_grads
    )
    feed_grads = exchange(feed_grads, lines)
    out_grads = to_members(out_grads)
    qkv_parts = to_members(qkv_parts)
    out_grads = call(
        functools.partial(sum_split_kernel, members),
        (struct((shard, local), BF),) * groups,
        "s" + "v" * members,
        scratch=[pltpu.VMEM((groups, shard, local), BF)],
        moved=groups * shard * local * 12,
    )(ids, *out_grads)
    out_grads = to_groups(out_grads)
    gx_other = [swap(piece) for piece in gx_own]
    grad_up, grad_down, grad_out, gain_two = call(
        functools.partial(rows_kernel, groups),
        (struct((shard, local), F32),)
        + (struct((local, shard), F32),) * 2
        + (struct((shard, LANES), F32),),
        "v" * (groups + 2),
        moved=shard * local * 36,
    )(feed_grads, w_up, *out_grads)
    grad_q, grad_k, grad_v, small = call(
        functools.partial(qkv_rows_kernel, mine),
        (struct((shard, local), F32),) * 3 + (struct((shard, LANES), F32),),
        "s" + "v" * (members + 3),
        scratch=[pltpu.VMEM((members, shard, WIDE), F32)],
        moved=shard * local * 24,
    )(ids, *qkv_parts, w_query, w_key, w_value)
    lane = lax.broadcasted_iota(jnp.int32, small.shape, 1)
    small = jnp.where(lane == 2, gain_two, small)
    small = small + swap(small)
    gx_other, small = tie(gx_other, small)
    grad_tokens = call(
        functools.partial(place_kernel, groups),
        struct((groups, tok_rows, width), F32),
        "s" + "v" * (2 * groups),
        moved=rows * width * 8,
    )(ids, *gx_own, *gx_other)
    return (
        layer_out,
        grad_tokens,
        grad_q,
        grad_k,
        grad_v,
        grad_out,
        grad_up,
        grad_down,
        small[:, 0] / gain_attn.astype(F32),
        small[:, 2] / gain_mlp.astype(F32),
        small[:size, 1],
    )


def fits(shapes, mesh):
    groups, stream, width = shapes[0].shape
    count, cores = mesh.shape["ctx"], mesh.shape["tp"]
    size = shapes[11].shape[0]
    if cores != 2 or count % groups:
        return False
    members = count // groups
    local_heads = shapes[3].shape[1] // cores // size
    return (
        groups & (groups - 1) == 0
        and members & (members - 1) == 0
        and members % 2 == 0
        and local_heads % members == 0
        and stream // count == LANES
        and stream % 512 == 0
        and size % 16 == 0
        and size <= LANES
        and size <= width // count
        and width // count % 16 == 0
        and 3 * local_heads // members * size + 2 <= WIDE
        and 3 * local_heads // members * size >= WIDE - LANES
        and width % (LANES * 2) == 0
    )


def segment_of(starts, positions):
    return jnp.sum((starts[None, :] <= positions[:, None]).astype(jnp.int32), axis=1)


def contract_rows(left, right):
    return lax.dot_general(
        left, right, (((0,), (0,)), ((), ())), preferred_element_type=jnp.float32
    )


def contract_cols(left, right):
    return lax.dot_general(
        left, right, (((1,), (1,)), ((), ())), preferred_element_type=jnp.float32
    )


def per_device(
    tokens,
    cotangent,
    doc_lengths,
    w_query,
    w_key,
    w_value,
    w_out,
    w_up,
    w_down,
    gain_attn,
    gain_mlp,
    query_scale,
):
    micro_count, tok_rows, model_width = tokens.shape
    head_size = query_scale.shape[0]
    local_cols = w_query.shape[1]
    head_count = local_cols // head_size
    stream = tok_rows * lax.axis_size("ctx")
    key_block = min(512, stream)
    block_count = stream // key_block
    positions = lax.axis_index("ctx") * tok_rows + jnp.arange(tok_rows, dtype=jnp.int32)
    local_sums = None
    scale_sum = jnp.zeros((head_size,), jnp.float32)
    outputs = []
    input_grads = []
    for micro_step in range(micro_count):
        gathered = (
            lax.all_gather(w_query, "ctx", axis=0, tiled=True),
            lax.all_gather(w_key, "ctx", axis=0, tiled=True),
            lax.all_gather(w_value, "ctx", axis=0, tiled=True),
            lax.all_gather(w_up, "ctx", axis=0, tiled=True),
            lax.all_gather(gain_attn, "ctx", axis=0, tiled=True),
            lax.all_gather(gain_mlp, "ctx", axis=0, tiled=True),
            lax.all_gather(w_out, "ctx", axis=1, tiled=True),
            lax.all_gather(w_down, "ctx", axis=1, tiled=True),
        )
        w_qkv = jnp.concatenate([gathered[0], gathered[1], gathered[2]], axis=1)
        up_full = gathered[3]
        gain_one = gathered[4].astype(jnp.float32)
        gain_two = gathered[5].astype(jnp.float32)
        out_full = gathered[6]
        down_full = gathered[7]
        lengths = doc_lengths[micro_step]
        starts = jnp.cumsum(lengths) - lengths
        query_seg = segment_of(starts, positions)
        stream_in = tokens[micro_step].astype(jnp.float32)
        scale_one = inverse_rms(stream_in)
        normed_one = (stream_in * scale_one * gain_one).astype(jnp.bfloat16)
        projected = jnp.dot(normed_one, w_qkv, preferred_element_type=jnp.float32)
        query_raw = projected[:, :local_cols].reshape(tok_rows, head_count, head_size)
        query_heads = (query_raw * query_scale).astype(jnp.bfloat16)
        key_local = projected[:, local_cols : 2 * local_cols].astype(jnp.bfloat16)
        value_local = projected[:, 2 * local_cols :].astype(jnp.bfloat16)
        row_top = jnp.full((head_count, tok_rows), MASKED, jnp.float32)
        key_piece = lax.all_gather(key_local, "ctx", axis=0, tiled=True)
        value_piece = lax.all_gather(value_local, "ctx", axis=0, tiled=True)
        length = key_piece.shape[0]
        key_pos = jnp.arange(length, dtype=jnp.int32)
        allowed = (key_pos[None, :] <= positions[:, None]) & (
            segment_of(starts, key_pos)[None, :] == query_seg[:, None]
        )
        scores = jnp.einsum(
            "qhd,khd->hqk",
            query_heads,
            key_piece.reshape(length, head_count, head_size),
            preferred_element_type=jnp.float32,
        )
        scores = jnp.where(allowed[None], scores, MASKED)
        new_top = jnp.maximum(row_top, jnp.max(scores, axis=-1))
        probs = jnp.where(allowed[None], jnp.exp(scores - new_top[:, :, None]), 0.0)
        row_sum = jnp.sum(probs, axis=-1)
        update = jnp.einsum(
            "hqk,khd->qhd",
            probs.astype(jnp.bfloat16),
            value_piece.reshape(length, head_count, head_size),
            preferred_element_type=jnp.float32,
        )
        weighted = update
        row_top, row_sum, weighted = (new_top, row_sum, weighted)
        attn_heads = weighted / jnp.transpose(row_sum)[:, :, None]
        log_total = row_top + jnp.log(row_sum)
        attn_low = attn_heads.reshape(tok_rows, local_cols).astype(jnp.bfloat16)
        attn_out = lax.psum(
            jnp.dot(attn_low, out_full, preferred_element_type=jnp.float32).astype(jnp.bfloat16),
            "tp",
        ).astype(jnp.float32)
        hidden = stream_in + attn_out
        scale_two = inverse_rms(hidden)
        normed_two = (hidden * scale_two * gain_two).astype(jnp.bfloat16)
        up_raw = jnp.dot(normed_two, up_full, preferred_element_type=jnp.float32)
        activated = jax.nn.silu(up_raw).astype(jnp.bfloat16)
        mlp_out = lax.psum(
            jnp.dot(activated, down_full, preferred_element_type=jnp.float32).astype(jnp.bfloat16),
            "tp",
        ).astype(jnp.float32)
        outputs.append((hidden + mlp_out).astype(jnp.bfloat16))
        grad_out = cotangent[micro_step]
        grad_down = contract_rows(activated, grad_out)
        grad_act = contract_cols(grad_out, down_full)
        sigma = jax.nn.sigmoid(up_raw)
        grad_up_raw = (grad_act * sigma * (1.0 + up_raw * (1.0 - sigma))).astype(jnp.bfloat16)
        grad_up = contract_rows(normed_two, grad_up_raw)
        grad_normed_two = lax.psum(
            contract_cols(grad_up_raw, up_full).astype(jnp.bfloat16), "tp"
        ).astype(jnp.float32)
        grad_gain_two = jnp.sum(grad_normed_two * hidden * scale_two, axis=0)
        weighted_two = grad_normed_two * gain_two
        grad_hidden = (
            grad_out.astype(jnp.float32)
            + scale_two * weighted_two
            - hidden * scale_two**3 * jnp.mean(weighted_two * hidden, axis=-1, keepdims=True)
        )
        hidden_low = grad_hidden.astype(jnp.bfloat16)
        grad_out_proj = contract_rows(attn_low, hidden_low)
        grad_attn = (
            contract_cols(hidden_low, out_full)
            .astype(jnp.bfloat16)
            .reshape(tok_rows, head_count, head_size)
        )
        delta = jnp.einsum("qhd,qhd->hq", grad_attn.astype(jnp.float32), attn_heads)
        key_all, value_all = (
            lax.all_gather(key_local, "ctx", axis=0, tiled=True),
            lax.all_gather(value_local, "ctx", axis=0, tiled=True),
        )

        def block_terms(key_piece, value_piece, offset):
            key_heads = key_piece.reshape(key_block, head_count, head_size)
            value_heads = value_piece.reshape(key_block, head_count, head_size)
            key_pos = offset + jnp.arange(key_block, dtype=jnp.int32)
            allowed = (key_pos[None, :] <= positions[:, None]) & (
                segment_of(starts, key_pos)[None, :] == query_seg[:, None]
            )
            scores = jnp.einsum(
                "qhd,khd->hqk", query_heads, key_heads, preferred_element_type=jnp.float32
            )
            probs = jnp.where(allowed[None], jnp.exp(scores - log_total[:, :, None]), 0.0)
            grad_probs = jnp.einsum(
                "qhd,khd->hqk", grad_attn, value_heads, preferred_element_type=jnp.float32
            )
            grad_scores = (probs * (grad_probs - delta[:, :, None])).astype(jnp.bfloat16)
            return (key_heads, probs, grad_scores)

        key_blocks = (
            key_all.reshape(block_count, key_block, local_cols),
            value_all.reshape(block_count, key_block, local_cols),
            jnp.arange(block_count, dtype=jnp.int32) * key_block,
        )
        zero_query = jnp.zeros((tok_rows, head_count, head_size), jnp.float32)

        def grad_block(grad_query, packed):
            key_heads, probs, grad_scores = block_terms(packed[0], packed[1], packed[2])
            grad_value = jnp.einsum(
                "hqk,qhd->khd",
                probs.astype(jnp.bfloat16),
                grad_attn,
                preferred_element_type=jnp.float32,
            )
            grad_query = grad_query + jnp.einsum(
                "hqk,khd->qhd", grad_scores, key_heads, preferred_element_type=jnp.float32
            )
            grad_key = jnp.einsum(
                "hqk,qhd->khd", grad_scores, query_heads, preferred_element_type=jnp.float32
            )
            return (
                grad_query,
                (
                    grad_key.reshape(key_block, local_cols),
                    grad_value.reshape(key_block, local_cols),
                ),
            )

        grad_query, (key_terms, value_terms) = lax.scan(grad_block, zero_query, key_blocks)
        key_grad, value_grad = (
            lax.psum_scatter(
                key_terms.reshape(stream, local_cols).astype(jnp.bfloat16),
                "ctx",
                scatter_dimension=0,
                tiled=True,
            ).astype(jnp.float32),
            lax.psum_scatter(
                value_terms.reshape(stream, local_cols).astype(jnp.bfloat16),
                "ctx",
                scatter_dimension=0,
                tiled=True,
            ).astype(jnp.float32),
        )
        grad_query_raw = (
            (grad_query * query_scale).astype(jnp.bfloat16).reshape(tok_rows, local_cols)
        )
        scale_part = jnp.sum(grad_query * query_raw, axis=(0, 1))
        grad_cols = jnp.concatenate(
            [grad_query_raw, key_grad.astype(jnp.bfloat16), value_grad.astype(jnp.bfloat16)], axis=1
        )
        grad_qkv = contract_rows(normed_one, grad_cols)
        grad_normed_one, scale_total = (
            lax.psum(contract_cols(grad_cols, w_qkv).astype(jnp.bfloat16), "tp").astype(
                jnp.float32
            ),
            lax.psum(scale_part.astype(jnp.bfloat16), "tp").astype(jnp.float32),
        )
        scale_sum = scale_sum + scale_total
        grad_gain_one = jnp.sum(grad_normed_one * stream_in * scale_one, axis=0)
        weighted_one = grad_normed_one * gain_one
        input_grads.append(
            grad_hidden
            + scale_one * weighted_one
            - stream_in * scale_one**3 * jnp.mean(weighted_one * stream_in, axis=-1, keepdims=True)
        )
        grads = (
            grad_qkv[:, :local_cols],
            grad_qkv[:, local_cols : 2 * local_cols],
            grad_qkv[:, 2 * local_cols :],
            grad_up,
            grad_gain_one,
            grad_gain_two,
            grad_out_proj,
            grad_down,
        )
        shares = (
            lax.psum_scatter(
                grads[0].astype(jnp.bfloat16), "ctx", scatter_dimension=0, tiled=True
            ).astype(jnp.float32),
            lax.psum_scatter(
                grads[1].astype(jnp.bfloat16), "ctx", scatter_dimension=0, tiled=True
            ).astype(jnp.float32),
            lax.psum_scatter(
                grads[2].astype(jnp.bfloat16), "ctx", scatter_dimension=0, tiled=True
            ).astype(jnp.float32),
            lax.psum_scatter(
                grads[3].astype(jnp.bfloat16), "ctx", scatter_dimension=0, tiled=True
            ).astype(jnp.float32),
            lax.psum_scatter(
                grads[4].astype(jnp.bfloat16), "ctx", scatter_dimension=0, tiled=True
            ).astype(jnp.float32),
            lax.psum_scatter(
                grads[5].astype(jnp.bfloat16), "ctx", scatter_dimension=0, tiled=True
            ).astype(jnp.float32),
            lax.psum_scatter(
                grads[6].astype(jnp.bfloat16), "ctx", scatter_dimension=1, tiled=True
            ).astype(jnp.float32),
            lax.psum_scatter(
                grads[7].astype(jnp.bfloat16), "ctx", scatter_dimension=1, tiled=True
            ).astype(jnp.float32),
        )
        local_sums = (
            shares
            if local_sums is None
            else tuple((total + extra for total, extra in zip(local_sums, shares)))
        )
    scale_grad = lax.psum(scale_sum, "ctx")
    return (
        jnp.stack(outputs),
        jnp.stack(input_grads),
        local_sums[0],
        local_sums[1],
        local_sums[2],
        local_sums[6],
        local_sums[3],
        local_sums[7],
        local_sums[4],
        local_sums[5],
        scale_grad,
    )


def solution(mesh):
    in_specs = (
        P(None, "ctx", None),
        P(None, "ctx", None),
        P(),
        P("ctx", "tp"),
        P("ctx", "tp"),
        P("ctx", "tp"),
        P("tp", "ctx"),
        P("ctx", "tp"),
        P("tp", "ctx"),
        P("ctx"),
        P("ctx"),
        P(),
    )
    out_specs = (
        P(None, "ctx", None),
        P(None, "ctx", None),
        P("ctx", "tp"),
        P("ctx", "tp"),
        P("ctx", "tp"),
        P("tp", "ctx"),
        P("ctx", "tp"),
        P("tp", "ctx"),
        P("ctx"),
        P("ctx"),
        P(),
    )

    def run(*arrays):
        body = stream_per_group if fits(arrays, mesh) else per_device
        return jax.shard_map(
            body, mesh=mesh, in_specs=in_specs, out_specs=out_specs, check_vma=False
        )(*arrays)

    return run
```

```python
import functools
import math

import jax
import jax.numpy as jnp
from jax import lax
from jax.experimental import pallas as pl
from jax.experimental.pallas import tpu as pltpu
from jax.sharding import PartitionSpec as P

EPSILON = 1e-06
MASKED = -1e30
LANES = 128
WIDE = 512
BF = jnp.bfloat16
F32 = jnp.float32
SPARE_VMEM = 12 * 1024 * 1024


def call(kernel, out_shape, kinds, scratch=(), flops=0, moved=0, aliases=None):
    vmem = pl.BlockSpec(memory_space=pltpu.VMEM)
    smem = pl.BlockSpec(memory_space=pltpu.SMEM)
    hbm = pl.BlockSpec(memory_space=pl.ANY)
    room = sum(
        math.prod(ref.shape) * jnp.dtype(ref.dtype).itemsize
        for ref in scratch
        if ref.memory_space == pltpu.VMEM
    )
    return pl.pallas_call(
        kernel,
        out_shape=out_shape,
        in_specs=[{"s": smem, "v": vmem, "h": hbm}[kind] for kind in kinds],
        out_specs=jax.tree.map(lambda _: vmem, out_shape),
        scratch_shapes=list(scratch),
        input_output_aliases=aliases or {},
        compiler_params=pltpu.CompilerParams(vmem_limit_bytes=room + SPARE_VMEM),
        cost_estimate=pl.CostEstimate(
            flops=int(flops), transcendentals=0, bytes_accessed=int(moved)
        ),
    )


def struct(shape, dtype):
    return jax.ShapeDtypeStruct(tuple(shape), dtype)


def nn(a, b):
    return jnp.dot(a, b, preferred_element_type=F32)


def nt(a, b):
    return lax.dot_general(a, b, (((1,), (1,)), ((), ())), preferred_element_type=F32)


def tn(a, b):
    return lax.dot_general(a, b, (((0,), (0,)), ((), ())), preferred_element_type=F32)


def at(start, size, step=None):
    return pl.ds(pl.multiple_of(start, step or size), size)


def inverse_rms(values):
    return lax.rsqrt(jnp.mean(values * values, axis=-1, keepdims=True) + EPSILON)


def split_kernel(ids, whole, *out):
    z, c = ids[0], ids[2]
    half = out[0].shape[0]
    for kz in range(len(out)):
        out[kz][...] = whole[z ^ kz, at(c * half, half), :]


def split(ids, whole):
    groups, rows, width = whole.shape
    return call(
        split_kernel,
        (struct((rows // 2, width), whole.dtype),) * groups,
        "sv",
        moved=whole.size * 4,
    )(ids, whole)


def assemble_kernel(ids, own, other, out):
    groups, half, _ = own.shape
    c = ids[2]
    for kz in range(groups):
        out[ids[0] ^ kz, at(c * half, half), :] = own[kz].astype(out.dtype)
        out[ids[0] ^ kz, at((1 - c) * half, half), :] = other[kz].astype(out.dtype)


def assemble(ids, own, other, dtype):
    groups, half, width = own.shape
    return call(
        assemble_kernel, struct((groups, 2 * half, width), dtype), "svv", moved=own.size * 12
    )(ids, own, other)


def place_kernel(groups, ids, *refs):
    own, other, out = refs[:groups], refs[groups : 2 * groups], refs[2 * groups]
    half = own[0].shape[0]
    z, c = ids[0], ids[2]
    for kz in range(groups):
        out[z ^ kz, at(c * half, half), :] = own[kz][...].astype(out.dtype)
        out[z ^ kz, at((1 - c) * half, half), :] = other[kz][...].astype(out.dtype)


def pack_kernel(mine, ids, query, key, value, gains, *refs):
    out, tmp = refs[:-1], refs[-1]
    rows = query.shape[0]
    rest = jnp.concatenate([gains[...], jnp.zeros((rows, WIDE - 3 * mine - 2), BF)], axis=1)
    for k in range(len(out)):
        cols = slice(k * mine, (k + 1) * mine)
        tmp[k] = jnp.concatenate([query[:, cols], key[:, cols], value[:, cols], rest], axis=1)
    for kj in range(len(out)):
        out[kj][...] = tmp[ids[1] ^ kj]


def stack_kernel(up, out_t, down_t, out):
    cols = up.shape[1]
    for g in range(out.shape[0]):
        for n, part in enumerate((up, out_t, down_t)):
            out[g, :, n * cols : (n + 1) * cols] = part[...]


def spread_kernel(heads, size, ids, pieces, w, w_t, gains, rows_ref):
    groups, members, rows, _ = pieces.shape
    for kz in range(groups):
        for kj in range(members):
            where = at((kz * members + (ids[1] ^ kj)) * rows, rows, 16)
            rows_ref[where, :] = pieces[kz, kj]
    block = rows_ref[...]
    zeros = jnp.zeros((block.shape[0], LANES - size), BF)
    for h in range(3 * heads):
        w[:, h * LANES : (h + 1) * LANES] = jnp.concatenate(
            [block[:, h * size : (h + 1) * size], zeros], axis=1
        )
    w_t[...] = w[...].T
    first = 3 * heads * size - (WIDE - LANES)
    gains[...] = block[:, WIDE - LANES :].astype(F32).T[first : first + 8, :]


def order_kernel(ids, *refs):
    pieces, out = refs[:-3], refs[-3:]
    groups, rows, _ = pieces[0].shape
    members, cols = len(pieces), out[0].shape[1]
    for kj in range(members):
        for kz in range(groups):
            where = at((kz * members + (ids[1] ^ kj)) * rows, rows, 16)
            for n in range(3):
                out[n][where, :] = pieces[kj][kz, :, n * cols : (n + 1) * cols]


def project_kernel(members, step, ids, *refs):
    pieces = refs[: 2 * members]
    w, gain, scale, proj, normed = refs[2 * members :]
    groups, half, _ = pieces[0].shape
    z, j, c = ids[0], ids[1], ids[2]
    for kj in range(members):
        for kc in range(2):
            for kz in range(groups):
                base = (z ^ kz) * (members * 2) + (j ^ kj) * 2 + (c ^ kc)
                normed[at(base * half, half), :] = pieces[kc * members + kj][kz]

    def block(n, _):
        rows = at(n * step, step)
        x = normed[rows, :].astype(F32)
        xn = (x * inverse_rms(x) * gain[0:1, :]).astype(BF)
        normed[rows, :] = xn
        proj[rows, :] = (nn(xn, w[...]) * scale[...]).astype(BF)
        return 0

    lax.fori_loop(0, normed.shape[0] // step, block, 0)


def doc_bounds(lengths, z, place):
    start, begin, end = jnp.int32(0), jnp.int32(0), jnp.int32(0)
    for d in range(lengths.shape[1]):
        stop = start + lengths[z, d]
        inside = start <= place
        begin = jnp.where(inside, start, begin)
        end = jnp.where(inside, stop, end)
        start = stop
    return begin, end


def doc_starts(lengths, z, stream):
    place = lax.broadcasted_iota(jnp.int32, (8, stream), 1)
    start, row = jnp.int32(0), jnp.zeros((8, stream), jnp.int32)
    for d in range(lengths.shape[1]):
        row = jnp.where(place >= start, start, row)
        start = start + lengths[z, d]
    return row


def attend_kernel(heads, size, members, bq, bk, ids, lengths, proj, *refs):
    outs, (kept, sent, vt, doc) = refs[:members], refs[members:]
    stream = proj.shape[0]
    z, j = ids[0], ids[1]
    doc[...] = doc_starts(lengths, z, stream)
    for h in range(heads):
        vt[h] = proj[:, (2 * heads + h) * LANES : (2 * heads + h + 1) * LANES].T

    def one_query_block(qb, _):
        rows = at(qb * bq, bq)
        qpos = qb * bq + lax.broadcasted_iota(jnp.int32, (1, bq), 1)
        queries = [proj[rows, h * LANES : (h + 1) * LANES] for h in range(heads)]

        def one_key_block(kb, carry):
            keys = at(kb * bk, bk)
            kpos = kb * bk + lax.broadcasted_iota(jnp.int32, (bk, bq), 0)
            allowed = (kpos <= qpos) & (kpos >= doc[0:1, rows])
            new = []
            for h in range(heads):
                top, total, acc = carry[h]
                k = proj[keys, (heads + h) * LANES : (heads + h + 1) * LANES]
                s = jnp.where(allowed, nt(k, queries[h]), MASKED)
                top2 = jnp.maximum(top, jnp.max(s, axis=0, keepdims=True))
                p = jnp.exp(s - top2)
                alpha = jnp.exp(top - top2)
                total = total * alpha + jnp.sum(p, axis=0, keepdims=True)
                acc = acc * alpha + nn(vt[h, :, keys], p.astype(BF))
                new.append((top2, total, acc))
            return tuple(new)

        zero = (
            jnp.full((1, bq), MASKED, F32),
            jnp.zeros((1, bq), F32),
            jnp.zeros((LANES, bq), F32),
        )
        begin, _ = doc_bounds(lengths, z, qb * bq)
        end = (qb * bq + bq + bk - 1) // bk
        carry = lax.fori_loop(begin // bk, end, one_key_block, (zero,) * heads)
        for h in range(heads):
            top, total, acc = carry[h]
            o = acc / total
            kept[h, :LANES, rows] = o
            kept[h, LANES:, rows] = jnp.broadcast_to(top + jnp.log(total), (8, bq))
            low = o[:size].astype(BF)
            for part in range(bq // LANES):
                block = qb * (bq // LANES) + part
                lanes = at(block // members * LANES, LANES)
                sent[(block % members) ^ j, h * size : (h + 1) * size, lanes] = low[
                    :, part * LANES : (part + 1) * LANES
                ]
        return 0

    lax.fori_loop(0, stream // bq, one_query_block, 0)
    for kj in range(members):
        outs[kj][...] = sent[kj]


def store_weights(heads, size, count, scale_sum, full, out):
    rows = out.shape[0] // count
    pad = WIDE - 3 * heads * size
    s = scale_sum[:size, :pad]
    high = s.astype(BF)
    rest = (s - high.astype(F32)).astype(BF)
    lane = lax.broadcasted_iota(jnp.int32, (size, pad), 1)
    tail = jnp.where(lane == 0, high, jnp.where(lane == 1, rest, jnp.zeros_like(rest)))
    tail = [tail, jnp.zeros((rows - size, pad), BF)] if rows > size else [tail]
    tail = jnp.concatenate(tail, axis=0)
    for n in range(count):
        block = full[n * rows : (n + 1) * rows, :].astype(BF)
        out[n * rows : (n + 1) * rows, :] = jnp.concatenate(
            [block[:, h * LANES : h * LANES + size] for h in range(3 * heads)] + [tail], axis=1
        )


def attend_back_kernel(heads, size, members, bq, bk, ids, lengths, proj, kept, scale, w, normed, *refs):
    pieces = refs[:members]
    grads, there, weights, dot_, do_, kt, dqt, delta, doc, rows_ref, full = refs[members:]
    stream = proj.shape[0]
    groups = pieces[0].shape[1] // LANES
    z, j = ids[0], ids[1]
    doc[...] = doc_starts(lengths, z, stream)
    for h in range(heads):
        kt[h] = proj[:, (heads + h) * LANES : (heads + h + 1) * LANES].T
        dot_[h, size:, :] = jnp.zeros((LANES - size, stream), BF)
        for kj in range(members):
            for g in range(groups):
                lanes = at((g * members + (j ^ kj)) * LANES, LANES)
                dot_[h, :size, lanes] = pieces[kj][
                    h * size : (h + 1) * size, g * LANES : (g + 1) * LANES
                ]
        do_[h] = dot_[h].T
        delta[h] = jnp.broadcast_to(
            jnp.sum(dot_[h].astype(F32) * kept[h, :LANES, :], axis=0, keepdims=True), (8, stream)
        )
        dqt[h] = jnp.zeros((LANES, stream), F32)

    def one_key_block(kb, _):
        keys = at(kb * bk, bk)
        kpos = kb * bk + lax.broadcasted_iota(jnp.int32, (bk, bq), 0)
        ks = [proj[keys, (heads + h) * LANES : (heads + h + 1) * LANES] for h in range(heads)]
        vs = [
            proj[keys, (2 * heads + h) * LANES : (2 * heads + h + 1) * LANES] for h in range(heads)
        ]

        def one_query_block(qb, carry):
            rows = at(qb * bq, bq)
            qpos = qb * bq + lax.broadcasted_iota(jnp.int32, (1, bq), 1)
            allowed = (kpos <= qpos) & (kpos >= doc[0:1, rows])
            new = []
            for h in range(heads):
                dk, dv = carry[h]
                q = proj[rows, h * LANES : (h + 1) * LANES]
                p = jnp.exp(nt(ks[h], q) - kept[h, LANES : LANES + 1, rows])
                p = jnp.where(allowed, p, 0.0)
                dp = nn(vs[h], dot_[h, :, rows])
                ds = (p * (dp - delta[h, 0:1, rows])).astype(BF)
                dv = dv + nn(p.astype(BF), do_[h, rows, :])
                dk = dk + nn(ds, q)
                dqt[h, :, rows] += nn(kt[h, :, keys], ds)
                new.append((dk, dv))
            return tuple(new)

        _, final = doc_bounds(lengths, z, kb * bk + bk - 1)
        zero = jnp.zeros((bk, LANES), F32)
        carry = lax.fori_loop(
            kb * bk // bq, (final + bq - 1) // bq, one_query_block, ((zero, zero),) * heads
        )
        for h in range(heads):
            for n in range(2):
                cols = ((n + 1) * heads + h) * LANES
                grads[keys, cols : cols + LANES] = carry[h][n].astype(BF)
        return 0

    lax.fori_loop(0, stream // bk, one_key_block, 0)
    total = jnp.zeros((1, LANES), F32)
    for h in range(heads):
        dq = dqt[h].T
        q = proj[:, h * LANES : (h + 1) * LANES].astype(F32)
        total = total + jnp.sum(dq * q, axis=0, keepdims=True)
        grads[:, h * LANES : (h + 1) * LANES] = (dq * scale[...]).astype(BF)
    _, _, half, width = there.shape

    def one_member(kj, _):
        y = nn(input_rows(ids, grads, rows_ref, kj, 1, members, half), w[...])
        there[kj] = y.reshape(groups, half, width).astype(BF)
        return 0

    lax.fori_loop(0, members, one_member, 0)
    total = jnp.broadcast_to(total / scale[...], (LANES, LANES)).T
    full[...] = tn(normed[...], grads[...])
    store_weights(heads, size, groups * members, total, full, weights)


def out_kernel(ids, *refs):
    pieces, (w, ob_t, part) = refs[:-3], refs[-3:]
    mine = pieces[0].shape[0]
    for kj in range(len(pieces)):
        ob_t[at((ids[1] ^ kj) * mine, mine, 16), :] = pieces[kj][...]
    part[...] = nt(ob_t[...].T, w[...]).astype(BF)


def mlp_kernel(groups, ids, *refs):
    x_own, x_other = refs[0], refs[1]
    g_own, g_other, attn, attn_other, up, down, gains = refs[2:9]
    hidden, normed, act, grad_up, cot, part, back = refs[9:]
    half = x_own.shape[1]
    z, c = ids[0], ids[2]
    for kz in range(groups):
        for kc in range(2):
            rows = at((z ^ kz) * (2 * half) + (c ^ kc) * half, half)
            hidden[rows, :] = (x_other if kc else x_own)[kz].astype(F32) + (
                attn[rows, :].astype(F32) + attn_other[rows, :].astype(F32)
            )
            cot[rows, :] = (g_other if kc else g_own)[kz]
    step = hidden.shape[0] // 2

    def block(n, _):
        rows = at(n * step, step)
        h = hidden[rows, :]
        xn = (h * inverse_rms(h) * gains[1:2, :]).astype(BF)
        u = nn(xn, up[...])
        sigma = jax.nn.sigmoid(u)
        a = (u * sigma).astype(BF)
        da = nn(cot[rows, :], down[...])
        du = (da * sigma * (1.0 + u * (1.0 - sigma))).astype(BF)
        part[rows, :] = nt(a, down[...]).astype(BF)
        back[rows, :] = nt(du, up[...]).astype(BF)
        normed[rows, :] = xn
        act[rows, :] = a
        grad_up[rows, :] = du
        return 0

    lax.fori_loop(0, 2, block, 0)


def hidden_kernel(groups, members, ids, *refs):
    hidden, cot, part, part_other, back, back_other, w, gains = refs[:8]
    low, dh_half = refs[8:10]
    pieces, out = refs[10 : 10 + members], refs[10 + members : 10 + members + groups]
    dh, lay, do_t = refs[10 + members + groups :]
    rows_all = hidden.shape[0]
    half = rows_all // groups // 2
    mine = pieces[0].shape[0]
    z, j, c = ids[0], ids[1], ids[2]
    step = rows_all // groups

    def block(n, _):
        rows = at(n * step, step)
        h = hidden[rows, :]
        scale = inverse_rms(h)
        grad = back[rows, :].astype(F32) + back_other[rows, :].astype(F32)
        weighted = grad * gains[1:2, :]
        d = (
            cot[rows, :].astype(F32)
            + scale * weighted
            - h * scale**3 * jnp.mean(weighted * h, axis=-1, keepdims=True)
        )
        dh[rows, :] = d
        low[rows, :] = d.astype(BF)
        lay[rows, :] = (
            h + (part[rows, :].astype(F32) + part_other[rows, :].astype(F32))
        ).astype(BF)
        return 0

    lax.fori_loop(0, groups, block, 0)
    do_t[...] = nn(low[...], w[...]).T.astype(BF)
    for kj in range(members):
        pieces[kj][...] = do_t[at((j ^ kj) * mine, mine, 16), :]
    for g in range(groups):
        out[g][...] = lay[at((z ^ g) * 2 * half + c * half, half), :]
        dh_half[g] = dh[at(g * 2 * half + c * half, half), :]


def by_member(ids, full, out, first=0):
    groups, rows, _ = out[0].shape
    for kj in range(len(out)):
        for g in range(groups):
            where = at((g * len(out) + (ids[1] ^ kj)) * rows, rows, 16)
            out[kj][g, :, first : first + full.shape[1]] = full[where, :]


def feed_weights_kernel(ids, normed, grad_up, cot, act, *refs):
    out, full = refs[:-1], refs[-1]
    full[...] = tn(normed[...], grad_up[...]).astype(BF)
    by_member(ids, full, out)
    full[...] = tn(cot[...], act[...]).astype(BF)
    by_member(ids, full, out, full.shape[1])


def out_weights_kernel(ids, low, ob_t, *refs):
    out, full = refs[:-1], refs[-1]
    full[...] = tn(low[...], ob_t[...].T).astype(BF)
    by_member(ids, full, out)


def sum_members_kernel(*refs):
    total = refs[0][...].astype(F32)
    for part in refs[1:-1]:
        total = total + part[...].astype(F32)
    refs[-1][...] = total.astype(BF)


def sum_split_kernel(members, ids, *refs):
    parts, out, tmp = refs[:members], refs[members:-1], refs[-1]
    total = parts[0][...].astype(F32)
    for part in parts[1:]:
        total = total + part[...].astype(F32)
    tmp[...] = total.astype(BF)
    for kz in range(len(out)):
        out[kz][...] = tmp[ids[0] ^ kz]


def rows_kernel(groups, parts, up, *refs):
    outs, (grad_up, grad_down, grad_out, gain) = refs[:groups], refs[groups:]
    cols = up.shape[1]
    total = parts[0].astype(F32)
    for g in range(1, parts.shape[0]):
        total = total + parts[g].astype(F32)
    grad_up[...] = total[:, :cols]
    grad_down[...] = total[:, cols:].T
    term = jnp.sum(total[:, :cols] * up[...].astype(F32), axis=1, keepdims=True)
    gain[...] = jnp.broadcast_to(term, gain.shape)
    total = outs[0][...].astype(F32)
    for part in outs[1:]:
        total = total + part[...].astype(F32)
    grad_out[...] = total.T


def input_rows(ids, grads, rows_ref, kj, which, members, half):
    for g in range(rows_ref.shape[0] // half):
        base = (g * members + (ids[1] ^ kj)) * 2 + (ids[2] ^ which)
        rows_ref[g * half : (g + 1) * half, :] = grads[at(base * half, half), :]
    return rows_ref[...]


def input_here_kernel(ids, grads, w, other, *refs):
    out, rows_ref = refs[:-1], refs[-1]
    members, (groups, half, width) = len(out), out[0].shape
    for kj in reversed(range(members)):
        y = nn(input_rows(ids, grads, rows_ref, kj, 0, members, half), w[...])
        y = y + other[kj].reshape(groups * half, width).astype(F32)
        out[kj][...] = y.reshape(groups, half, width).astype(BF)


def qkv_sum_kernel(ids, parts, *refs):
    out, tmp = refs[:-1], refs[-1]
    total = parts[0].astype(F32)
    for g in range(1, parts.shape[0]):
        total = total + parts[g].astype(F32)
    tmp[...] = total
    rows = out[0].shape[0]
    for kj in range(len(out)):
        out[kj][...] = tmp[at((ids[1] ^ kj) * rows, rows, 16), :].astype(BF)


def qkv_rows_kernel(mine, ids, *refs):
    members = len(refs) - 8
    pieces, (query, key, value, dq, dk, dv, small, tmp) = refs[:members], refs[members:]
    for kj in range(members):
        tmp[ids[1] ^ kj] = pieces[kj][...].astype(F32)
    gain = None
    for n, (w, dw) in enumerate(((query, dq), (key, dk), (value, dv))):
        dw[...] = jnp.concatenate(
            [tmp[k][:, n * mine : (n + 1) * mine] for k in range(members)], axis=1
        )
        term = jnp.sum(dw[...] * w[...].astype(F32), axis=1, keepdims=True)
        gain = term if gain is None else gain + term
    scale = tmp[0][:, 3 * mine : 3 * mine + 2]
    for k in range(1, members):
        scale = scale + tmp[k][:, 3 * mine : 3 * mine + 2]
    scale = jnp.sum(scale, axis=1, keepdims=True)
    lane = lax.broadcasted_iota(jnp.int32, small.shape, 1)
    small[...] = jnp.where(lane == 0, gain, jnp.where(lane == 1, scale, 0.0))


def tokens_kernel(groups, ids, *refs):
    x, dh, gains = refs[:3]
    parts, out = refs[3:-groups], refs[-groups:]
    z = ids[0]
    for kz in range(groups):
        grad = parts[0][z ^ kz].astype(F32)
        for part in parts[1:]:
            grad = grad + part[z ^ kz].astype(F32)
        xx = x[kz].astype(F32)
        scale = inverse_rms(xx)
        weighted = grad * gains[0:1, :]
        out[kz][...] = (
            dh[z ^ kz]
            + scale * weighted
            - xx * scale**3 * jnp.mean(weighted * xx, axis=-1, keepdims=True)
        ).astype(BF)


def stream_per_group(
    tokens,
    cotangent,
    doc_lengths,
    w_query,
    w_key,
    w_value,
    w_out,
    w_up,
    w_down,
    gain_attn,
    gain_mlp,
    query_scale,
):
    groups, tok_rows, width = tokens.shape
    count = lax.axis_size("ctx")
    members = count // groups
    size = query_scale.shape[0]
    local = w_query.shape[1]
    shard = width // count
    heads = local // size // members
    half = tok_rows // 2
    stream = tok_rows * count
    mine = heads * size
    rows = groups * tok_rows
    padded = 3 * heads * LANES
    me = lax.axis_index("ctx")
    ids = jnp.stack([me // members, me % members, lax.axis_index("tp")]).astype(jnp.int32)

    planes = [[g * members + k for k in range(members)] for g in range(groups)]
    lines = [[g * members + k for g in range(groups)] for k in range(members)]

    def across(a, mask):
        return lax.ppermute(a, "ctx", [(i, i ^ mask) for i in range(count)])

    def shift(a, by):
        pairs = [(i, i + by * members) for i in range(count)]
        return lax.ppermute(a, "ctx", [(i, k) for i, k in pairs if 0 <= k < count])

    def swap(a):
        return lax.ppermute(a, "tp", [(0, 1), (1, 0)])

    def to_groups(parts):
        return [parts[0]] + [across(parts[k], k * members) for k in range(1, groups)]

    def to_members(parts):
        return [parts[0]] + [across(parts[k], k) for k in range(1, members)]

    def exchange(a, teams):
        return lax.all_to_all(a, "ctx", 0, 0, axis_index_groups=teams, tiled=True)

    def tie(*values):
        return lax.optimization_barrier(values)

    def quarter(own, beside, above):
        cut = groups // 2
        return jnp.concatenate([across(above[:cut], 1), across(beside[cut:], 2)])

    packed = call(
        functools.partial(pack_kernel, mine),
        (struct((shard, WIDE), BF),) * members,
        "svvvv",
        scratch=[pltpu.VMEM((members, shard, WIDE), BF)],
        moved=shard * WIDE * members * 4,
    )(ids, w_query, w_key, w_value, jnp.stack([gain_attn, gain_mlp], axis=1))
    own = jnp.stack(to_groups(split(ids, tokens)))

    shards = call(
        stack_kernel,
        struct((groups, shard, 3 * local), BF),
        "vvv",
        moved=groups * shard * local * 8,
    )(w_up, w_out.T, w_down.T)
    own, packed, shards = tie(own, packed, shards)
    shards = exchange(shards, lines)
    cols = to_members(packed)
    late, cols = tie(own, cols)
    pieces = to_members([own] * (members - 1) + [late])
    pieces, cols, shards = tie(pieces, jnp.stack(cols), shards)
    cols = jnp.concatenate([cols] * groups)

    cols = exchange(cols, lines).reshape(groups, members, shard, WIDE)
    others = [swap(piece) for piece in pieces]
    if members == 4:
        beside, above = across(shards, 1), across(shards, 2)
        cols, others, beside, above = tie(cols, others, beside, above)
        shards = [shards, beside, above, quarter(shards, beside, above)]
    else:
        cols, others, shards = tie(cols, others, to_members([shards] * members))
    pieces = pieces + others
    g_parts, cols = tie(split(ids, cotangent), cols)
    g_own = to_groups(g_parts)
    w_qkv, w_qkv_t, gains = call(
        functools.partial(spread_kernel, heads, size),
        (struct((width, padded), BF), struct((padded, width), BF), struct((8, width), F32)),
        "sv",
        scratch=[pltpu.VMEM((width, WIDE), BF)],
        moved=width * padded * 6,
    )(ids, cols)
    scale_row = jnp.pad(query_scale, (0, LANES - size), constant_values=1.0)[None, :]
    scale_all = jnp.concatenate(
        [scale_row] * heads + [jnp.ones((1, 2 * heads * LANES), F32)], axis=1
    )

    proj, normed = call(
        functools.partial(project_kernel, members, 512),
        (struct((stream, padded), BF), struct((stream, width), BF)),
        "s" + "v" * (2 * members + 3),
        flops=2 * stream * width * padded,
        moved=stream * width * 4,
    )(ids, *pieces, w_qkv, gains, scale_all)

    bq, bk = 512, 512
    *sent, kept = call(
        functools.partial(attend_kernel, heads, size, members, bq, bk),
        (struct((mine, rows), BF),) * members + (struct((heads, LANES + 8, stream), F32),),
        "ssv",
        scratch=[
            pltpu.VMEM((members, mine, rows), BF),
            pltpu.VMEM((heads, LANES, stream), BF),
            pltpu.VMEM((8, stream), jnp.int32),
        ],
        flops=2 * stream * stream * LANES * heads,
        moved=stream * LANES * heads * 10,
    )(ids, doc_lengths, proj)
    sent, shards, g_own = tie(sent, shards, g_own)
    arrived = to_members(sent)
    g_own = jnp.stack(g_own)
    g_other = swap(g_own)
    up_full, out_t, down_t = call(
        order_kernel,
        (struct((width, local), BF),) * 3,
        "s" + "v" * members,
        moved=width * local * 12,
    )(ids, *shards)

    ob_t, attn = call(
        out_kernel,
        (struct((local, rows), BF), struct((rows, width), BF)),
        "s" + "v" * (members + 1),
        flops=2 * rows * local * width,
        moved=local * width * 4,
    )(ids, *arrived, out_t)
    hidden, normed_two, activated, grad_up_raw, cot, part, back = call(
        functools.partial(mlp_kernel, groups),
        (
            struct((rows, width), F32),
            struct((rows, width), BF),
            struct((rows, local), BF),
            struct((rows, local), BF),
            struct((rows, width), BF),
            struct((rows, width), BF),
            struct((rows, width), BF),
        ),
        "s" + "v" * 9,
        flops=8 * rows * local * width,
        moved=local * width * 12,
    )(ids, pieces[0], pieces[members], g_own, g_other, attn, swap(attn), up_full, down_t, gains)
    back_other, part_other = swap(back), swap(part)
    feed_grads = call(
        feed_weights_kernel,
        (struct((groups, shard, 2 * local), BF),) * members,
        "svvvv",
        scratch=[pltpu.VMEM((width, local), BF)],
        flops=4 * rows * local * width,
        moved=local * width * 8,
    )(ids, normed_two, grad_up_raw, cot, activated)
    back_other, part_other, feed_grads = tie(back_other, part_other, feed_grads)
    hidden_low, dh_half, *results = call(
        functools.partial(hidden_kernel, groups, members),
        (struct((rows, width), BF), struct((groups, half, width), F32))
        + (struct((mine, rows), BF),) * members
        + (struct((half, width), BF),) * groups,
        "s" + "v" * 8,
        scratch=[
            pltpu.VMEM((rows, width), F32),
            pltpu.VMEM((rows, width), BF),
            pltpu.VMEM((local, rows), BF),
        ],
        flops=2 * rows * local * width,
        moved=local * width * 12,
    )(ids, hidden, cot, part, part_other, back, back_other, out_t, gains)
    do_pieces, out_parts = to_members(results[:members]), results[members:]
    out_grads = call(
        out_weights_kernel,
        (struct((groups, shard, local), BF),) * members,
        "svv",
        scratch=[pltpu.VMEM((width, local), BF)],
        flops=2 * rows * local * width,
        moved=local * width * 4,
    )(ids, hidden_low, ob_t)
    do_pieces, out_grads, out_parts, feed_grads = tie(do_pieces, out_grads, out_parts, feed_grads)

    feed_grads = to_members(feed_grads)
    out_own = to_groups(out_parts)

    grads, there, qkv_parts = call(
        functools.partial(attend_back_kernel, heads, size, members, bq, bk),
        (
            struct((stream, padded), BF),
            struct((members, groups, half, width), BF),
            struct((width, WIDE), BF),
        ),
        "ssvvvvv" + "v" * members,
        scratch=[
            pltpu.VMEM((heads, LANES, stream), BF),
            pltpu.VMEM((heads, stream, LANES), BF),
            pltpu.VMEM((heads, LANES, stream), BF),
            pltpu.VMEM((heads, LANES, stream), F32),
            pltpu.VMEM((heads, 8, stream), F32),
            pltpu.VMEM((8, stream), jnp.int32),
            pltpu.VMEM((groups * half, padded), BF),
            pltpu.VMEM((width, padded), F32),
        ],
        flops=5 * stream * stream * LANES * heads,
        moved=stream * LANES * heads * 20,
    )(ids, doc_lengths, proj, kept, scale_row, w_qkv_t, normed, *do_pieces)
    there, grads, qkv_parts, feed_grads, out_own[1], out_own[2], out_grads = tie(
        there, grads, qkv_parts, feed_grads, out_own[1], out_own[2], out_grads
    )

    there = swap(there)
    here = call(
        input_here_kernel,
        (struct((groups, half, width), BF),) * members,
        "svvv",
        scratch=[pltpu.VMEM((groups * half, padded), BF)],
        flops=stream * width * padded,
        moved=stream * width * 2,
    )(ids, grads, w_qkv_t, there)
    here, feed_grads, qkv_parts = tie(here, feed_grads, qkv_parts)
    sums = to_members(here)
    qkv_parts = exchange(qkv_parts, lines).reshape(groups, width // groups, WIDE)
    feed_grads = call(
        sum_members_kernel,
        struct((groups, shard, 2 * local), BF),
        "v" * members,
        moved=groups * shard * local * 24,
    )(*feed_grads)
    sums, feed_grads, out_grads = tie(sums, feed_grads, out_grads)
    grad_x = call(
        functools.partial(tokens_kernel, groups),
        (struct((half, width), BF),) * groups,
        "svvv" + "v" * len(sums),
        moved=groups * half * width * 12,
    )(ids, pieces[0], dh_half, gains, *sums)
    grad_x, qkv_parts, out_own, feed_grads, out_grads = tie(
        grad_x, qkv_parts, out_own, feed_grads, out_grads
    )
    feed_grads = exchange(feed_grads, lines)
    gx_own = to_groups(grad_x)
    out_grads = to_members(out_grads)
    out_own = jnp.stack(out_own)
    layer_out = assemble(ids, out_own, swap(out_own), BF)
    qkv_parts = call(
        qkv_sum_kernel,
        (struct((shard, WIDE), BF),) * members,
        "sv",
        scratch=[pltpu.VMEM((width // groups, WIDE), F32)],
        moved=width * WIDE * 4,
    )(ids, qkv_parts)
    gx_own, qkv_parts, layer_out, out_grads = tie(gx_own, qkv_parts, layer_out, out_grads)
    qkv_parts = to_members(qkv_parts)
    out_grads = call(
        functools.partial(sum_split_kernel, members),
        (struct((shard, local), BF),) * groups,
        "s" + "v" * members,
        scratch=[pltpu.VMEM((groups, shard, local), BF)],
        moved=groups * shard * local * 12,
    )(ids, *out_grads)
    out_grads = to_groups(out_grads)
    gx_other = [swap(piece) for piece in gx_own]
    grad_up, grad_down, grad_out, gain_two = call(
        functools.partial(rows_kernel, groups),
        (struct((shard, local), F32),)
        + (struct((local, shard), F32),) * 2
        + (struct((shard, LANES), F32),),
        "v" * (groups + 2),
        moved=shard * local * 36,
    )(feed_grads, w_up, *out_grads)
    grad_q, grad_k, grad_v, small = call(
        functools.partial(qkv_rows_kernel, mine),
        (struct((shard, local), F32),) * 3 + (struct((shard, LANES), F32),),
        "s" + "v" * (members + 3),
        scratch=[pltpu.VMEM((members, shard, WIDE), F32)],
        moved=shard * local * 24,
    )(ids, *qkv_parts, w_query, w_key, w_value)
    lane = lax.broadcasted_iota(jnp.int32, small.shape, 1)
    small = jnp.where(lane == 2, gain_two, small)
    small = small + swap(small)
    gx_other, small = tie(gx_other, small)
    grad_tokens = call(
        functools.partial(place_kernel, groups),
        struct((groups, tok_rows, width), F32),
        "s" + "v" * (2 * groups),
        moved=rows * width * 8,
    )(ids, *gx_own, *gx_other)
    return (
        layer_out,
        grad_tokens,
        grad_q,
        grad_k,
        grad_v,
        grad_out,
        grad_up,
        grad_down,
        small[:, 0] / gain_attn.astype(F32),
        small[:, 2] / gain_mlp.astype(F32),
        small[:size, 1],
    )


def fits(shapes, mesh):
    groups, stream, width = shapes[0].shape
    count, cores = mesh.shape["ctx"], mesh.shape["tp"]
    size = shapes[11].shape[0]
    if cores != 2 or count % groups:
        return False
    members = count // groups
    local_heads = shapes[3].shape[1] // cores // size
    return (
        groups & (groups - 1) == 0
        and members & (members - 1) == 0
        and members % 2 == 0
        and local_heads % members == 0
        and stream // count == LANES
        and stream % 512 == 0
        and size % 16 == 0
        and size <= LANES
        and size <= width // count
        and width // count % 16 == 0
        and 3 * local_heads // members * size + 2 <= WIDE
        and 3 * local_heads // members * size >= WIDE - LANES
        and width % (LANES * 2) == 0
    )


def segment_of(starts, positions):
    return jnp.sum((starts[None, :] <= positions[:, None]).astype(jnp.int32), axis=1)


def contract_rows(left, right):
    return lax.dot_general(
        left, right, (((0,), (0,)), ((), ())), preferred_element_type=jnp.float32
    )


def contract_cols(left, right):
    return lax.dot_general(
        left, right, (((1,), (1,)), ((), ())), preferred_element_type=jnp.float32
    )


def per_device(
    tokens,
    cotangent,
    doc_lengths,
    w_query,
    w_key,
    w_value,
    w_out,
    w_up,
    w_down,
    gain_attn,
    gain_mlp,
    query_scale,
):
    micro_count, tok_rows, model_width = tokens.shape
    head_size = query_scale.shape[0]
    local_cols = w_query.shape[1]
    head_count = local_cols // head_size
    stream = tok_rows * lax.axis_size("ctx")
    key_block = min(512, stream)
    block_count = stream // key_block
    positions = lax.axis_index("ctx") * tok_rows + jnp.arange(tok_rows, dtype=jnp.int32)
    local_sums = None
    scale_sum = jnp.zeros((head_size,), jnp.float32)
    outputs = []
    input_grads = []
    for micro_step in range(micro_count):
        gathered = (
            lax.all_gather(w_query, "ctx", axis=0, tiled=True),
            lax.all_gather(w_key, "ctx", axis=0, tiled=True),
            lax.all_gather(w_value, "ctx", axis=0, tiled=True),
            lax.all_gather(w_up, "ctx", axis=0, tiled=True),
            lax.all_gather(gain_attn, "ctx", axis=0, tiled=True),
            lax.all_gather(gain_mlp, "ctx", axis=0, tiled=True),
            lax.all_gather(w_out, "ctx", axis=1, tiled=True),
            lax.all_gather(w_down, "ctx", axis=1, tiled=True),
        )
        w_qkv = jnp.concatenate([gathered[0], gathered[1], gathered[2]], axis=1)
        up_full = gathered[3]
        gain_one = gathered[4].astype(jnp.float32)
        gain_two = gathered[5].astype(jnp.float32)
        out_full = gathered[6]
        down_full = gathered[7]
        lengths = doc_lengths[micro_step]
        starts = jnp.cumsum(lengths) - lengths
        query_seg = segment_of(starts, positions)
        stream_in = tokens[micro_step].astype(jnp.float32)
        scale_one = inverse_rms(stream_in)
        normed_one = (stream_in * scale_one * gain_one).astype(jnp.bfloat16)
        projected = jnp.dot(normed_one, w_qkv, preferred_element_type=jnp.float32)
        query_raw = projected[:, :local_cols].reshape(tok_rows, head_count, head_size)
        query_heads = (query_raw * query_scale).astype(jnp.bfloat16)
        key_local = projected[:, local_cols : 2 * local_cols].astype(jnp.bfloat16)
        value_local = projected[:, 2 * local_cols :].astype(jnp.bfloat16)
        row_top = jnp.full((head_count, tok_rows), MASKED, jnp.float32)
        key_piece = lax.all_gather(key_local, "ctx", axis=0, tiled=True)
        value_piece = lax.all_gather(value_local, "ctx", axis=0, tiled=True)
        length = key_piece.shape[0]
        key_pos = jnp.arange(length, dtype=jnp.int32)
        allowed = (key_pos[None, :] <= positions[:, None]) & (
            segment_of(starts, key_pos)[None, :] == query_seg[:, None]
        )
        scores = jnp.einsum(
            "qhd,khd->hqk",
            query_heads,
            key_piece.reshape(length, head_count, head_size),
            preferred_element_type=jnp.float32,
        )
        scores = jnp.where(allowed[None], scores, MASKED)
        new_top = jnp.maximum(row_top, jnp.max(scores, axis=-1))
        probs = jnp.where(allowed[None], jnp.exp(scores - new_top[:, :, None]), 0.0)
        row_sum = jnp.sum(probs, axis=-1)
        update = jnp.einsum(
            "hqk,khd->qhd",
            probs.astype(jnp.bfloat16),
            value_piece.reshape(length, head_count, head_size),
            preferred_element_type=jnp.float32,
        )
        weighted = update
        row_top, row_sum, weighted = (new_top, row_sum, weighted)
        attn_heads = weighted / jnp.transpose(row_sum)[:, :, None]
        log_total = row_top + jnp.log(row_sum)
        attn_low = attn_heads.reshape(tok_rows, local_cols).astype(jnp.bfloat16)
        attn_out = lax.psum(
            jnp.dot(attn_low, out_full, preferred_element_type=jnp.float32).astype(jnp.bfloat16),
            "tp",
        ).astype(jnp.float32)
        hidden = stream_in + attn_out
        scale_two = inverse_rms(hidden)
        normed_two = (hidden * scale_two * gain_two).astype(jnp.bfloat16)
        up_raw = jnp.dot(normed_two, up_full, preferred_element_type=jnp.float32)
        activated = jax.nn.silu(up_raw).astype(jnp.bfloat16)
        mlp_out = lax.psum(
            jnp.dot(activated, down_full, preferred_element_type=jnp.float32).astype(jnp.bfloat16),
            "tp",
        ).astype(jnp.float32)
        outputs.append((hidden + mlp_out).astype(jnp.bfloat16))
        grad_out = cotangent[micro_step]
        grad_down = contract_rows(activated, grad_out)
        grad_act = contract_cols(grad_out, down_full)
        sigma = jax.nn.sigmoid(up_raw)
        grad_up_raw = (grad_act * sigma * (1.0 + up_raw * (1.0 - sigma))).astype(jnp.bfloat16)
        grad_up = contract_rows(normed_two, grad_up_raw)
        grad_normed_two = lax.psum(
            contract_cols(grad_up_raw, up_full).astype(jnp.bfloat16), "tp"
        ).astype(jnp.float32)
        grad_gain_two = jnp.sum(grad_normed_two * hidden * scale_two, axis=0)
        weighted_two = grad_normed_two * gain_two
        grad_hidden = (
            grad_out.astype(jnp.float32)
            + scale_two * weighted_two
            - hidden * scale_two**3 * jnp.mean(weighted_two * hidden, axis=-1, keepdims=True)
        )
        hidden_low = grad_hidden.astype(jnp.bfloat16)
        grad_out_proj = contract_rows(attn_low, hidden_low)
        grad_attn = (
            contract_cols(hidden_low, out_full)
            .astype(jnp.bfloat16)
            .reshape(tok_rows, head_count, head_size)
        )
        delta = jnp.einsum("qhd,qhd->hq", grad_attn.astype(jnp.float32), attn_heads)
        key_all, value_all = (
            lax.all_gather(key_local, "ctx", axis=0, tiled=True),
            lax.all_gather(value_local, "ctx", axis=0, tiled=True),
        )

        def block_terms(key_piece, value_piece, offset):
            key_heads = key_piece.reshape(key_block, head_count, head_size)
            value_heads = value_piece.reshape(key_block, head_count, head_size)
            key_pos = offset + jnp.arange(key_block, dtype=jnp.int32)
            allowed = (key_pos[None, :] <= positions[:, None]) & (
                segment_of(starts, key_pos)[None, :] == query_seg[:, None]
            )
            scores = jnp.einsum(
                "qhd,khd->hqk", query_heads, key_heads, preferred_element_type=jnp.float32
            )
            probs = jnp.where(allowed[None], jnp.exp(scores - log_total[:, :, None]), 0.0)
            grad_probs = jnp.einsum(
                "qhd,khd->hqk", grad_attn, value_heads, preferred_element_type=jnp.float32
            )
            grad_scores = (probs * (grad_probs - delta[:, :, None])).astype(jnp.bfloat16)
            return (key_heads, probs, grad_scores)

        key_blocks = (
            key_all.reshape(block_count, key_block, local_cols),
            value_all.reshape(block_count, key_block, local_cols),
            jnp.arange(block_count, dtype=jnp.int32) * key_block,
        )
        zero_query = jnp.zeros((tok_rows, head_count, head_size), jnp.float32)

        def grad_block(grad_query, packed):
            key_heads, probs, grad_scores = block_terms(packed[0], packed[1], packed[2])
            grad_value = jnp.einsum(
                "hqk,qhd->khd",
                probs.astype(jnp.bfloat16),
                grad_attn,
                preferred_element_type=jnp.float32,
            )
            grad_query = grad_query + jnp.einsum(
                "hqk,khd->qhd", grad_scores, key_heads, preferred_element_type=jnp.float32
            )
            grad_key = jnp.einsum(
                "hqk,qhd->khd", grad_scores, query_heads, preferred_element_type=jnp.float32
            )
            return (
                grad_query,
                (
                    grad_key.reshape(key_block, local_cols),
                    grad_value.reshape(key_block, local_cols),
                ),
            )

        grad_query, (key_terms, value_terms) = lax.scan(grad_block, zero_query, key_blocks)
        key_grad, value_grad = (
            lax.psum_scatter(
                key_terms.reshape(stream, local_cols).astype(jnp.bfloat16),
                "ctx",
                scatter_dimension=0,
                tiled=True,
            ).astype(jnp.float32),
            lax.psum_scatter(
                value_terms.reshape(stream, local_cols).astype(jnp.bfloat16),
                "ctx",
                scatter_dimension=0,
                tiled=True,
            ).astype(jnp.float32),
        )
        grad_query_raw = (
            (grad_query * query_scale).astype(jnp.bfloat16).reshape(tok_rows, local_cols)
        )
        scale_part = jnp.sum(grad_query * query_raw, axis=(0, 1))
        grad_cols = jnp.concatenate(
            [grad_query_raw, key_grad.astype(jnp.bfloat16), value_grad.astype(jnp.bfloat16)], axis=1
        )
        grad_qkv = contract_rows(normed_one, grad_cols)
        grad_normed_one, scale_total = (
            lax.psum(contract_cols(grad_cols, w_qkv).astype(jnp.bfloat16), "tp").astype(
                jnp.float32
            ),
            lax.psum(scale_part.astype(jnp.bfloat16), "tp").astype(jnp.float32),
        )
        scale_sum = scale_sum + scale_total
        grad_gain_one = jnp.sum(grad_normed_one * stream_in * scale_one, axis=0)
        weighted_one = grad_normed_one * gain_one
        input_grads.append(
            grad_hidden
            + scale_one * weighted_one
            - stream_in * scale_one**3 * jnp.mean(weighted_one * stream_in, axis=-1, keepdims=True)
        )
        grads = (
            grad_qkv[:, :local_cols],
            grad_qkv[:, local_cols : 2 * local_cols],
            grad_qkv[:, 2 * local_cols :],
            grad_up,
            grad_gain_one,
            grad_gain_two,
            grad_out_proj,
            grad_down,
        )
        shares = (
            lax.psum_scatter(
                grads[0].astype(jnp.bfloat16), "ctx", scatter_dimension=0, tiled=True
            ).astype(jnp.float32),
            lax.psum_scatter(
                grads[1].astype(jnp.bfloat16), "ctx", scatter_dimension=0, tiled=True
            ).astype(jnp.float32),
            lax.psum_scatter(
                grads[2].astype(jnp.bfloat16), "ctx", scatter_dimension=0, tiled=True
            ).astype(jnp.float32),
            lax.psum_scatter(
                grads[3].astype(jnp.bfloat16), "ctx", scatter_dimension=0, tiled=True
            ).astype(jnp.float32),
            lax.psum_scatter(
                grads[4].astype(jnp.bfloat16), "ctx", scatter_dimension=0, tiled=True
            ).astype(jnp.float32),
            lax.psum_scatter(
                grads[5].astype(jnp.bfloat16), "ctx", scatter_dimension=0, tiled=True
            ).astype(jnp.float32),
            lax.psum_scatter(
                grads[6].astype(jnp.bfloat16), "ctx", scatter_dimension=1, tiled=True
            ).astype(jnp.float32),
            lax.psum_scatter(
                grads[7].astype(jnp.bfloat16), "ctx", scatter_dimension=1, tiled=True
            ).astype(jnp.float32),
        )
        local_sums = (
            shares
            if local_sums is None
            else tuple((total + extra for total, extra in zip(local_sums, shares)))
        )
    scale_grad = lax.psum(scale_sum, "ctx")
    return (
        jnp.stack(outputs),
        jnp.stack(input_grads),
        local_sums[0],
        local_sums[1],
        local_sums[2],
        local_sums[6],
        local_sums[3],
        local_sums[7],
        local_sums[4],
        local_sums[5],
        scale_grad,
    )


def solution(mesh):
    in_specs = (
        P(None, "ctx", None),
        P(None, "ctx", None),
        P(),
        P("ctx", "tp"),
        P("ctx", "tp"),
        P("ctx", "tp"),
        P("tp", "ctx"),
        P("ctx", "tp"),
        P("tp", "ctx"),
        P("ctx"),
        P("ctx"),
        P(),
    )
    out_specs = (
        P(None, "ctx", None),
        P(None, "ctx", None),
        P("ctx", "tp"),
        P("ctx", "tp"),
        P("ctx", "tp"),
        P("tp", "ctx"),
        P("ctx", "tp"),
        P("tp", "ctx"),
        P("ctx"),
        P("ctx"),
        P(),
    )

    def run(*arrays):
        body = stream_per_group if fits(arrays, mesh) else per_device
        return jax.shard_map(
            body, mesh=mesh, in_specs=in_specs, out_specs=out_specs, check_vma=False
        )(*arrays)

    return run
```

```python
import functools
import math

import jax
import jax.numpy as jnp
from jax import lax
from jax.experimental import pallas as pl
from jax.experimental.pallas import tpu as pltpu
from jax.sharding import PartitionSpec as P

EPSILON = 1e-06
MASKED = -1e30
LANES = 128
WIDE = 512
BF = jnp.bfloat16
F32 = jnp.float32
SPARE_VMEM = 12 * 1024 * 1024


def call(kernel, out_shape, kinds, scratch=(), flops=0, moved=0, aliases=None):
    vmem = pl.BlockSpec(memory_space=pltpu.VMEM)
    smem = pl.BlockSpec(memory_space=pltpu.SMEM)
    hbm = pl.BlockSpec(memory_space=pl.ANY)
    room = sum(
        math.prod(ref.shape) * jnp.dtype(ref.dtype).itemsize
        for ref in scratch
        if ref.memory_space == pltpu.VMEM
    )
    return pl.pallas_call(
        kernel,
        out_shape=out_shape,
        in_specs=[{"s": smem, "v": vmem, "h": hbm}[kind] for kind in kinds],
        out_specs=jax.tree.map(lambda _: vmem, out_shape),
        scratch_shapes=list(scratch),
        input_output_aliases=aliases or {},
        compiler_params=pltpu.CompilerParams(vmem_limit_bytes=room + SPARE_VMEM),
        cost_estimate=pl.CostEstimate(
            flops=int(flops), transcendentals=0, bytes_accessed=int(moved)
        ),
    )


def struct(shape, dtype):
    return jax.ShapeDtypeStruct(tuple(shape), dtype)


def nn(a, b):
    return jnp.dot(a, b, preferred_element_type=F32)


def nt(a, b):
    return lax.dot_general(a, b, (((1,), (1,)), ((), ())), preferred_element_type=F32)


def tn(a, b):
    return lax.dot_general(a, b, (((0,), (0,)), ((), ())), preferred_element_type=F32)


def at(start, size, step=None):
    return pl.ds(pl.multiple_of(start, step or size), size)


def inverse_rms(values):
    return lax.rsqrt(jnp.mean(values * values, axis=-1, keepdims=True) + EPSILON)


def split_kernel(ids, whole, *out):
    z, c = ids[0], ids[2]
    half = out[0].shape[0]
    for kz in range(len(out)):
        out[kz][...] = whole[z ^ kz, at(c * half, half), :]


def split(ids, whole):
    groups, rows, width = whole.shape
    return call(
        split_kernel,
        (struct((rows // 2, width), whole.dtype),) * groups,
        "sv",
        moved=whole.size * 4,
    )(ids, whole)


def assemble_kernel(ids, own, other, out):
    groups, half, _ = own.shape
    c = ids[2]
    for kz in range(groups):
        out[ids[0] ^ kz, at(c * half, half), :] = own[kz].astype(out.dtype)
        out[ids[0] ^ kz, at((1 - c) * half, half), :] = other[kz].astype(out.dtype)


def assemble(ids, own, other, dtype):
    groups, half, width = own.shape
    return call(
        assemble_kernel, struct((groups, 2 * half, width), dtype), "svv", moved=own.size * 12
    )(ids, own, other)


def place_kernel(groups, ids, *refs):
    own, other, out = refs[:groups], refs[groups : 2 * groups], refs[2 * groups]
    half = own[0].shape[0]
    z, c = ids[0], ids[2]
    for kz in range(groups):
        out[z ^ kz, at(c * half, half), :] = own[kz][...].astype(out.dtype)
        out[z ^ kz, at((1 - c) * half, half), :] = other[kz][...].astype(out.dtype)


def pack_kernel(mine, ids, query, key, value, gains, *refs):
    out, tmp = refs[:-1], refs[-1]
    rows = query.shape[0]
    rest = jnp.concatenate([gains[...], jnp.zeros((rows, WIDE - 3 * mine - 2), BF)], axis=1)
    for k in range(len(out)):
        cols = slice(k * mine, (k + 1) * mine)
        tmp[k] = jnp.concatenate([query[:, cols], key[:, cols], value[:, cols], rest], axis=1)
    for kj in range(len(out)):
        out[kj][...] = tmp[ids[1] ^ kj]


def stack_kernel(up, out_t, down_t, out):
    cols = up.shape[1]
    for g in range(out.shape[0]):
        for n, part in enumerate((up, out_t, down_t)):
            out[g, :, n * cols : (n + 1) * cols] = part[...]


def spread_kernel(heads, size, ids, pieces, w, w_t, gains, rows_ref):
    groups, members, rows, _ = pieces.shape
    for kz in range(groups):
        for kj in range(members):
            where = at((kz * members + (ids[1] ^ kj)) * rows, rows, 16)
            rows_ref[where, :] = pieces[kz, kj]
    block = rows_ref[...]
    zeros = jnp.zeros((block.shape[0], LANES - size), BF)
    for h in range(3 * heads):
        w[:, h * LANES : (h + 1) * LANES] = jnp.concatenate(
            [block[:, h * size : (h + 1) * size], zeros], axis=1
        )
    w_t[...] = w[...].T
    first = 3 * heads * size - (WIDE - LANES)
    gains[...] = block[:, WIDE - LANES :].astype(F32).T[first : first + 8, :]


def order_kernel(ids, *refs):
    pieces, out = refs[:-3], refs[-3:]
    groups, rows, _ = pieces[0].shape
    members, cols = len(pieces), out[0].shape[1]
    for kj in range(members):
        for kz in range(groups):
            where = at((kz * members + (ids[1] ^ kj)) * rows, rows, 16)
            for n in range(3):
                out[n][where, :] = pieces[kj][kz, :, n * cols : (n + 1) * cols]


def project_kernel(members, step, ids, *refs):
    pieces = refs[: 2 * members]
    w, gain, scale, proj, normed = refs[2 * members :]
    groups, half, _ = pieces[0].shape
    z, j, c = ids[0], ids[1], ids[2]
    for kj in range(members):
        for kc in range(2):
            for kz in range(groups):
                base = (z ^ kz) * (members * 2) + (j ^ kj) * 2 + (c ^ kc)
                normed[at(base * half, half), :] = pieces[kc * members + kj][kz]

    def block(n, _):
        rows = at(n * step, step)
        x = normed[rows, :].astype(F32)
        xn = (x * inverse_rms(x) * gain[0:1, :]).astype(BF)
        normed[rows, :] = xn
        proj[rows, :] = (nn(xn, w[...]) * scale[...]).astype(BF)
        return 0

    lax.fori_loop(0, normed.shape[0] // step, block, 0)


def doc_bounds(lengths, z, place):
    start, begin, end = jnp.int32(0), jnp.int32(0), jnp.int32(0)
    for d in range(lengths.shape[1]):
        stop = start + lengths[z, d]
        inside = start <= place
        begin = jnp.where(inside, start, begin)
        end = jnp.where(inside, stop, end)
        start = stop
    return begin, end


def doc_starts(lengths, z, stream):
    place = lax.broadcasted_iota(jnp.int32, (8, stream), 1)
    start, row = jnp.int32(0), jnp.zeros((8, stream), jnp.int32)
    for d in range(lengths.shape[1]):
        row = jnp.where(place >= start, start, row)
        start = start + lengths[z, d]
    return row


def attend_kernel(heads, size, members, bq, bk, ids, lengths, proj, *refs):
    outs, (kept, sent, vt, doc) = refs[:members], refs[members:]
    stream = proj.shape[0]
    z, j = ids[0], ids[1]
    doc[...] = doc_starts(lengths, z, stream)
    for h in range(heads):
        vt[h] = proj[:, (2 * heads + h) * LANES : (2 * heads + h + 1) * LANES].T

    def one_query_block(qb, _):
        rows = at(qb * bq, bq)
        qpos = qb * bq + lax.broadcasted_iota(jnp.int32, (1, bq), 1)
        queries = [proj[rows, h * LANES : (h + 1) * LANES] for h in range(heads)]

        def one_key_block(kb, carry):
            keys = at(kb * bk, bk)
            kpos = kb * bk + lax.broadcasted_iota(jnp.int32, (bk, bq), 0)
            allowed = (kpos <= qpos) & (kpos >= doc[0:1, rows])
            new = []
            for h in range(heads):
                top, total, acc = carry[h]
                k = proj[keys, (heads + h) * LANES : (heads + h + 1) * LANES]
                s = jnp.where(allowed, nt(k, queries[h]), MASKED)
                top2 = jnp.maximum(top, jnp.max(s, axis=0, keepdims=True))
                p = jnp.exp(s - top2)
                alpha = jnp.exp(top - top2)
                total = total * alpha + jnp.sum(p, axis=0, keepdims=True)
                acc = acc * alpha + nn(vt[h, :, keys], p.astype(BF))
                new.append((top2, total, acc))
            return tuple(new)

        zero = (
            jnp.full((1, bq), MASKED, F32),
            jnp.zeros((1, bq), F32),
            jnp.zeros((LANES, bq), F32),
        )
        begin, _ = doc_bounds(lengths, z, qb * bq)
        end = (qb * bq + bq + bk - 1) // bk
        carry = lax.fori_loop(begin // bk, end, one_key_block, (zero,) * heads)
        for h in range(heads):
            top, total, acc = carry[h]
            o = acc / total
            kept[h, :LANES, rows] = o
            kept[h, LANES:, rows] = jnp.broadcast_to(top + jnp.log(total), (8, bq))
            low = o[:size].astype(BF)
            for part in range(bq // LANES):
                block = qb * (bq // LANES) + part
                lanes = at(block // members * LANES, LANES)
                sent[(block % members) ^ j, h * size : (h + 1) * size, lanes] = low[
                    :, part * LANES : (part + 1) * LANES
                ]
        return 0

    lax.fori_loop(0, stream // bq, one_query_block, 0)
    for kj in range(members):
        outs[kj][...] = sent[kj]


def store_weights(heads, size, count, scale_sum, full, out):
    rows = out.shape[0] // count
    pad = WIDE - 3 * heads * size
    s = scale_sum[:size, :pad]
    high = s.astype(BF)
    rest = (s - high.astype(F32)).astype(BF)
    lane = lax.broadcasted_iota(jnp.int32, (size, pad), 1)
    tail = jnp.where(lane == 0, high, jnp.where(lane == 1, rest, jnp.zeros_like(rest)))
    tail = [tail, jnp.zeros((rows - size, pad), BF)] if rows > size else [tail]
    tail = jnp.concatenate(tail, axis=0)
    for n in range(count):
        block = full[n * rows : (n + 1) * rows, :].astype(BF)
        out[n * rows : (n + 1) * rows, :] = jnp.concatenate(
            [block[:, h * LANES : h * LANES + size] for h in range(3 * heads)] + [tail], axis=1
        )


def attend_back_kernel(heads, size, members, bq, bk, ids, lengths, proj, kept, scale, w, normed, *refs):
    pieces = refs[:members]
    grads, there = refs[members : members + 2]
    weights, refs = refs[members + 2 : -9], refs[-9:]
    dot_, do_, kt, dqt, delta, doc, rows_ref, full, padless = refs
    stream = proj.shape[0]
    groups = pieces[0].shape[1] // LANES
    z, j = ids[0], ids[1]
    doc[...] = doc_starts(lengths, z, stream)
    for h in range(heads):
        kt[h] = proj[:, (heads + h) * LANES : (heads + h + 1) * LANES].T
        dot_[h, size:, :] = jnp.zeros((LANES - size, stream), BF)
        for kj in range(members):
            for g in range(groups):
                lanes = at((g * members + (j ^ kj)) * LANES, LANES)
                dot_[h, :size, lanes] = pieces[kj][
                    h * size : (h + 1) * size, g * LANES : (g + 1) * LANES
                ]
        do_[h] = dot_[h].T
        delta[h] = jnp.broadcast_to(
            jnp.sum(dot_[h].astype(F32) * kept[h, :LANES, :], axis=0, keepdims=True), (8, stream)
        )
        dqt[h] = jnp.zeros((LANES, stream), F32)

    def one_key_block(kb, _):
        keys = at(kb * bk, bk)
        kpos = kb * bk + lax.broadcasted_iota(jnp.int32, (bk, bq), 0)
        ks = [proj[keys, (heads + h) * LANES : (heads + h + 1) * LANES] for h in range(heads)]
        vs = [
            proj[keys, (2 * heads + h) * LANES : (2 * heads + h + 1) * LANES] for h in range(heads)
        ]

        def one_query_block(qb, carry):
            rows = at(qb * bq, bq)
            qpos = qb * bq + lax.broadcasted_iota(jnp.int32, (1, bq), 1)
            allowed = (kpos <= qpos) & (kpos >= doc[0:1, rows])
            new = []
            for h in range(heads):
                dk, dv = carry[h]
                q = proj[rows, h * LANES : (h + 1) * LANES]
                p = jnp.exp(nt(ks[h], q) - kept[h, LANES : LANES + 1, rows])
                p = jnp.where(allowed, p, 0.0)
                dp = nn(vs[h], dot_[h, :, rows])
                ds = (p * (dp - delta[h, 0:1, rows])).astype(BF)
                dv = dv + nn(p.astype(BF), do_[h, rows, :])
                dk = dk + nn(ds, q)
                dqt[h, :, rows] += nn(kt[h, :, keys], ds)
                new.append((dk, dv))
            return tuple(new)

        _, final = doc_bounds(lengths, z, kb * bk + bk - 1)
        zero = jnp.zeros((bk, LANES), F32)
        carry = lax.fori_loop(
            kb * bk // bq, (final + bq - 1) // bq, one_query_block, ((zero, zero),) * heads
        )
        for h in range(heads):
            for n in range(2):
                cols = ((n + 1) * heads + h) * LANES
                grads[keys, cols : cols + LANES] = carry[h][n].astype(BF)
        return 0

    lax.fori_loop(0, stream // bk, one_key_block, 0)
    total = jnp.zeros((1, LANES), F32)
    for h in range(heads):
        dq = dqt[h].T
        q = proj[:, h * LANES : (h + 1) * LANES].astype(F32)
        total = total + jnp.sum(dq * q, axis=0, keepdims=True)
        grads[:, h * LANES : (h + 1) * LANES] = (dq * scale[...]).astype(BF)
    _, _, half, width = there.shape

    def one_member(kj, _):
        y = nn(input_rows(ids, grads, rows_ref, kj, 1, members, half), w[...])
        there[kj] = y.reshape(groups, half, width).astype(BF)
        return 0

    lax.fori_loop(0, members, one_member, 0)
    total = jnp.broadcast_to(total / scale[...], (LANES, LANES)).T
    full[...] = tn(normed[...], grads[...])
    store_weights(heads, size, groups * members, total, full, padless)
    rows = weights[0].shape[0]
    for kz in range(groups):
        weights[kz][...] = padless[at((z ^ kz) * rows, rows, 16), :]


def out_kernel(ids, *refs):
    pieces, (w, ob_t, part) = refs[:-3], refs[-3:]
    mine = pieces[0].shape[0]
    for kj in range(len(pieces)):
        ob_t[at((ids[1] ^ kj) * mine, mine, 16), :] = pieces[kj][...]
    part[...] = nt(ob_t[...].T, w[...]).astype(BF)


def mlp_kernel(groups, ids, *refs):
    x_own, x_other = refs[0], refs[1]
    g_own, g_other, attn, attn_other, up, down, gains = refs[2:9]
    hidden, normed, act, grad_up, cot, part, back = refs[9:]
    half = x_own.shape[1]
    z, c = ids[0], ids[2]
    for kz in range(groups):
        for kc in range(2):
            rows = at((z ^ kz) * (2 * half) + (c ^ kc) * half, half)
            hidden[rows, :] = (x_other if kc else x_own)[kz].astype(F32) + (
                attn[rows, :].astype(F32) + attn_other[rows, :].astype(F32)
            )
            cot[rows, :] = (g_other if kc else g_own)[kz]
    step = hidden.shape[0] // 2

    def block(n, _):
        rows = at(n * step, step)
        h = hidden[rows, :]
        xn = (h * inverse_rms(h) * gains[1:2, :]).astype(BF)
        u = nn(xn, up[...])
        sigma = jax.nn.sigmoid(u)
        a = (u * sigma).astype(BF)
        da = nn(cot[rows, :], down[...])
        du = (da * sigma * (1.0 + u * (1.0 - sigma))).astype(BF)
        part[rows, :] = nt(a, down[...]).astype(BF)
        back[rows, :] = nt(du, up[...]).astype(BF)
        normed[rows, :] = xn
        act[rows, :] = a
        grad_up[rows, :] = du
        return 0

    lax.fori_loop(0, 2, block, 0)


def hidden_kernel(groups, members, ids, *refs):
    hidden, cot, part, part_other, back, back_other, w, gains = refs[:8]
    low, dh_half = refs[8:10]
    pieces, out = refs[10 : 10 + members], refs[10 + members : 10 + members + groups]
    dh, lay, do_t = refs[10 + members + groups :]
    rows_all = hidden.shape[0]
    half = rows_all // groups // 2
    mine = pieces[0].shape[0]
    z, j, c = ids[0], ids[1], ids[2]
    step = rows_all // groups

    def block(n, _):
        rows = at(n * step, step)
        h = hidden[rows, :]
        scale = inverse_rms(h)
        grad = back[rows, :].astype(F32) + back_other[rows, :].astype(F32)
        weighted = grad * gains[1:2, :]
        d = (
            cot[rows, :].astype(F32)
            + scale * weighted
            - h * scale**3 * jnp.mean(weighted * h, axis=-1, keepdims=True)
        )
        dh[rows, :] = d
        low[rows, :] = d.astype(BF)
        lay[rows, :] = (
            h + (part[rows, :].astype(F32) + part_other[rows, :].astype(F32))
        ).astype(BF)
        return 0

    lax.fori_loop(0, groups, block, 0)
    do_t[...] = nn(low[...], w[...]).T.astype(BF)
    for kj in range(members):
        pieces[kj][...] = do_t[at((j ^ kj) * mine, mine, 16), :]
    for g in range(groups):
        out[g][...] = lay[at((z ^ g) * 2 * half + c * half, half), :]
        dh_half[g] = dh[at(g * 2 * half + c * half, half), :]


def by_member(ids, full, out, first=0):
    groups, rows, _ = out[0].shape
    for kj in range(len(out)):
        for g in range(groups):
            where = at((g * len(out) + (ids[1] ^ kj)) * rows, rows, 16)
            out[kj][g, :, first : first + full.shape[1]] = full[where, :]


def feed_weights_kernel(ids, normed, grad_up, cot, act, *refs):
    out, full = refs[:-1], refs[-1]
    full[...] = tn(normed[...], grad_up[...]).astype(BF)
    by_member(ids, full, out)
    full[...] = tn(cot[...], act[...]).astype(BF)
    by_member(ids, full, out, full.shape[1])


def out_weights_kernel(ids, low, ob_t, *refs):
    out, full = refs[:-1], refs[-1]
    full[...] = tn(low[...], ob_t[...].T).astype(BF)
    by_member(ids, full, out)


def sum_members_kernel(*refs):
    total = refs[0][...].astype(F32)
    for part in refs[1:-1]:
        total = total + part[...].astype(F32)
    refs[-1][...] = total.astype(BF)


def sum_split_kernel(members, ids, *refs):
    parts, out, tmp = refs[:members], refs[members:-1], refs[-1]
    total = parts[0][...].astype(F32)
    for part in parts[1:]:
        total = total + part[...].astype(F32)
    tmp[...] = total.astype(BF)
    for kz in range(len(out)):
        out[kz][...] = tmp[ids[0] ^ kz]


def rows_kernel(groups, parts, up, *refs):
    outs, (grad_up, grad_down, grad_out, gain) = refs[:groups], refs[groups:]
    cols = up.shape[1]
    total = parts[0].astype(F32)
    for g in range(1, parts.shape[0]):
        total = total + parts[g].astype(F32)
    grad_up[...] = total[:, :cols]
    grad_down[...] = total[:, cols:]
    term = jnp.sum(total[:, :cols] * up[...].astype(F32), axis=1, keepdims=True)
    gain[...] = jnp.broadcast_to(term, gain.shape)
    total = outs[0][...].astype(F32)
    for part in outs[1:]:
        total = total + part[...].astype(F32)
    grad_out[...] = total


def input_rows(ids, grads, rows_ref, kj, which, members, half):
    for g in range(rows_ref.shape[0] // half):
        base = (g * members + (ids[1] ^ kj)) * 2 + (ids[2] ^ which)
        rows_ref[g * half : (g + 1) * half, :] = grads[at(base * half, half), :]
    return rows_ref[...]


def input_here_kernel(ids, grads, w, other, *refs):
    out, rows_ref = refs[:-1], refs[-1]
    members, (groups, half, width) = len(out), out[0].shape
    for kj in reversed(range(members)):
        y = nn(input_rows(ids, grads, rows_ref, kj, 0, members, half), w[...])
        y = y + other[kj].reshape(groups * half, width).astype(F32)
        out[kj][...] = y.reshape(groups, half, width).astype(BF)


def qkv_sum_kernel(groups, ids, *refs):
    parts, out, tmp = refs[:groups], refs[groups:-1], refs[-1]
    total = parts[0][...].astype(F32)
    for part in parts[1:]:
        total = total + part[...].astype(F32)
    tmp[...] = total
    rows = out[0].shape[0]
    for kj in range(len(out)):
        out[kj][...] = tmp[at((ids[1] ^ kj) * rows, rows, 16), :].astype(BF)


def qkv_rows_kernel(mine, ids, *refs):
    members = len(refs) - 8
    pieces, (query, key, value, dq, dk, dv, small, tmp) = refs[:members], refs[members:]
    for kj in range(members):
        tmp[ids[1] ^ kj] = pieces[kj][...].astype(F32)
    gain = None
    for n, (w, dw) in enumerate(((query, dq), (key, dk), (value, dv))):
        dw[...] = jnp.concatenate(
            [tmp[k][:, n * mine : (n + 1) * mine] for k in range(members)], axis=1
        )
        term = jnp.sum(dw[...] * w[...].astype(F32), axis=1, keepdims=True)
        gain = term if gain is None else gain + term
    scale = tmp[0][:, 3 * mine : 3 * mine + 2]
    for k in range(1, members):
        scale = scale + tmp[k][:, 3 * mine : 3 * mine + 2]
    scale = jnp.sum(scale, axis=1, keepdims=True)
    lane = lax.broadcasted_iota(jnp.int32, small.shape, 1)
    small[...] = jnp.where(lane == 0, gain, jnp.where(lane == 1, scale, 0.0))


def tokens_kernel(groups, ids, *refs):
    x, dh, gains = refs[:3]
    parts, out = refs[3:-groups], refs[-groups:]
    z = ids[0]
    for kz in range(groups):
        grad = parts[0][z ^ kz].astype(F32)
        for part in parts[1:]:
            grad = grad + part[z ^ kz].astype(F32)
        xx = x[kz].astype(F32)
        scale = inverse_rms(xx)
        weighted = grad * gains[0:1, :]
        out[kz][...] = (
            dh[z ^ kz]
            + scale * weighted
            - xx * scale**3 * jnp.mean(weighted * xx, axis=-1, keepdims=True)
        ).astype(BF)


def stream_per_group(
    tokens,
    cotangent,
    doc_lengths,
    w_query,
    w_key,
    w_value,
    w_out,
    w_up,
    w_down,
    gain_attn,
    gain_mlp,
    query_scale,
):
    groups, tok_rows, width = tokens.shape
    count = lax.axis_size("ctx")
    members = count // groups
    size = query_scale.shape[0]
    local = w_query.shape[1]
    shard = width // count
    heads = local // size // members
    half = tok_rows // 2
    stream = tok_rows * count
    mine = heads * size
    rows = groups * tok_rows
    padded = 3 * heads * LANES
    me = lax.axis_index("ctx")
    ids = jnp.stack([me // members, me % members, lax.axis_index("tp")]).astype(jnp.int32)

    planes = [[g * members + k for k in range(members)] for g in range(groups)]
    lines = [[g * members + k for g in range(groups)] for k in range(members)]

    def across(a, mask):
        return lax.ppermute(a, "ctx", [(i, i ^ mask) for i in range(count)])

    def shift(a, by):
        pairs = [(i, i + by * members) for i in range(count)]
        return lax.ppermute(a, "ctx", [(i, k) for i, k in pairs if 0 <= k < count])

    def swap(a):
        return lax.ppermute(a, "tp", [(0, 1), (1, 0)])

    def to_groups(parts):
        return [parts[0]] + [across(parts[k], k * members) for k in range(1, groups)]

    def to_members(parts):
        return [parts[0]] + [across(parts[k], k) for k in range(1, members)]

    def exchange(a, teams):
        return lax.all_to_all(a, "ctx", 0, 0, axis_index_groups=teams, tiled=True)

    def tie(*values):
        return lax.optimization_barrier(values)

    def quarter(own, beside, above):
        cut = groups // 2
        return jnp.concatenate([across(above[:cut], 1), across(beside[cut:], 2)])

    packed = call(
        functools.partial(pack_kernel, mine),
        (struct((shard, WIDE), BF),) * members,
        "svvvv",
        scratch=[pltpu.VMEM((members, shard, WIDE), BF)],
        moved=shard * WIDE * members * 4,
    )(ids, w_query, w_key, w_value, jnp.stack([gain_attn, gain_mlp], axis=1))
    own = jnp.stack(to_groups(split(ids, tokens)))

    shards = call(
        stack_kernel,
        struct((groups, shard, 3 * local), BF),
        "vvv",
        moved=groups * shard * local * 8,
    )(w_up, w_out.T, w_down.T)
    own, packed, shards = tie(own, packed, shards)
    shards = exchange(shards, lines)
    cols = to_members(packed)
    late, cols = tie(own, cols)
    pieces = to_members([own] * (members - 1) + [late])
    pieces, cols, shards = tie(pieces, jnp.stack(cols), shards)
    cols = jnp.concatenate([cols] * groups)

    cols = exchange(cols, lines).reshape(groups, members, shard, WIDE)
    others = [swap(piece) for piece in pieces]
    if members == 4:
        beside, above = across(shards, 1), across(shards, 2)
        cols, others, beside, above = tie(cols, others, beside, above)
        shards = [shards, beside, above, quarter(shards, beside, above)]
    else:
        cols, others, shards = tie(cols, others, to_members([shards] * members))
    pieces = pieces + others
    g_parts, cols = tie(split(ids, cotangent), cols)
    g_own = to_groups(g_parts)
    w_qkv, w_qkv_t, gains = call(
        functools.partial(spread_kernel, heads, size),
        (struct((width, padded), BF), struct((padded, width), BF), struct((8, width), F32)),
        "sv",
        scratch=[pltpu.VMEM((width, WIDE), BF)],
        moved=width * padded * 6,
    )(ids, cols)
    scale_row = jnp.pad(query_scale, (0, LANES - size), constant_values=1.0)[None, :]
    scale_all = jnp.concatenate(
        [scale_row] * heads + [jnp.ones((1, 2 * heads * LANES), F32)], axis=1
    )

    proj, normed = call(
        functools.partial(project_kernel, members, 512),
        (struct((stream, padded), BF), struct((stream, width), BF)),
        "s" + "v" * (2 * members + 3),
        flops=2 * stream * width * padded,
        moved=stream * width * 4,
    )(ids, *pieces, w_qkv, gains, scale_all)

    bq, bk = 512, 512
    *sent, kept = call(
        functools.partial(attend_kernel, heads, size, members, bq, bk),
        (struct((mine, rows), BF),) * members + (struct((heads, LANES + 8, stream), F32),),
        "ssv",
        scratch=[
            pltpu.VMEM((members, mine, rows), BF),
            pltpu.VMEM((heads, LANES, stream), BF),
            pltpu.VMEM((8, stream), jnp.int32),
        ],
        flops=2 * stream * stream * LANES * heads,
        moved=stream * LANES * heads * 10,
    )(ids, doc_lengths, proj)
    sent, shards, g_own = tie(sent, shards, g_own)
    arrived = to_members(sent)
    g_own = jnp.stack(g_own)
    g_other = swap(g_own)
    up_full, out_t, down_t = call(
        order_kernel,
        (struct((width, local), BF),) * 3,
        "s" + "v" * members,
        moved=width * local * 12,
    )(ids, *shards)

    ob_t, attn = call(
        out_kernel,
        (struct((local, rows), BF), struct((rows, width), BF)),
        "s" + "v" * (members + 1),
        flops=2 * rows * local * width,
        moved=local * width * 4,
    )(ids, *arrived, out_t)
    hidden, normed_two, activated, grad_up_raw, cot, part, back = call(
        functools.partial(mlp_kernel, groups),
        (
            struct((rows, width), F32),
            struct((rows, width), BF),
            struct((rows, local), BF),
            struct((rows, local), BF),
            struct((rows, width), BF),
            struct((rows, width), BF),
            struct((rows, width), BF),
        ),
        "s" + "v" * 9,
        flops=8 * rows * local * width,
        moved=local * width * 12,
    )(ids, pieces[0], pieces[members], g_own, g_other, attn, swap(attn), up_full, down_t, gains)
    back_other, part_other = swap(back), swap(part)
    feed_grads = call(
        feed_weights_kernel,
        (struct((groups, shard, 2 * local), BF),) * members,
        "svvvv",
        scratch=[pltpu.VMEM((width, local), BF)],
        flops=4 * rows * local * width,
        moved=local * width * 8,
    )(ids, normed_two, grad_up_raw, cot, activated)
    back_other, part_other, feed_grads = tie(back_other, part_other, feed_grads)
    hidden_low, dh_half, *results = call(
        functools.partial(hidden_kernel, groups, members),
        (struct((rows, width), BF), struct((groups, half, width), F32))
        + (struct((mine, rows), BF),) * members
        + (struct((half, width), BF),) * groups,
        "s" + "v" * 8,
        scratch=[
            pltpu.VMEM((rows, width), F32),
            pltpu.VMEM((rows, width), BF),
            pltpu.VMEM((local, rows), BF),
        ],
        flops=2 * rows * local * width,
        moved=local * width * 12,
    )(ids, hidden, cot, part, part_other, back, back_other, out_t, gains)
    do_pieces, out_parts = to_members(results[:members]), results[members:]
    out_grads = call(
        out_weights_kernel,
        (struct((groups, shard, local), BF),) * members,
        "svv",
        scratch=[pltpu.VMEM((width, local), BF)],
        flops=2 * rows * local * width,
        moved=local * width * 4,
    )(ids, hidden_low, ob_t)
    out_own = [across(part, members) if kz == 1 else part for kz, part in enumerate(out_parts)]
    do_pieces, out_grads, out_own, feed_grads = tie(do_pieces, out_grads, out_own, feed_grads)

    feed_grads = to_members(feed_grads)
    out_own = [
        across(part, kz * members) if kz > 1 else part for kz, part in enumerate(out_own)
    ]

    grads, there, *qkv_parts = call(
        functools.partial(attend_back_kernel, heads, size, members, bq, bk),
        (
            struct((stream, padded), BF),
            struct((members, groups, half, width), BF),
        )
        + (struct((width // groups, WIDE), BF),) * groups,
        "ssvvvvv" + "v" * members,
        scratch=[
            pltpu.VMEM((heads, LANES, stream), BF),
            pltpu.VMEM((heads, stream, LANES), BF),
            pltpu.VMEM((heads, LANES, stream), BF),
            pltpu.VMEM((heads, LANES, stream), F32),
            pltpu.VMEM((heads, 8, stream), F32),
            pltpu.VMEM((8, stream), jnp.int32),
            pltpu.VMEM((groups * half, padded), BF),
            pltpu.VMEM((width, padded), F32),
            pltpu.VMEM((width, WIDE), BF),
        ],
        flops=5 * stream * stream * LANES * heads,
        moved=stream * LANES * heads * 20,
    )(ids, doc_lengths, proj, kept, scale_row, w_qkv_t, normed, *do_pieces)
    there, grads, qkv_parts, feed_grads, out_own, out_grads = tie(
        there, grads, qkv_parts, feed_grads, out_own, out_grads
    )

    there = swap(there)
    out_own = jnp.stack(out_own)
    out_other = swap(out_own)
    here = call(
        input_here_kernel,
        (struct((groups, half, width), BF),) * members,
        "svvv",
        scratch=[pltpu.VMEM((groups * half, padded), BF)],
        flops=stream * width * padded,
        moved=stream * width * 2,
    )(ids, grads, w_qkv_t, there)
    qkv_parts = [
        across(part, members) if kz == 1 else part for kz, part in enumerate(qkv_parts)
    ]
    here, feed_grads, qkv_parts, out_own, out_other = tie(
        here, feed_grads, qkv_parts, out_own, out_other
    )
    layer_out = assemble(ids, out_own, out_other, BF)
    sums = to_members(here)
    qkv_parts = [
        across(part, kz * members) if kz > 1 else part for kz, part in enumerate(qkv_parts)
    ]
    feed_grads = call(
        sum_members_kernel,
        struct((groups, shard, 2 * local), BF),
        "v" * members,
        moved=groups * shard * local * 24,
    )(*feed_grads)
    sums, feed_grads, out_grads, qkv_parts, layer_out = tie(
        sums, feed_grads, out_grads, qkv_parts, layer_out
    )
    grad_x = call(
        functools.partial(tokens_kernel, groups),
        (struct((half, width), BF),) * groups,
        "svvv" + "v" * len(sums),
        moved=groups * half * width * 12,
    )(ids, pieces[0], dh_half, gains, *sums)
    grad_x, qkv_parts, feed_grads, out_grads = tie(grad_x, qkv_parts, feed_grads, out_grads)
    feed_grads = exchange(feed_grads, lines)
    gx_own = to_groups(grad_x)
    out_grads = to_members(out_grads)
    qkv_parts = call(
        functools.partial(qkv_sum_kernel, groups),
        (struct((shard, WIDE), BF),) * members,
        "s" + "v" * groups,
        scratch=[pltpu.VMEM((width // groups, WIDE), F32)],
        moved=width * WIDE * 4,
    )(ids, *qkv_parts)
    gx_own, qkv_parts, out_grads = tie(gx_own, qkv_parts, out_grads)
    qkv_parts = to_members(qkv_parts)
    out_grads = call(
        functools.partial(sum_split_kernel, members),
        (struct((shard, local), BF),) * groups,
        "s" + "v" * members,
        scratch=[pltpu.VMEM((groups, shard, local), BF)],
        moved=groups * shard * local * 12,
    )(ids, *out_grads)
    out_grads = to_groups(out_grads)
    gx_other = [swap(piece) for piece in gx_own]
    grad_up, grad_down, grad_out, gain_two = call(
        functools.partial(rows_kernel, groups),
        (struct((shard, local), F32),) * 3 + (struct((shard, LANES), F32),),
        "v" * (groups + 2),
        moved=shard * local * 36,
    )(feed_grads, w_up, *out_grads)
    grad_q, grad_k, grad_v, small = call(
        functools.partial(qkv_rows_kernel, mine),
        (struct((shard, local), F32),) * 3 + (struct((shard, LANES), F32),),
        "s" + "v" * (members + 3),
        scratch=[pltpu.VMEM((members, shard, WIDE), F32)],
        moved=shard * local * 24,
    )(ids, *qkv_parts, w_query, w_key, w_value)
    lane = lax.broadcasted_iota(jnp.int32, small.shape, 1)
    small = jnp.where(lane == 2, gain_two, small)
    small = small + swap(small)
    gx_other, small = tie(gx_other, small)
    grad_tokens = call(
        functools.partial(place_kernel, groups),
        struct((groups, tok_rows, width), F32),
        "s" + "v" * (2 * groups),
        moved=rows * width * 8,
    )(ids, *gx_own, *gx_other)
    return (
        layer_out,
        grad_tokens,
        grad_q,
        grad_k,
        grad_v,
        grad_out.T,
        grad_up,
        grad_down.T,
        small[:, 0] / gain_attn.astype(F32),
        small[:, 2] / gain_mlp.astype(F32),
        small[:size, 1],
    )


def fits(shapes, mesh):
    groups, stream, width = shapes[0].shape
    count, cores = mesh.shape["ctx"], mesh.shape["tp"]
    size = shapes[11].shape[0]
    if cores != 2 or count % groups:
        return False
    members = count // groups
    local_heads = shapes[3].shape[1] // cores // size
    return (
        groups & (groups - 1) == 0
        and members & (members - 1) == 0
        and members % 2 == 0
        and local_heads % members == 0
        and stream // count == LANES
        and stream % 512 == 0
        and size % 16 == 0
        and size <= LANES
        and size <= width // count
        and width // count % 16 == 0
        and 3 * local_heads // members * size + 2 <= WIDE
        and 3 * local_heads // members * size >= WIDE - LANES
        and width % (LANES * 2) == 0
    )


def segment_of(starts, positions):
    return jnp.sum((starts[None, :] <= positions[:, None]).astype(jnp.int32), axis=1)


def contract_rows(left, right):
    return lax.dot_general(
        left, right, (((0,), (0,)), ((), ())), preferred_element_type=jnp.float32
    )


def contract_cols(left, right):
    return lax.dot_general(
        left, right, (((1,), (1,)), ((), ())), preferred_element_type=jnp.float32
    )


def per_device(
    tokens,
    cotangent,
    doc_lengths,
    w_query,
    w_key,
    w_value,
    w_out,
    w_up,
    w_down,
    gain_attn,
    gain_mlp,
    query_scale,
):
    micro_count, tok_rows, model_width = tokens.shape
    head_size = query_scale.shape[0]
    local_cols = w_query.shape[1]
    head_count = local_cols // head_size
    stream = tok_rows * lax.axis_size("ctx")
    key_block = min(512, stream)
    block_count = stream // key_block
    positions = lax.axis_index("ctx") * tok_rows + jnp.arange(tok_rows, dtype=jnp.int32)
    local_sums = None
    scale_sum = jnp.zeros((head_size,), jnp.float32)
    outputs = []
    input_grads = []
    for micro_step in range(micro_count):
        gathered = (
            lax.all_gather(w_query, "ctx", axis=0, tiled=True),
            lax.all_gather(w_key, "ctx", axis=0, tiled=True),
            lax.all_gather(w_value, "ctx", axis=0, tiled=True),
            lax.all_gather(w_up, "ctx", axis=0, tiled=True),
            lax.all_gather(gain_attn, "ctx", axis=0, tiled=True),
            lax.all_gather(gain_mlp, "ctx", axis=0, tiled=True),
            lax.all_gather(w_out, "ctx", axis=1, tiled=True),
            lax.all_gather(w_down, "ctx", axis=1, tiled=True),
        )
        w_qkv = jnp.concatenate([gathered[0], gathered[1], gathered[2]], axis=1)
        up_full = gathered[3]
        gain_one = gathered[4].astype(jnp.float32)
        gain_two = gathered[5].astype(jnp.float32)
        out_full = gathered[6]
        down_full = gathered[7]
        lengths = doc_lengths[micro_step]
        starts = jnp.cumsum(lengths) - lengths
        query_seg = segment_of(starts, positions)
        stream_in = tokens[micro_step].astype(jnp.float32)
        scale_one = inverse_rms(stream_in)
        normed_one = (stream_in * scale_one * gain_one).astype(jnp.bfloat16)
        projected = jnp.dot(normed_one, w_qkv, preferred_element_type=jnp.float32)
        query_raw = projected[:, :local_cols].reshape(tok_rows, head_count, head_size)
        query_heads = (query_raw * query_scale).astype(jnp.bfloat16)
        key_local = projected[:, local_cols : 2 * local_cols].astype(jnp.bfloat16)
        value_local = projected[:, 2 * local_cols :].astype(jnp.bfloat16)
        row_top = jnp.full((head_count, tok_rows), MASKED, jnp.float32)
        key_piece = lax.all_gather(key_local, "ctx", axis=0, tiled=True)
        value_piece = lax.all_gather(value_local, "ctx", axis=0, tiled=True)
        length = key_piece.shape[0]
        key_pos = jnp.arange(length, dtype=jnp.int32)
        allowed = (key_pos[None, :] <= positions[:, None]) & (
            segment_of(starts, key_pos)[None, :] == query_seg[:, None]
        )
        scores = jnp.einsum(
            "qhd,khd->hqk",
            query_heads,
            key_piece.reshape(length, head_count, head_size),
            preferred_element_type=jnp.float32,
        )
        scores = jnp.where(allowed[None], scores, MASKED)
        new_top = jnp.maximum(row_top, jnp.max(scores, axis=-1))
        probs = jnp.where(allowed[None], jnp.exp(scores - new_top[:, :, None]), 0.0)
        row_sum = jnp.sum(probs, axis=-1)
        update = jnp.einsum(
            "hqk,khd->qhd",
            probs.astype(jnp.bfloat16),
            value_piece.reshape(length, head_count, head_size),
            preferred_element_type=jnp.float32,
        )
        weighted = update
        row_top, row_sum, weighted = (new_top, row_sum, weighted)
        attn_heads = weighted / jnp.transpose(row_sum)[:, :, None]
        log_total = row_top + jnp.log(row_sum)
        attn_low = attn_heads.reshape(tok_rows, local_cols).astype(jnp.bfloat16)
        attn_out = lax.psum(
            jnp.dot(attn_low, out_full, preferred_element_type=jnp.float32).astype(jnp.bfloat16),
            "tp",
        ).astype(jnp.float32)
        hidden = stream_in + attn_out
        scale_two = inverse_rms(hidden)
        normed_two = (hidden * scale_two * gain_two).astype(jnp.bfloat16)
        up_raw = jnp.dot(normed_two, up_full, preferred_element_type=jnp.float32)
        activated = jax.nn.silu(up_raw).astype(jnp.bfloat16)
        mlp_out = lax.psum(
            jnp.dot(activated, down_full, preferred_element_type=jnp.float32).astype(jnp.bfloat16),
            "tp",
        ).astype(jnp.float32)
        outputs.append((hidden + mlp_out).astype(jnp.bfloat16))
        grad_out = cotangent[micro_step]
        grad_down = contract_rows(activated, grad_out)
        grad_act = contract_cols(grad_out, down_full)
        sigma = jax.nn.sigmoid(up_raw)
        grad_up_raw = (grad_act * sigma * (1.0 + up_raw * (1.0 - sigma))).astype(jnp.bfloat16)
        grad_up = contract_rows(normed_two, grad_up_raw)
        grad_normed_two = lax.psum(
            contract_cols(grad_up_raw, up_full).astype(jnp.bfloat16), "tp"
        ).astype(jnp.float32)
        grad_gain_two = jnp.sum(grad_normed_two * hidden * scale_two, axis=0)
        weighted_two = grad_normed_two * gain_two
        grad_hidden = (
            grad_out.astype(jnp.float32)
            + scale_two * weighted_two
            - hidden * scale_two**3 * jnp.mean(weighted_two * hidden, axis=-1, keepdims=True)
        )
        hidden_low = grad_hidden.astype(jnp.bfloat16)
        grad_out_proj = contract_rows(attn_low, hidden_low)
        grad_attn = (
            contract_cols(hidden_low, out_full)
            .astype(jnp.bfloat16)
            .reshape(tok_rows, head_count, head_size)
        )
        delta = jnp.einsum("qhd,qhd->hq", grad_attn.astype(jnp.float32), attn_heads)
        key_all, value_all = (
            lax.all_gather(key_local, "ctx", axis=0, tiled=True),
            lax.all_gather(value_local, "ctx", axis=0, tiled=True),
        )

        def block_terms(key_piece, value_piece, offset):
            key_heads = key_piece.reshape(key_block, head_count, head_size)
            value_heads = value_piece.reshape(key_block, head_count, head_size)
            key_pos = offset + jnp.arange(key_block, dtype=jnp.int32)
            allowed = (key_pos[None, :] <= positions[:, None]) & (
                segment_of(starts, key_pos)[None, :] == query_seg[:, None]
            )
            scores = jnp.einsum(
                "qhd,khd->hqk", query_heads, key_heads, preferred_element_type=jnp.float32
            )
            probs = jnp.where(allowed[None], jnp.exp(scores - log_total[:, :, None]), 0.0)
            grad_probs = jnp.einsum(
                "qhd,khd->hqk", grad_attn, value_heads, preferred_element_type=jnp.float32
            )
            grad_scores = (probs * (grad_probs - delta[:, :, None])).astype(jnp.bfloat16)
            return (key_heads, probs, grad_scores)

        key_blocks = (
            key_all.reshape(block_count, key_block, local_cols),
            value_all.reshape(block_count, key_block, local_cols),
            jnp.arange(block_count, dtype=jnp.int32) * key_block,
        )
        zero_query = jnp.zeros((tok_rows, head_count, head_size), jnp.float32)

        def grad_block(grad_query, packed):
            key_heads, probs, grad_scores = block_terms(packed[0], packed[1], packed[2])
            grad_value = jnp.einsum(
                "hqk,qhd->khd",
                probs.astype(jnp.bfloat16),
                grad_attn,
                preferred_element_type=jnp.float32,
            )
            grad_query = grad_query + jnp.einsum(
                "hqk,khd->qhd", grad_scores, key_heads, preferred_element_type=jnp.float32
            )
            grad_key = jnp.einsum(
                "hqk,qhd->khd", grad_scores, query_heads, preferred_element_type=jnp.float32
            )
            return (
                grad_query,
                (
                    grad_key.reshape(key_block, local_cols),
                    grad_value.reshape(key_block, local_cols),
                ),
            )

        grad_query, (key_terms, value_terms) = lax.scan(grad_block, zero_query, key_blocks)
        key_grad, value_grad = (
            lax.psum_scatter(
                key_terms.reshape(stream, local_cols).astype(jnp.bfloat16),
                "ctx",
                scatter_dimension=0,
                tiled=True,
            ).astype(jnp.float32),
            lax.psum_scatter(
                value_terms.reshape(stream, local_cols).astype(jnp.bfloat16),
                "ctx",
                scatter_dimension=0,
                tiled=True,
            ).astype(jnp.float32),
        )
        grad_query_raw = (
            (grad_query * query_scale).astype(jnp.bfloat16).reshape(tok_rows, local_cols)
        )
        scale_part = jnp.sum(grad_query * query_raw, axis=(0, 1))
        grad_cols = jnp.concatenate(
            [grad_query_raw, key_grad.astype(jnp.bfloat16), value_grad.astype(jnp.bfloat16)], axis=1
        )
        grad_qkv = contract_rows(normed_one, grad_cols)
        grad_normed_one, scale_total = (
            lax.psum(contract_cols(grad_cols, w_qkv).astype(jnp.bfloat16), "tp").astype(
                jnp.float32
            ),
            lax.psum(scale_part.astype(jnp.bfloat16), "tp").astype(jnp.float32),
        )
        scale_sum = scale_sum + scale_total
        grad_gain_one = jnp.sum(grad_normed_one * stream_in * scale_one, axis=0)
        weighted_one = grad_normed_one * gain_one
        input_grads.append(
            grad_hidden
            + scale_one * weighted_one
            - stream_in * scale_one**3 * jnp.mean(weighted_one * stream_in, axis=-1, keepdims=True)
        )
        grads = (
            grad_qkv[:, :local_cols],
            grad_qkv[:, local_cols : 2 * local_cols],
            grad_qkv[:, 2 * local_cols :],
            grad_up,
            grad_gain_one,
            grad_gain_two,
            grad_out_proj,
            grad_down,
        )
        shares = (
            lax.psum_scatter(
                grads[0].astype(jnp.bfloat16), "ctx", scatter_dimension=0, tiled=True
            ).astype(jnp.float32),
            lax.psum_scatter(
                grads[1].astype(jnp.bfloat16), "ctx", scatter_dimension=0, tiled=True
            ).astype(jnp.float32),
            lax.psum_scatter(
                grads[2].astype(jnp.bfloat16), "ctx", scatter_dimension=0, tiled=True
            ).astype(jnp.float32),
            lax.psum_scatter(
                grads[3].astype(jnp.bfloat16), "ctx", scatter_dimension=0, tiled=True
            ).astype(jnp.float32),
            lax.psum_scatter(
                grads[4].astype(jnp.bfloat16), "ctx", scatter_dimension=0, tiled=True
            ).astype(jnp.float32),
            lax.psum_scatter(
                grads[5].astype(jnp.bfloat16), "ctx", scatter_dimension=0, tiled=True
            ).astype(jnp.float32),
            lax.psum_scatter(
                grads[6].astype(jnp.bfloat16), "ctx", scatter_dimension=1, tiled=True
            ).astype(jnp.float32),
            lax.psum_scatter(
                grads[7].astype(jnp.bfloat16), "ctx", scatter_dimension=1, tiled=True
            ).astype(jnp.float32),
        )
        local_sums = (
            shares
            if local_sums is None
            else tuple((total + extra for total, extra in zip(local_sums, shares)))
        )
    scale_grad = lax.psum(scale_sum, "ctx")
    return (
        jnp.stack(outputs),
        jnp.stack(input_grads),
        local_sums[0],
        local_sums[1],
        local_sums[2],
        local_sums[6],
        local_sums[3],
        local_sums[7],
        local_sums[4],
        local_sums[5],
        scale_grad,
    )


def solution(mesh):
    in_specs = (
        P(None, "ctx", None),
        P(None, "ctx", None),
        P(),
        P("ctx", "tp"),
        P("ctx", "tp"),
        P("ctx", "tp"),
        P("tp", "ctx"),
        P("ctx", "tp"),
        P("tp", "ctx"),
        P("ctx"),
        P("ctx"),
        P(),
    )
    out_specs = (
        P(None, "ctx", None),
        P(None, "ctx", None),
        P("ctx", "tp"),
        P("ctx", "tp"),
        P("ctx", "tp"),
        P("tp", "ctx"),
        P("ctx", "tp"),
        P("tp", "ctx"),
        P("ctx"),
        P("ctx"),
        P(),
    )

    def run(*arrays):
        body = stream_per_group if fits(arrays, mesh) else per_device
        return jax.shard_map(
            body, mesh=mesh, in_specs=in_specs, out_specs=out_specs, check_vma=False
        )(*arrays)

    return run
```

```python
import functools
import math

import jax
import jax.numpy as jnp
from jax import lax
from jax.experimental import pallas as pl
from jax.experimental.pallas import tpu as pltpu
from jax.sharding import PartitionSpec as P

EPSILON = 1e-06
MASKED = -1e30
LANES = 128
WIDE = 512
BF = jnp.bfloat16
F32 = jnp.float32
SPARE_VMEM = 12 * 1024 * 1024


def call(kernel, out_shape, kinds, scratch=(), flops=0, moved=0, aliases=None):
    vmem = pl.BlockSpec(memory_space=pltpu.VMEM)
    smem = pl.BlockSpec(memory_space=pltpu.SMEM)
    hbm = pl.BlockSpec(memory_space=pl.ANY)
    room = sum(
        math.prod(ref.shape) * jnp.dtype(ref.dtype).itemsize
        for ref in scratch
        if ref.memory_space == pltpu.VMEM
    )
    return pl.pallas_call(
        kernel,
        out_shape=out_shape,
        in_specs=[{"s": smem, "v": vmem, "h": hbm}[kind] for kind in kinds],
        out_specs=jax.tree.map(lambda _: vmem, out_shape),
        scratch_shapes=list(scratch),
        input_output_aliases=aliases or {},
        compiler_params=pltpu.CompilerParams(vmem_limit_bytes=room + SPARE_VMEM),
        cost_estimate=pl.CostEstimate(
            flops=int(flops), transcendentals=0, bytes_accessed=int(moved)
        ),
    )


def struct(shape, dtype):
    return jax.ShapeDtypeStruct(tuple(shape), dtype)


def nn(a, b):
    return jnp.dot(a, b, preferred_element_type=F32)


def nt(a, b):
    return lax.dot_general(a, b, (((1,), (1,)), ((), ())), preferred_element_type=F32)


def tn(a, b):
    return lax.dot_general(a, b, (((0,), (0,)), ((), ())), preferred_element_type=F32)


def at(start, size, step=None):
    return pl.ds(pl.multiple_of(start, step or size), size)


def inverse_rms(values):
    return lax.rsqrt(jnp.mean(values * values, axis=-1, keepdims=True) + EPSILON)


def split_kernel(ids, whole, *out):
    z, c = ids[0], ids[2]
    half = out[0].shape[0]
    for kz in range(len(out)):
        out[kz][...] = whole[z ^ kz, at(c * half, half), :]


def split(ids, whole):
    groups, rows, width = whole.shape
    return call(
        split_kernel,
        (struct((rows // 2, width), whole.dtype),) * groups,
        "sv",
        moved=whole.size * 4,
    )(ids, whole)


def assemble_kernel(ids, own, other, out):
    groups, half, _ = own.shape
    c = ids[2]
    for kz in range(groups):
        out[ids[0] ^ kz, at(c * half, half), :] = own[kz].astype(out.dtype)
        out[ids[0] ^ kz, at((1 - c) * half, half), :] = other[kz].astype(out.dtype)


def assemble(ids, own, other, dtype):
    groups, half, width = own.shape
    return call(
        assemble_kernel, struct((groups, 2 * half, width), dtype), "svv", moved=own.size * 12
    )(ids, own, other)


def place_kernel(groups, ids, *refs):
    own, other, out = refs[:groups], refs[groups : 2 * groups], refs[2 * groups]
    half = own[0].shape[0]
    z, c = ids[0], ids[2]
    for kz in range(groups):
        out[z ^ kz, at(c * half, half), :] = own[kz][...].astype(out.dtype)
        out[z ^ kz, at((1 - c) * half, half), :] = other[kz][...].astype(out.dtype)


def pack_kernel(mine, ids, query, key, value, gains, *refs):
    out, tmp = refs[:-1], refs[-1]
    rows = query.shape[0]
    rest = jnp.concatenate([gains[...], jnp.zeros((rows, WIDE - 3 * mine - 2), BF)], axis=1)
    for k in range(len(out)):
        cols = slice(k * mine, (k + 1) * mine)
        tmp[k] = jnp.concatenate([query[:, cols], key[:, cols], value[:, cols], rest], axis=1)
    for kj in range(len(out)):
        out[kj][...] = tmp[ids[1] ^ kj]


def stack_kernel(up, out_t, down_t, out):
    cols = up.shape[1]
    for g in range(out.shape[0]):
        for n, part in enumerate((up, out_t, down_t)):
            out[g, :, n * cols : (n + 1) * cols] = part[...]


def spread_kernel(heads, size, ids, pieces, w, w_t, gains, rows_ref):
    groups, members, rows, _ = pieces.shape
    for kz in range(groups):
        for kj in range(members):
            where = at((kz * members + (ids[1] ^ kj)) * rows, rows, 16)
            rows_ref[where, :] = pieces[kz, kj]
    block = rows_ref[...]
    zeros = jnp.zeros((block.shape[0], LANES - size), BF)
    for h in range(3 * heads):
        w[:, h * LANES : (h + 1) * LANES] = jnp.concatenate(
            [block[:, h * size : (h + 1) * size], zeros], axis=1
        )
    w_t[...] = w[...].T
    first = 3 * heads * size - (WIDE - LANES)
    gains[...] = block[:, WIDE - LANES :].astype(F32).T[first : first + 8, :]


def order_kernel(ids, *refs):
    pieces, out = refs[:-3], refs[-3:]
    groups, rows, _ = pieces[0].shape
    members, cols = len(pieces), out[0].shape[1]
    for kj in range(members):
        for kz in range(groups):
            where = at((kz * members + (ids[1] ^ kj)) * rows, rows, 16)
            for n in range(3):
                out[n][where, :] = pieces[kj][kz, :, n * cols : (n + 1) * cols]


def project_kernel(members, step, ids, *refs):
    pieces = refs[: 2 * members]
    w, gain, scale, proj, normed = refs[2 * members :]
    groups, half, _ = pieces[0].shape
    z, j, c = ids[0], ids[1], ids[2]
    for kj in range(members):
        for kc in range(2):
            for kz in range(groups):
                base = (z ^ kz) * (members * 2) + (j ^ kj) * 2 + (c ^ kc)
                normed[at(base * half, half), :] = pieces[kc * members + kj][kz]

    def block(n, _):
        rows = at(n * step, step)
        x = normed[rows, :].astype(F32)
        xn = (x * inverse_rms(x) * gain[0:1, :]).astype(BF)
        normed[rows, :] = xn
        proj[rows, :] = (nn(xn, w[...]) * scale[...]).astype(BF)
        return 0

    lax.fori_loop(0, normed.shape[0] // step, block, 0)


def doc_bounds(lengths, z, place):
    start, begin, end = jnp.int32(0), jnp.int32(0), jnp.int32(0)
    for d in range(lengths.shape[1]):
        stop = start + lengths[z, d]
        inside = start <= place
        begin = jnp.where(inside, start, begin)
        end = jnp.where(inside, stop, end)
        start = stop
    return begin, end


def doc_starts(lengths, z, stream):
    place = lax.broadcasted_iota(jnp.int32, (8, stream), 1)
    start, row = jnp.int32(0), jnp.zeros((8, stream), jnp.int32)
    for d in range(lengths.shape[1]):
        row = jnp.where(place >= start, start, row)
        start = start + lengths[z, d]
    return row


def attend_kernel(heads, size, members, bq, bk, ids, lengths, proj, *refs):
    outs, (kept, sent, vt, doc) = refs[:members], refs[members:]
    stream = proj.shape[0]
    z, j = ids[0], ids[1]
    doc[...] = doc_starts(lengths, z, stream)
    for h in range(heads):
        vt[h] = proj[:, (2 * heads + h) * LANES : (2 * heads + h + 1) * LANES].T

    def one_query_block(qb, _):
        rows = at(qb * bq, bq)
        qpos = qb * bq + lax.broadcasted_iota(jnp.int32, (1, bq), 1)
        queries = [proj[rows, h * LANES : (h + 1) * LANES] for h in range(heads)]

        def one_key_block(kb, carry):
            keys = at(kb * bk, bk)
            kpos = kb * bk + lax.broadcasted_iota(jnp.int32, (bk, bq), 0)
            allowed = (kpos <= qpos) & (kpos >= doc[0:1, rows])
            new = []
            for h in range(heads):
                top, total, acc = carry[h]
                k = proj[keys, (heads + h) * LANES : (heads + h + 1) * LANES]
                s = jnp.where(allowed, nt(k, queries[h]), MASKED)
                top2 = jnp.maximum(top, jnp.max(s, axis=0, keepdims=True))
                p = jnp.exp(s - top2)
                alpha = jnp.exp(top - top2)
                total = total * alpha + jnp.sum(p, axis=0, keepdims=True)
                acc = acc * alpha + nn(vt[h, :, keys], p.astype(BF))
                new.append((top2, total, acc))
            return tuple(new)

        zero = (
            jnp.full((1, bq), MASKED, F32),
            jnp.zeros((1, bq), F32),
            jnp.zeros((LANES, bq), F32),
        )
        begin, _ = doc_bounds(lengths, z, qb * bq)
        end = (qb * bq + bq + bk - 1) // bk
        carry = lax.fori_loop(begin // bk, end, one_key_block, (zero,) * heads)
        for h in range(heads):
            top, total, acc = carry[h]
            o = acc / total
            kept[h, :LANES, rows] = o
            kept[h, LANES:, rows] = jnp.broadcast_to(top + jnp.log(total), (8, bq))
            low = o[:size].astype(BF)
            for part in range(bq // LANES):
                block = qb * (bq // LANES) + part
                lanes = at(block // members * LANES, LANES)
                sent[(block % members) ^ j, h * size : (h + 1) * size, lanes] = low[
                    :, part * LANES : (part + 1) * LANES
                ]
        return 0

    lax.fori_loop(0, stream // bq, one_query_block, 0)
    for kj in range(members):
        outs[kj][...] = sent[kj]


def store_weights(heads, size, count, scale_sum, full, out):
    rows = out.shape[0] // count
    pad = WIDE - 3 * heads * size
    s = scale_sum[:size, :pad]
    high = s.astype(BF)
    rest = (s - high.astype(F32)).astype(BF)
    lane = lax.broadcasted_iota(jnp.int32, (size, pad), 1)
    tail = jnp.where(lane == 0, high, jnp.where(lane == 1, rest, jnp.zeros_like(rest)))
    tail = [tail, jnp.zeros((rows - size, pad), BF)] if rows > size else [tail]
    tail = jnp.concatenate(tail, axis=0)
    for n in range(count):
        block = full[n * rows : (n + 1) * rows, :].astype(BF)
        out[n * rows : (n + 1) * rows, :] = jnp.concatenate(
            [block[:, h * LANES : h * LANES + size] for h in range(3 * heads)] + [tail], axis=1
        )


def attend_back_kernel(heads, size, members, bq, bk, ids, lengths, proj, kept, scale, w, normed, *refs):
    pieces = refs[:members]
    grads, there = refs[members : members + 2]
    weights, refs = refs[members + 2 : -9], refs[-9:]
    dot_, do_, kt, dqt, delta, doc, rows_ref, full, padless = refs
    stream = proj.shape[0]
    groups = pieces[0].shape[1] // LANES
    z, j = ids[0], ids[1]
    doc[...] = doc_starts(lengths, z, stream)
    for h in range(heads):
        kt[h] = proj[:, (heads + h) * LANES : (heads + h + 1) * LANES].T
        dot_[h, size:, :] = jnp.zeros((LANES - size, stream), BF)
        for kj in range(members):
            for g in range(groups):
                lanes = at((g * members + (j ^ kj)) * LANES, LANES)
                dot_[h, :size, lanes] = pieces[kj][
                    h * size : (h + 1) * size, g * LANES : (g + 1) * LANES
                ]
        do_[h] = dot_[h].T
        delta[h] = jnp.broadcast_to(
            jnp.sum(dot_[h].astype(F32) * kept[h, :LANES, :], axis=0, keepdims=True), (8, stream)
        )
        dqt[h] = jnp.zeros((LANES, stream), F32)

    def one_key_block(kb, _):
        keys = at(kb * bk, bk)
        kpos = kb * bk + lax.broadcasted_iota(jnp.int32, (bk, bq), 0)
        ks = [proj[keys, (heads + h) * LANES : (heads + h + 1) * LANES] for h in range(heads)]
        vs = [
            proj[keys, (2 * heads + h) * LANES : (2 * heads + h + 1) * LANES] for h in range(heads)
        ]

        def one_query_block(qb, carry):
            rows = at(qb * bq, bq)
            qpos = qb * bq + lax.broadcasted_iota(jnp.int32, (1, bq), 1)
            allowed = (kpos <= qpos) & (kpos >= doc[0:1, rows])
            new = []
            for h in range(heads):
                dk, dv = carry[h]
                q = proj[rows, h * LANES : (h + 1) * LANES]
                p = jnp.exp(nt(ks[h], q) - kept[h, LANES : LANES + 1, rows])
                p = jnp.where(allowed, p, 0.0)
                dp = nn(vs[h], dot_[h, :, rows])
                ds = (p * (dp - delta[h, 0:1, rows])).astype(BF)
                dv = dv + nn(p.astype(BF), do_[h, rows, :])
                dk = dk + nn(ds, q)
                dqt[h, :, rows] += nn(kt[h, :, keys], ds)
                new.append((dk, dv))
            return tuple(new)

        _, final = doc_bounds(lengths, z, kb * bk + bk - 1)
        zero = jnp.zeros((bk, LANES), F32)
        carry = lax.fori_loop(
            kb * bk // bq, (final + bq - 1) // bq, one_query_block, ((zero, zero),) * heads
        )
        for h in range(heads):
            for n in range(2):
                cols = ((n + 1) * heads + h) * LANES
                grads[keys, cols : cols + LANES] = carry[h][n].astype(BF)
        return 0

    lax.fori_loop(0, stream // bk, one_key_block, 0)
    total = jnp.zeros((1, LANES), F32)
    for h in range(heads):
        dq = dqt[h].T
        q = proj[:, h * LANES : (h + 1) * LANES].astype(F32)
        total = total + jnp.sum(dq * q, axis=0, keepdims=True)
        grads[:, h * LANES : (h + 1) * LANES] = (dq * scale[...]).astype(BF)
    _, _, half, width = there.shape

    def one_member(kj, _):
        y = nn(input_rows(ids, grads, rows_ref, kj, 1, members, half), w[...])
        there[kj] = y.reshape(groups, half, width).astype(BF)
        return 0

    lax.fori_loop(0, members, one_member, 0)
    total = jnp.broadcast_to(total / scale[...], (LANES, LANES)).T
    full[...] = tn(normed[...], grads[...])
    store_weights(heads, size, groups * members, total, full, padless)
    rows = weights[0].shape[0]
    for kz in range(groups):
        weights[kz][...] = padless[at((z ^ kz) * rows, rows, 16), :]


def out_kernel(ids, *refs):
    pieces, (w, ob_t, part) = refs[:-3], refs[-3:]
    mine = pieces[0].shape[0]
    for kj in range(len(pieces)):
        ob_t[at((ids[1] ^ kj) * mine, mine, 16), :] = pieces[kj][...]
    part[...] = nt(ob_t[...].T, w[...]).astype(BF)


def mlp_kernel(groups, ids, *refs):
    x_own, x_other = refs[0], refs[1]
    g_own, g_other, attn, attn_other, up, down, gains = refs[2:9]
    hidden, normed, act, grad_up, cot, part, back = refs[9:]
    half = x_own.shape[1]
    z, c = ids[0], ids[2]
    for kz in range(groups):
        for kc in range(2):
            rows = at((z ^ kz) * (2 * half) + (c ^ kc) * half, half)
            hidden[rows, :] = (x_other if kc else x_own)[kz].astype(F32) + (
                attn[rows, :].astype(F32) + attn_other[rows, :].astype(F32)
            )
            cot[rows, :] = (g_other if kc else g_own)[kz]
    step = hidden.shape[0] // 2

    def block(n, _):
        rows = at(n * step, step)
        h = hidden[rows, :]
        xn = (h * inverse_rms(h) * gains[1:2, :]).astype(BF)
        u = nn(xn, up[...])
        sigma = jax.nn.sigmoid(u)
        a = (u * sigma).astype(BF)
        da = nn(cot[rows, :], down[...])
        du = (da * sigma * (1.0 + u * (1.0 - sigma))).astype(BF)
        part[rows, :] = nt(a, down[...]).astype(BF)
        back[rows, :] = nt(du, up[...]).astype(BF)
        normed[rows, :] = xn
        act[rows, :] = a
        grad_up[rows, :] = du
        return 0

    lax.fori_loop(0, 2, block, 0)


def hidden_kernel(groups, members, ids, *refs):
    hidden, cot, part, part_other, back, back_other, w, gains = refs[:8]
    low, dh_half = refs[8:10]
    pieces, out = refs[10 : 10 + members], refs[10 + members : 10 + members + groups]
    dh, lay, do_t = refs[10 + members + groups :]
    rows_all = hidden.shape[0]
    half = rows_all // groups // 2
    mine = pieces[0].shape[0]
    z, j, c = ids[0], ids[1], ids[2]
    step = rows_all // groups

    def block(n, _):
        rows = at(n * step, step)
        h = hidden[rows, :]
        scale = inverse_rms(h)
        grad = back[rows, :].astype(F32) + back_other[rows, :].astype(F32)
        weighted = grad * gains[1:2, :]
        d = (
            cot[rows, :].astype(F32)
            + scale * weighted
            - h * scale**3 * jnp.mean(weighted * h, axis=-1, keepdims=True)
        )
        dh[rows, :] = d
        low[rows, :] = d.astype(BF)
        lay[rows, :] = (
            h + (part[rows, :].astype(F32) + part_other[rows, :].astype(F32))
        ).astype(BF)
        return 0

    lax.fori_loop(0, groups, block, 0)
    do_t[...] = nn(low[...], w[...]).T.astype(BF)
    for kj in range(members):
        pieces[kj][...] = do_t[at((j ^ kj) * mine, mine, 16), :]
    for g in range(groups):
        out[g][...] = lay[at((z ^ g) * 2 * half + c * half, half), :]
        dh_half[g] = dh[at(g * 2 * half + c * half, half), :]


def by_member(ids, full, out, first=0):
    groups, rows, _ = out[0].shape
    for kj in range(len(out)):
        for g in range(groups):
            where = at((g * len(out) + (ids[1] ^ kj)) * rows, rows, 16)
            out[kj][g, :, first : first + full.shape[1]] = full[where, :]


def feed_weights_kernel(ids, normed, grad_up, cot, act, *refs):
    out, full = refs[:-1], refs[-1]
    full[...] = tn(normed[...], grad_up[...]).astype(BF)
    by_member(ids, full, out)
    full[...] = tn(cot[...], act[...]).astype(BF)
    by_member(ids, full, out, full.shape[1])


def out_weights_kernel(ids, low, ob_t, *refs):
    out, full = refs[:-1], refs[-1]
    full[...] = tn(low[...], ob_t[...].T).astype(BF)
    by_member(ids, full, out)


def sum_members_kernel(*refs):
    total = refs[0][...].astype(F32)
    for part in refs[1:-1]:
        total = total + part[...].astype(F32)
    refs[-1][...] = total.astype(BF)


def sum_split_kernel(members, ids, *refs):
    parts, out, tmp = refs[:members], refs[members:-1], refs[-1]
    total = parts[0][...].astype(F32)
    for part in parts[1:]:
        total = total + part[...].astype(F32)
    tmp[...] = total.astype(BF)
    for kz in range(len(out)):
        out[kz][...] = tmp[ids[0] ^ kz]


def rows_kernel(groups, parts, up, *refs):
    outs, (grad_up, grad_down, grad_out, gain) = refs[:groups], refs[groups:]
    cols = up.shape[1]
    total = parts[0].astype(F32)
    for g in range(1, parts.shape[0]):
        total = total + parts[g].astype(F32)
    grad_up[...] = total[:, :cols]
    grad_down[...] = total[:, cols:]
    term = jnp.sum(total[:, :cols] * up[...].astype(F32), axis=1, keepdims=True)
    gain[...] = jnp.broadcast_to(term, gain.shape)
    total = outs[0][...].astype(F32)
    for part in outs[1:]:
        total = total + part[...].astype(F32)
    grad_out[...] = total


def input_rows(ids, grads, rows_ref, kj, which, members, half):
    for g in range(rows_ref.shape[0] // half):
        base = (g * members + (ids[1] ^ kj)) * 2 + (ids[2] ^ which)
        rows_ref[g * half : (g + 1) * half, :] = grads[at(base * half, half), :]
    return rows_ref[...]


def input_here_kernel(ids, grads, w, other, *refs):
    out, rows_ref = refs[:-1], refs[-1]
    members, (groups, half, width) = len(out), out[0].shape
    for kj in reversed(range(members)):
        y = nn(input_rows(ids, grads, rows_ref, kj, 0, members, half), w[...])
        y = y + other[kj].reshape(groups * half, width).astype(F32)
        out[kj][...] = y.reshape(groups, half, width).astype(BF)


def qkv_sum_kernel(groups, ids, *refs):
    parts, out, tmp = refs[:groups], refs[groups:-1], refs[-1]
    total = parts[0][...].astype(F32)
    for part in parts[1:]:
        total = total + part[...].astype(F32)
    tmp[...] = total
    rows = out[0].shape[0]
    for kj in range(len(out)):
        out[kj][...] = tmp[at((ids[1] ^ kj) * rows, rows, 16), :].astype(BF)


def qkv_rows_kernel(mine, ids, *refs):
    members = len(refs) - 8
    pieces, (query, key, value, dq, dk, dv, small, tmp) = refs[:members], refs[members:]
    for kj in range(members):
        tmp[ids[1] ^ kj] = pieces[kj][...].astype(F32)
    gain = None
    for n, (w, dw) in enumerate(((query, dq), (key, dk), (value, dv))):
        dw[...] = jnp.concatenate(
            [tmp[k][:, n * mine : (n + 1) * mine] for k in range(members)], axis=1
        )
        term = jnp.sum(dw[...] * w[...].astype(F32), axis=1, keepdims=True)
        gain = term if gain is None else gain + term
    scale = tmp[0][:, 3 * mine : 3 * mine + 2]
    for k in range(1, members):
        scale = scale + tmp[k][:, 3 * mine : 3 * mine + 2]
    scale = jnp.sum(scale, axis=1, keepdims=True)
    lane = lax.broadcasted_iota(jnp.int32, small.shape, 1)
    small[...] = jnp.where(lane == 0, gain, jnp.where(lane == 1, scale, 0.0))


def tokens_kernel(groups, ids, *refs):
    x, dh, gains = refs[:3]
    parts, out = refs[3:-groups], refs[-groups:]
    z = ids[0]
    for kz in range(groups):
        grad = parts[0][z ^ kz].astype(F32)
        for part in parts[1:]:
            grad = grad + part[z ^ kz].astype(F32)
        xx = x[kz].astype(F32)
        scale = inverse_rms(xx)
        weighted = grad * gains[0:1, :]
        out[kz][...] = (
            dh[z ^ kz]
            + scale * weighted
            - xx * scale**3 * jnp.mean(weighted * xx, axis=-1, keepdims=True)
        ).astype(BF)


def stream_per_group(
    tokens,
    cotangent,
    doc_lengths,
    w_query,
    w_key,
    w_value,
    w_out,
    w_up,
    w_down,
    gain_attn,
    gain_mlp,
    query_scale,
):
    groups, tok_rows, width = tokens.shape
    count = lax.axis_size("ctx")
    members = count // groups
    size = query_scale.shape[0]
    local = w_query.shape[1]
    shard = width // count
    heads = local // size // members
    half = tok_rows // 2
    stream = tok_rows * count
    mine = heads * size
    rows = groups * tok_rows
    padded = 3 * heads * LANES
    me = lax.axis_index("ctx")
    ids = jnp.stack([me // members, me % members, lax.axis_index("tp")]).astype(jnp.int32)

    planes = [[g * members + k for k in range(members)] for g in range(groups)]
    lines = [[g * members + k for g in range(groups)] for k in range(members)]

    def across(a, mask):
        return lax.ppermute(a, "ctx", [(i, i ^ mask) for i in range(count)])

    def shift(a, by):
        pairs = [(i, i + by * members) for i in range(count)]
        return lax.ppermute(a, "ctx", [(i, k) for i, k in pairs if 0 <= k < count])

    def swap(a):
        return lax.ppermute(a, "tp", [(0, 1), (1, 0)])

    def to_groups(parts):
        return [parts[0]] + [across(parts[k], k * members) for k in range(1, groups)]

    def to_members(parts):
        return [parts[0]] + [across(parts[k], k) for k in range(1, members)]

    def exchange(a, teams):
        return lax.all_to_all(a, "ctx", 0, 0, axis_index_groups=teams, tiled=True)

    def tie(*values):
        return lax.optimization_barrier(values)

    def quarter(own, beside, above):
        cut = groups // 2
        return jnp.concatenate([across(above[:cut], 1), across(beside[cut:], 2)])

    packed = call(
        functools.partial(pack_kernel, mine),
        (struct((shard, WIDE), BF),) * members,
        "svvvv",
        scratch=[pltpu.VMEM((members, shard, WIDE), BF)],
        moved=shard * WIDE * members * 4,
    )(ids, w_query, w_key, w_value, jnp.stack([gain_attn, gain_mlp], axis=1))
    own = jnp.stack(to_groups(split(ids, tokens)))

    shards = call(
        stack_kernel,
        struct((groups, shard, 3 * local), BF),
        "vvv",
        moved=groups * shard * local * 8,
    )(w_up, w_out.T, w_down.T)
    own, packed, shards = tie(own, packed, shards)
    shards = exchange(shards, lines)
    cols = to_members(packed)
    late, cols = tie(own, cols)
    pieces = to_members([own] * (members - 1) + [late])
    pieces, cols, shards = tie(pieces, jnp.stack(cols), shards)
    cols = jnp.concatenate([cols] * groups)

    cols = exchange(cols, lines).reshape(groups, members, shard, WIDE)
    others = [swap(piece) for piece in pieces]
    if members == 4:
        beside, above = across(shards, 1), across(shards, 2)
        cols, others, beside, above = tie(cols, others, beside, above)
        shards = [shards, beside, above, quarter(shards, beside, above)]
    else:
        cols, others, shards = tie(cols, others, to_members([shards] * members))
    pieces = pieces + others
    g_parts, cols = tie(split(ids, cotangent), cols)
    g_own = to_groups(g_parts)
    w_qkv, w_qkv_t, gains = call(
        functools.partial(spread_kernel, heads, size),
        (struct((width, padded), BF), struct((padded, width), BF), struct((8, width), F32)),
        "sv",
        scratch=[pltpu.VMEM((width, WIDE), BF)],
        moved=width * padded * 6,
    )(ids, cols)
    scale_row = jnp.pad(query_scale, (0, LANES - size), constant_values=1.0)[None, :]
    scale_all = jnp.concatenate(
        [scale_row] * heads + [jnp.ones((1, 2 * heads * LANES), F32)], axis=1
    )

    proj, normed = call(
        functools.partial(project_kernel, members, 512),
        (struct((stream, padded), BF), struct((stream, width), BF)),
        "s" + "v" * (2 * members + 3),
        flops=2 * stream * width * padded,
        moved=stream * width * 4,
    )(ids, *pieces, w_qkv, gains, scale_all)

    bq, bk = 512, 512
    *sent, kept = call(
        functools.partial(attend_kernel, heads, size, members, bq, bk),
        (struct((mine, rows), BF),) * members + (struct((heads, LANES + 8, stream), F32),),
        "ssv",
        scratch=[
            pltpu.VMEM((members, mine, rows), BF),
            pltpu.VMEM((heads, LANES, stream), BF),
            pltpu.VMEM((8, stream), jnp.int32),
        ],
        flops=2 * stream * stream * LANES * heads,
        moved=stream * LANES * heads * 10,
    )(ids, doc_lengths, proj)
    sent, shards, g_own = tie(sent, shards, g_own)
    arrived = to_members(sent)
    g_own = jnp.stack(g_own)
    g_other = swap(g_own)
    up_full, out_t, down_t = call(
        order_kernel,
        (struct((width, local), BF),) * 3,
        "s" + "v" * members,
        moved=width * local * 12,
    )(ids, *shards)

    ob_t, attn = call(
        out_kernel,
        (struct((local, rows), BF), struct((rows, width), BF)),
        "s" + "v" * (members + 1),
        flops=2 * rows * local * width,
        moved=local * width * 4,
    )(ids, *arrived, out_t)
    hidden, normed_two, activated, grad_up_raw, cot, part, back = call(
        functools.partial(mlp_kernel, groups),
        (
            struct((rows, width), F32),
            struct((rows, width), BF),
            struct((rows, local), BF),
            struct((rows, local), BF),
            struct((rows, width), BF),
            struct((rows, width), BF),
            struct((rows, width), BF),
        ),
        "s" + "v" * 9,
        flops=8 * rows * local * width,
        moved=local * width * 12,
    )(ids, pieces[0], pieces[members], g_own, g_other, attn, swap(attn), up_full, down_t, gains)
    back_other, part_other = swap(back), swap(part)
    feed_grads = call(
        feed_weights_kernel,
        (struct((groups, shard, 2 * local), BF),) * members,
        "svvvv",
        scratch=[pltpu.VMEM((width, local), BF)],
        flops=4 * rows * local * width,
        moved=local * width * 8,
    )(ids, normed_two, grad_up_raw, cot, activated)
    back_other, part_other, feed_grads = tie(back_other, part_other, feed_grads)
    hidden_low, dh_half, *results = call(
        functools.partial(hidden_kernel, groups, members),
        (struct((rows, width), BF), struct((groups, half, width), F32))
        + (struct((mine, rows), BF),) * members
        + (struct((half, width), BF),) * groups,
        "s" + "v" * 8,
        scratch=[
            pltpu.VMEM((rows, width), F32),
            pltpu.VMEM((rows, width), BF),
            pltpu.VMEM((local, rows), BF),
        ],
        flops=2 * rows * local * width,
        moved=local * width * 12,
    )(ids, hidden, cot, part, part_other, back, back_other, out_t, gains)
    do_pieces, out_parts = to_members(results[:members]), results[members:]
    out_grads = call(
        out_weights_kernel,
        (struct((groups, shard, local), BF),) * members,
        "svv",
        scratch=[pltpu.VMEM((width, local), BF)],
        flops=2 * rows * local * width,
        moved=local * width * 4,
    )(ids, hidden_low, ob_t)
    out_own = [across(part, members) if kz == 1 else part for kz, part in enumerate(out_parts)]
    do_pieces, out_grads, out_own, feed_grads = tie(do_pieces, out_grads, out_own, feed_grads)

    feed_grads = to_members(feed_grads)
    out_own = [
        across(part, kz * members) if kz > 1 else part for kz, part in enumerate(out_own)
    ]

    grads, there, *qkv_parts = call(
        functools.partial(attend_back_kernel, heads, size, members, bq, bk),
        (
            struct((stream, padded), BF),
            struct((members, groups, half, width), BF),
        )
        + (struct((width // groups, WIDE), BF),) * groups,
        "ssvvvvv" + "v" * members,
        scratch=[
            pltpu.VMEM((heads, LANES, stream), BF),
            pltpu.VMEM((heads, stream, LANES), BF),
            pltpu.VMEM((heads, LANES, stream), BF),
            pltpu.VMEM((heads, LANES, stream), F32),
            pltpu.VMEM((heads, 8, stream), F32),
            pltpu.VMEM((8, stream), jnp.int32),
            pltpu.VMEM((groups * half, padded), BF),
            pltpu.VMEM((width, padded), F32),
            pltpu.VMEM((width, WIDE), BF),
        ],
        flops=5 * stream * stream * LANES * heads,
        moved=stream * LANES * heads * 20,
    )(ids, doc_lengths, proj, kept, scale_row, w_qkv_t, normed, *do_pieces)
    there, grads, qkv_parts, feed_grads, out_own, out_grads = tie(
        there, grads, qkv_parts, feed_grads, out_own, out_grads
    )

    there = swap(there)
    out_own = jnp.stack(out_own)
    out_other = swap(out_own)
    here = call(
        input_here_kernel,
        (struct((groups, half, width), BF),) * members,
        "svvv",
        scratch=[pltpu.VMEM((groups * half, padded), BF)],
        flops=stream * width * padded,
        moved=stream * width * 2,
    )(ids, grads, w_qkv_t, there)
    qkv_parts = [
        across(part, members) if kz == 1 else part for kz, part in enumerate(qkv_parts)
    ]
    here, feed_grads, qkv_parts, out_own, out_other = tie(
        here, feed_grads, qkv_parts, out_own, out_other
    )
    layer_out = assemble(ids, out_own, out_other, BF)
    sums = to_members(here)
    qkv_parts = [
        across(part, kz * members) if kz > 1 else part for kz, part in enumerate(qkv_parts)
    ]
    feed_grads = call(
        sum_members_kernel,
        struct((groups, shard, 2 * local), BF),
        "v" * members,
        moved=groups * shard * local * 24,
    )(*feed_grads)
    sums, feed_grads, out_grads, qkv_parts, layer_out = tie(
        sums, feed_grads, out_grads, qkv_parts, layer_out
    )
    grad_x = call(
        functools.partial(tokens_kernel, groups),
        (struct((half, width), BF),) * groups,
        "svvv" + "v" * len(sums),
        moved=groups * half * width * 12,
    )(ids, pieces[0], dh_half, gains, *sums)
    grad_x, qkv_parts, feed_grads, out_grads = tie(grad_x, qkv_parts, feed_grads, out_grads)
    feed_grads = exchange(feed_grads, lines)
    gx_own = to_groups(grad_x)
    out_grads = to_members(out_grads)
    qkv_parts = call(
        functools.partial(qkv_sum_kernel, groups),
        (struct((shard, WIDE), BF),) * members,
        "s" + "v" * groups,
        scratch=[pltpu.VMEM((width // groups, WIDE), F32)],
        moved=width * WIDE * 4,
    )(ids, *qkv_parts)
    gx_own, qkv_parts, out_grads = tie(gx_own, qkv_parts, out_grads)
    qkv_parts = to_members(qkv_parts)
    out_grads = call(
        functools.partial(sum_split_kernel, members),
        (struct((shard, local), BF),) * groups,
        "s" + "v" * members,
        scratch=[pltpu.VMEM((groups, shard, local), BF)],
        moved=groups * shard * local * 12,
    )(ids, *out_grads)
    out_grads = to_groups(out_grads)
    gx_other = [swap(piece) for piece in gx_own]
    grad_up, grad_down, grad_out, gain_two = call(
        functools.partial(rows_kernel, groups),
        (struct((shard, local), F32),) * 3 + (struct((shard, LANES), F32),),
        "v" * (groups + 2),
        moved=shard * local * 36,
    )(feed_grads, w_up, *out_grads)
    grad_q, grad_k, grad_v, small = call(
        functools.partial(qkv_rows_kernel, mine),
        (struct((shard, local), F32),) * 3 + (struct((shard, LANES), F32),),
        "s" + "v" * (members + 3),
        scratch=[pltpu.VMEM((members, shard, WIDE), F32)],
        moved=shard * local * 24,
    )(ids, *qkv_parts, w_query, w_key, w_value)
    lane = lax.broadcasted_iota(jnp.int32, small.shape, 1)
    small = jnp.where(
        lane == 0,
        small / gain_attn.astype(F32)[:, None],
        jnp.where(lane == 2, gain_two / gain_mlp.astype(F32)[:, None], small),
    )
    small = small + swap(small)
    gx_other, small = tie(gx_other, small)
    grad_tokens = call(
        functools.partial(place_kernel, groups),
        struct((groups, tok_rows, width), F32),
        "s" + "v" * (2 * groups),
        moved=rows * width * 8,
    )(ids, *gx_own, *gx_other)
    return (
        layer_out,
        grad_tokens,
        grad_q,
        grad_k,
        grad_v,
        grad_out.T,
        grad_up,
        grad_down.T,
        small[:, 0],
        small[:, 2],
        small[:size, 1],
    )


def fits(shapes, mesh):
    groups, stream, width = shapes[0].shape
    count, cores = mesh.shape["ctx"], mesh.shape["tp"]
    size = shapes[11].shape[0]
    if cores != 2 or count % groups:
        return False
    members = count // groups
    local_heads = shapes[3].shape[1] // cores // size
    return (
        groups & (groups - 1) == 0
        and members & (members - 1) == 0
        and members % 2 == 0
        and local_heads % members == 0
        and stream // count == LANES
        and stream % 512 == 0
        and size % 16 == 0
        and size <= LANES
        and size <= width // count
        and width // count % 16 == 0
        and 3 * local_heads // members * size + 2 <= WIDE
        and 3 * local_heads // members * size >= WIDE - LANES
        and width % (LANES * 2) == 0
    )


def segment_of(starts, positions):
    return jnp.sum((starts[None, :] <= positions[:, None]).astype(jnp.int32), axis=1)


def contract_rows(left, right):
    return lax.dot_general(
        left, right, (((0,), (0,)), ((), ())), preferred_element_type=jnp.float32
    )


def contract_cols(left, right):
    return lax.dot_general(
        left, right, (((1,), (1,)), ((), ())), preferred_element_type=jnp.float32
    )


def per_device(
    tokens,
    cotangent,
    doc_lengths,
    w_query,
    w_key,
    w_value,
    w_out,
    w_up,
    w_down,
    gain_attn,
    gain_mlp,
    query_scale,
):
    micro_count, tok_rows, model_width = tokens.shape
    head_size = query_scale.shape[0]
    local_cols = w_query.shape[1]
    head_count = local_cols // head_size
    stream = tok_rows * lax.axis_size("ctx")
    key_block = min(512, stream)
    block_count = stream // key_block
    positions = lax.axis_index("ctx") * tok_rows + jnp.arange(tok_rows, dtype=jnp.int32)
    local_sums = None
    scale_sum = jnp.zeros((head_size,), jnp.float32)
    outputs = []
    input_grads = []
    for micro_step in range(micro_count):
        gathered = (
            lax.all_gather(w_query, "ctx", axis=0, tiled=True),
            lax.all_gather(w_key, "ctx", axis=0, tiled=True),
            lax.all_gather(w_value, "ctx", axis=0, tiled=True),
            lax.all_gather(w_up, "ctx", axis=0, tiled=True),
            lax.all_gather(gain_attn, "ctx", axis=0, tiled=True),
            lax.all_gather(gain_mlp, "ctx", axis=0, tiled=True),
            lax.all_gather(w_out, "ctx", axis=1, tiled=True),
            lax.all_gather(w_down, "ctx", axis=1, tiled=True),
        )
        w_qkv = jnp.concatenate([gathered[0], gathered[1], gathered[2]], axis=1)
        up_full = gathered[3]
        gain_one = gathered[4].astype(jnp.float32)
        gain_two = gathered[5].astype(jnp.float32)
        out_full = gathered[6]
        down_full = gathered[7]
        lengths = doc_lengths[micro_step]
        starts = jnp.cumsum(lengths) - lengths
        query_seg = segment_of(starts, positions)
        stream_in = tokens[micro_step].astype(jnp.float32)
        scale_one = inverse_rms(stream_in)
        normed_one = (stream_in * scale_one * gain_one).astype(jnp.bfloat16)
        projected = jnp.dot(normed_one, w_qkv, preferred_element_type=jnp.float32)
        query_raw = projected[:, :local_cols].reshape(tok_rows, head_count, head_size)
        query_heads = (query_raw * query_scale).astype(jnp.bfloat16)
        key_local = projected[:, local_cols : 2 * local_cols].astype(jnp.bfloat16)
        value_local = projected[:, 2 * local_cols :].astype(jnp.bfloat16)
        row_top = jnp.full((head_count, tok_rows), MASKED, jnp.float32)
        key_piece = lax.all_gather(key_local, "ctx", axis=0, tiled=True)
        value_piece = lax.all_gather(value_local, "ctx", axis=0, tiled=True)
        length = key_piece.shape[0]
        key_pos = jnp.arange(length, dtype=jnp.int32)
        allowed = (key_pos[None, :] <= positions[:, None]) & (
            segment_of(starts, key_pos)[None, :] == query_seg[:, None]
        )
        scores = jnp.einsum(
            "qhd,khd->hqk",
            query_heads,
            key_piece.reshape(length, head_count, head_size),
            preferred_element_type=jnp.float32,
        )
        scores = jnp.where(allowed[None], scores, MASKED)
        new_top = jnp.maximum(row_top, jnp.max(scores, axis=-1))
        probs = jnp.where(allowed[None], jnp.exp(scores - new_top[:, :, None]), 0.0)
        row_sum = jnp.sum(probs, axis=-1)
        update = jnp.einsum(
            "hqk,khd->qhd",
            probs.astype(jnp.bfloat16),
            value_piece.reshape(length, head_count, head_size),
            preferred_element_type=jnp.float32,
        )
        weighted = update
        row_top, row_sum, weighted = (new_top, row_sum, weighted)
        attn_heads = weighted / jnp.transpose(row_sum)[:, :, None]
        log_total = row_top + jnp.log(row_sum)
        attn_low = attn_heads.reshape(tok_rows, local_cols).astype(jnp.bfloat16)
        attn_out = lax.psum(
            jnp.dot(attn_low, out_full, preferred_element_type=jnp.float32).astype(jnp.bfloat16),
            "tp",
        ).astype(jnp.float32)
        hidden = stream_in + attn_out
        scale_two = inverse_rms(hidden)
        normed_two = (hidden * scale_two * gain_two).astype(jnp.bfloat16)
        up_raw = jnp.dot(normed_two, up_full, preferred_element_type=jnp.float32)
        activated = jax.nn.silu(up_raw).astype(jnp.bfloat16)
        mlp_out = lax.psum(
            jnp.dot(activated, down_full, preferred_element_type=jnp.float32).astype(jnp.bfloat16),
            "tp",
        ).astype(jnp.float32)
        outputs.append((hidden + mlp_out).astype(jnp.bfloat16))
        grad_out = cotangent[micro_step]
        grad_down = contract_rows(activated, grad_out)
        grad_act = contract_cols(grad_out, down_full)
        sigma = jax.nn.sigmoid(up_raw)
        grad_up_raw = (grad_act * sigma * (1.0 + up_raw * (1.0 - sigma))).astype(jnp.bfloat16)
        grad_up = contract_rows(normed_two, grad_up_raw)
        grad_normed_two = lax.psum(
            contract_cols(grad_up_raw, up_full).astype(jnp.bfloat16), "tp"
        ).astype(jnp.float32)
        grad_gain_two = jnp.sum(grad_normed_two * hidden * scale_two, axis=0)
        weighted_two = grad_normed_two * gain_two
        grad_hidden = (
            grad_out.astype(jnp.float32)
            + scale_two * weighted_two
            - hidden * scale_two**3 * jnp.mean(weighted_two * hidden, axis=-1, keepdims=True)
        )
        hidden_low = grad_hidden.astype(jnp.bfloat16)
        grad_out_proj = contract_rows(attn_low, hidden_low)
        grad_attn = (
            contract_cols(hidden_low, out_full)
            .astype(jnp.bfloat16)
            .reshape(tok_rows, head_count, head_size)
        )
        delta = jnp.einsum("qhd,qhd->hq", grad_attn.astype(jnp.float32), attn_heads)
        key_all, value_all = (
            lax.all_gather(key_local, "ctx", axis=0, tiled=True),
            lax.all_gather(value_local, "ctx", axis=0, tiled=True),
        )

        def block_terms(key_piece, value_piece, offset):
            key_heads = key_piece.reshape(key_block, head_count, head_size)
            value_heads = value_piece.reshape(key_block, head_count, head_size)
            key_pos = offset + jnp.arange(key_block, dtype=jnp.int32)
            allowed = (key_pos[None, :] <= positions[:, None]) & (
                segment_of(starts, key_pos)[None, :] == query_seg[:, None]
            )
            scores = jnp.einsum(
                "qhd,khd->hqk", query_heads, key_heads, preferred_element_type=jnp.float32
            )
            probs = jnp.where(allowed[None], jnp.exp(scores - log_total[:, :, None]), 0.0)
            grad_probs = jnp.einsum(
                "qhd,khd->hqk", grad_attn, value_heads, preferred_element_type=jnp.float32
            )
            grad_scores = (probs * (grad_probs - delta[:, :, None])).astype(jnp.bfloat16)
            return (key_heads, probs, grad_scores)

        key_blocks = (
            key_all.reshape(block_count, key_block, local_cols),
            value_all.reshape(block_count, key_block, local_cols),
            jnp.arange(block_count, dtype=jnp.int32) * key_block,
        )
        zero_query = jnp.zeros((tok_rows, head_count, head_size), jnp.float32)

        def grad_block(grad_query, packed):
            key_heads, probs, grad_scores = block_terms(packed[0], packed[1], packed[2])
            grad_value = jnp.einsum(
                "hqk,qhd->khd",
                probs.astype(jnp.bfloat16),
                grad_attn,
                preferred_element_type=jnp.float32,
            )
            grad_query = grad_query + jnp.einsum(
                "hqk,khd->qhd", grad_scores, key_heads, preferred_element_type=jnp.float32
            )
            grad_key = jnp.einsum(
                "hqk,qhd->khd", grad_scores, query_heads, preferred_element_type=jnp.float32
            )
            return (
                grad_query,
                (
                    grad_key.reshape(key_block, local_cols),
                    grad_value.reshape(key_block, local_cols),
                ),
            )

        grad_query, (key_terms, value_terms) = lax.scan(grad_block, zero_query, key_blocks)
        key_grad, value_grad = (
            lax.psum_scatter(
                key_terms.reshape(stream, local_cols).astype(jnp.bfloat16),
                "ctx",
                scatter_dimension=0,
                tiled=True,
            ).astype(jnp.float32),
            lax.psum_scatter(
                value_terms.reshape(stream, local_cols).astype(jnp.bfloat16),
                "ctx",
                scatter_dimension=0,
                tiled=True,
            ).astype(jnp.float32),
        )
        grad_query_raw = (
            (grad_query * query_scale).astype(jnp.bfloat16).reshape(tok_rows, local_cols)
        )
        scale_part = jnp.sum(grad_query * query_raw, axis=(0, 1))
        grad_cols = jnp.concatenate(
            [grad_query_raw, key_grad.astype(jnp.bfloat16), value_grad.astype(jnp.bfloat16)], axis=1
        )
        grad_qkv = contract_rows(normed_one, grad_cols)
        grad_normed_one, scale_total = (
            lax.psum(contract_cols(grad_cols, w_qkv).astype(jnp.bfloat16), "tp").astype(
                jnp.float32
            ),
            lax.psum(scale_part.astype(jnp.bfloat16), "tp").astype(jnp.float32),
        )
        scale_sum = scale_sum + scale_total
        grad_gain_one = jnp.sum(grad_normed_one * stream_in * scale_one, axis=0)
        weighted_one = grad_normed_one * gain_one
        input_grads.append(
            grad_hidden
            + scale_one * weighted_one
            - stream_in * scale_one**3 * jnp.mean(weighted_one * stream_in, axis=-1, keepdims=True)
        )
        grads = (
            grad_qkv[:, :local_cols],
            grad_qkv[:, local_cols : 2 * local_cols],
            grad_qkv[:, 2 * local_cols :],
            grad_up,
            grad_gain_one,
            grad_gain_two,
            grad_out_proj,
            grad_down,
        )
        shares = (
            lax.psum_scatter(
                grads[0].astype(jnp.bfloat16), "ctx", scatter_dimension=0, tiled=True
            ).astype(jnp.float32),
            lax.psum_scatter(
                grads[1].astype(jnp.bfloat16), "ctx", scatter_dimension=0, tiled=True
            ).astype(jnp.float32),
            lax.psum_scatter(
                grads[2].astype(jnp.bfloat16), "ctx", scatter_dimension=0, tiled=True
            ).astype(jnp.float32),
            lax.psum_scatter(
                grads[3].astype(jnp.bfloat16), "ctx", scatter_dimension=0, tiled=True
            ).astype(jnp.float32),
            lax.psum_scatter(
                grads[4].astype(jnp.bfloat16), "ctx", scatter_dimension=0, tiled=True
            ).astype(jnp.float32),
            lax.psum_scatter(
                grads[5].astype(jnp.bfloat16), "ctx", scatter_dimension=0, tiled=True
            ).astype(jnp.float32),
            lax.psum_scatter(
                grads[6].astype(jnp.bfloat16), "ctx", scatter_dimension=1, tiled=True
            ).astype(jnp.float32),
            lax.psum_scatter(
                grads[7].astype(jnp.bfloat16), "ctx", scatter_dimension=1, tiled=True
            ).astype(jnp.float32),
        )
        local_sums = (
            shares
            if local_sums is None
            else tuple((total + extra for total, extra in zip(local_sums, shares)))
        )
    scale_grad = lax.psum(scale_sum, "ctx")
    return (
        jnp.stack(outputs),
        jnp.stack(input_grads),
        local_sums[0],
        local_sums[1],
        local_sums[2],
        local_sums[6],
        local_sums[3],
        local_sums[7],
        local_sums[4],
        local_sums[5],
        scale_grad,
    )


def solution(mesh):
    in_specs = (
        P(None, "ctx", None),
        P(None, "ctx", None),
        P(),
        P("ctx", "tp"),
        P("ctx", "tp"),
        P("ctx", "tp"),
        P("tp", "ctx"),
        P("ctx", "tp"),
        P("tp", "ctx"),
        P("ctx"),
        P("ctx"),
        P(),
    )
    out_specs = (
        P(None, "ctx", None),
        P(None, "ctx", None),
        P("ctx", "tp"),
        P("ctx", "tp"),
        P("ctx", "tp"),
        P("tp", "ctx"),
        P("ctx", "tp"),
        P("tp", "ctx"),
        P("ctx"),
        P("ctx"),
        P(),
    )

    def run(*arrays):
        body = stream_per_group if fits(arrays, mesh) else per_device
        return jax.shard_map(
            body, mesh=mesh, in_specs=in_specs, out_specs=out_specs, check_vma=False
        )(*arrays)

    return run
```
